32 devices in a mesh: dp: 8 (over y, x, core), tensor: 4 (over z).
Axes of the slice: x: 2, y: 2, z: 4, core: 2. Of those that a mesh axis runs over, the one named last changes fastest.
Arguments:
- tokens: bfloat16 [16384, 768], P(('dp', 'tensor')), may hold values from -48 to 48
- counts: int32 [8], replicated, may hold values from 4 to 8
- routes: int32 [2, 16384, 2], P(None, 'dp'), may hold values from 0 to 3, all different within a row; in each aligned block of 2048 rows (0 to 2047, 2048 to 4095, ..., all dimensions but the last counted through in order) at most 1536 rows name the same one
- norm_gain: bfloat16 [3072], P(('dp', 'tensor')), may hold values from 0.5 to 1.5
- norm_bias: bfloat16 [3072], P(('dp', 'tensor')), may hold values from -0.59765625 to 0.59765625
- w_router: bfloat16 [6144], P(('dp', 'tensor')), may hold values from -0.15625 to 0.15625
- w_qkv: bfloat16 [2, 3, 768, 768], P(None, None, 'dp', 'tensor'), may hold values from -0.21875 to 0.21875
- w_out: bfloat16 [2, 768, 768], P(None, 'tensor', 'dp'), may hold values from -1.75 to 1.75
- w_in: bfloat16 [2, 4, 768, 3072], P(None, None, 'dp', 'tensor'), may hold values from -0.21875 to 0.21875
- w_back: bfloat16 [2, 4, 768, 3072], P(None, None, 'dp', 'tensor'), may hold values from -0.4375 to 0.4375
- cotangent: bfloat16 [16384, 768], P(('dp', 'tensor')), may hold values from -6 to 6
Outputs:
- out: float32 [16384, 768], P(('dp', 'tensor'))
- grad_input: float32 [16384, 768], P(('dp', 'tensor'))
- grad_gain: float32 [3072], P(('dp', 'tensor'))
- grad_bias: float32 [3072], P(('dp', 'tensor'))
- grad_router: float32 [6144], P(('dp', 'tensor'))
- grad_qkv: float32 [2, 3, 768, 768], P(None, None, 'dp', 'tensor')
- grad_out: float32 [2, 768, 768], P(None, 'tensor', 'dp')
- grad_in: float32 [2, 4, 768, 3072], P(None, None, 'dp', 'tensor')
- grad_back: float32 [2, 4, 768, 3072], P(None, None, 'dp', 'tensor')
- rms: float32 [2, 3], replicated
The draws below stay inside these ranges and needn't reach their ends.
Inputs may be any that keep to these rules, and one draw needn't show every extreme that they name: `routes`: each row names two different experts. Within the rows of one data group of one block no expert is named more than 1536 times, and in every draw some expert is named exactly 1536 times in some group.
All inputs are finite; a program needn't handle non-finite values.
Results may differ from the reference program's by a relative error of at most 0.038.
Values may be sent and summed in bfloat16 or wider, within the bound.
A program may use at most 320 MiB of HBM per device.

```python
import math
import jax
import jax.numpy as jnp
import numpy as np
from jax import lax

D = 768
HEADS = 12
HD = 64
FF = 3072
LEN = 197
SEQ = 256
LAYERS = 2
IMG_DEV = 8
E = 4
ROWS_GRP = 2048
TOKENS = 16384
SLOTS = 1536
N_DP = 8


def draw_tokens(key, part):
    row_frac = jnp.arange(TOKENS, dtype=jnp.float32)[:, None] / max(TOKENS - 1, 1)
    base = jnp.clip(jax.random.normal(key, (TOKENS, D), jnp.float32), -6.0, 6.0)
    row_scale = 1.0 + 2.0 * row_frac
    return (base * row_scale).astype(jnp.bfloat16)


def with_ends(values, stream_key, smallest, high):
    place = [jax.random.randint(jax.random.fold_in(stream_key, axis), (), 0, length) for axis, length in enumerate(values.shape)]
    longest = values.shape.index(max(values.shape))
    beside = place[:longest] + [(place[longest] + 1) % values.shape[longest]] + place[longest + 1:]
    return values.at[tuple(place)].set(smallest).at[tuple(beside)].set(high)


def raised(entries, key, source, target, shards_of, factor):
    owner, partner = [(jnp.arange(entries.shape[axis_at]) // (entries.shape[axis_at] // shards_of)).reshape([-1 if axis == axis_at else 1 for axis in range(entries.ndim)]) for axis_at in (source, target)]
    chosen = jax.random.permutation(key, shards_of)[partner]
    strong = (owner == chosen) | (owner == (partner + shards_of // 2) % shards_of)
    return jnp.where(strong, factor * entries, entries)


def steps_of(own_key, dims, shards, smallest, high):
    level, own = 1.0, jax.random.fold_in(own_key, 6)
    for position, shards_of in shards:
        heights = jnp.exp(jax.random.uniform(jax.random.fold_in(own, position), (shards_of,), jnp.float32, smallest / len(shards), high / len(shards)))
        level = level * jnp.repeat(heights, dims[position] // shards_of).reshape([-1 if axis == position else 1 for axis in range(len(dims))])
    return level


def assign_block(key, own, number, rows, number_of, top, most, slope):
    ranking = jax.random.permutation(key, number_of)
    packed, usual = load_shares(number_of, rows * top, most, slope, True), load_shares(number_of, rows * top, most, slope, False)
    places = jnp.arange(number_of)

    def named(sizes, turn):
        used = int((sizes > 0).sum())
        fixed = max(1, used // 4)
        moved = fixed + (places - fixed + turn * (used - fixed)) % max(1, number_of - fixed)
        return jnp.zeros((number_of,), jnp.int32).at[ranking[jnp.where(places < fixed, places, moved)]].set(jnp.asarray(sizes, jnp.int32))

    sizes = jnp.where(number % 4 == 0, named(packed, number // 4), named(usual, number - number // 4 - 1))
    mixed = jax.random.permutation(jax.random.fold_in(own, 3), number_of)
    source_of, taker = mixed[0:number_of // 2 * 2:2], mixed[1:number_of // 2 * 2:2]
    slack = jnp.minimum(sizes[source_of] - 1, most - sizes[taker]) // 2
    slack = jnp.where((source_of == ranking[0]) | (taker == ranking[0]) | (sizes[taker] == 0), 0, jnp.maximum(slack, 0))
    moved = jax.random.randint(jax.random.fold_in(own, 4), (number_of // 2,), 0, 1 << 20) % (slack + 1)
    sizes = sizes.at[source_of].add(-moved).at[taker].add(moved)
    labels = jnp.searchsorted(jnp.cumsum(sizes), jnp.arange(rows * top), side="right").astype(jnp.int32)
    grid = labels.reshape(top, rows).T
    grid = grid[jax.random.permutation(jax.random.fold_in(own, 1), rows)]
    turn = jax.random.randint(jax.random.fold_in(own, 2), (rows, 1), 0, top)
    return jnp.take_along_axis(grid, (jnp.arange(top)[None, :] + turn) % top, axis=1)


def load_shares(count, total, most, lean, full):
    loads = [(1 << 20) // math.isqrt(rank ** lean) + 1 for rank in range(1, count + 1)]
    largest = most if full else min(most, max(-(-total // count), total * loads[0] // sum(loads)))
    least = 1 if total - largest >= count - 1 else 0
    holding, rest = [largest] + [least] * (count - 1), total - largest - least * (count - 1)
    while rest > 0:
        free = [i for i in range(1, count) if holding[i] < largest] or [i for i in range(1, count) if holding[i] < most]
        mass, budget = sum([loads[i] for i in free]), rest
        for i in free:
            addition = min(most - holding[i], max(1, budget * loads[i] // mass), rest)
            holding[i] = holding[i] + addition
            rest = rest - addition
    return np.array(holding)


def gaussian(rng, dims, width, bound, pieces=(), kind=jnp.bfloat16):
    level = steps_of(rng, dims, pieces, -0.22, 0.18) if pieces else 1.0
    entries = jax.random.normal(rng, dims, jnp.float32) * width * level
    return jnp.minimum(jnp.maximum(entries, -bound), bound).astype(kind)


def gaussian_with(own_key, dims, scale, limit, split, heavy, kind=jnp.bfloat16):
    drawn = scale * jax.random.normal(own_key, dims, jnp.float32)
    if split:
        drawn = drawn * steps_of(own_key, dims, split, -0.22, 0.18)
    return jnp.clip(raised(drawn, jax.random.fold_in(own_key, 3), *heavy), -limit, limit).astype(kind)


def setup_inputs(seed: int = 0) -> dict:
    streams_of = jax.random.split(jax.random.key(seed), 12)
    tokens = draw_tokens(jax.random.fold_in(streams_of[11], 71), 0)
    counts = with_ends(jax.random.randint(streams_of[1], (N_DP,), IMG_DEV // 2, IMG_DEV + 1), jax.random.fold_in(streams_of[1], 1), IMG_DEV // 2, IMG_DEV).astype(jnp.int32)
    routes_keys = jax.random.split(jax.random.fold_in(streams_of[2], 1), LAYERS * TOKENS // ROWS_GRP)
    routes_turns = jax.random.permutation(jax.random.fold_in(streams_of[2], 3), LAYERS * TOKENS // ROWS_GRP)
    routes = jax.vmap(lambda own, number: assign_block(jax.random.fold_in(streams_of[2], 2), own, number, ROWS_GRP, E, 2, SLOTS, 2))(routes_keys, routes_turns).reshape((LAYERS, TOKENS, 2))
    norm_gain = jnp.clip(1.0 + 0.1 * jax.random.normal(streams_of[3], (LAYERS * 2 * D,), jnp.float32), 0.5, 1.5).astype(jnp.bfloat16)
    norm_bias = gaussian(streams_of[4], (LAYERS * 2 * D,), 0.1, 0.59765625, ((0, 32),))
    w_router = gaussian(streams_of[5], (LAYERS * D * E,), (2 * D) ** -0.5, 0.15625, ((0, 32),))
    w_qkv = gaussian(streams_of[6], (LAYERS, 3, D, D), D ** -0.5, 0.21875, ((2, 8), (3, 4)))
    w_out = gaussian(streams_of[7], (LAYERS, D, D), (max(D // 64, 1)) ** -0.5, 1.75, ((1, 4), (2, 8)))
    w_in = gaussian(streams_of[8], (LAYERS, E, D, FF), D ** -0.5, 0.21875, ((2, 8), (3, 4)))
    w_back = gaussian(streams_of[9], (LAYERS, E, D, FF), (max(FF // (E * E), 1)) ** -0.5, 0.4375, ((2, 8), (3, 4)))
    cotangent = gaussian_with(streams_of[10], (TOKENS, D), 1.0, 6.0, ((0, 32),), (0, 1, 32, 2.75))
    return {"tokens": tokens, "counts": counts, "routes": routes, "norm_gain": norm_gain, "norm_bias": norm_bias, "w_router": w_router, "w_qkv": w_qkv, "w_out": w_out, "w_in": w_in, "w_back": w_back, "cotangent": cotangent}


@jax.custom_vjp
def low(v):
    return lax.optimization_barrier(v.astype(jnp.bfloat16)).astype(jnp.float32)

@jax.custom_vjp
def low_back(v):
    return v

def low_keep(v):
    return (low(v), None)

def low_pass(kept, grad):
    return (grad,)

def back_keep(v):
    return (v, None)

def back_low(kept, grad):
    return (low(grad),)
low.defvjp(low_keep, low_pass)
low_back.defvjp(back_keep, back_low)
highest = lax.Precision.HIGHEST

def layer_norm(row_vals, gain_vec, bias_vec):
    row_mean = lax.optimization_barrier(jnp.mean(row_vals, axis=-1, keepdims=True))
    centred = row_vals - row_mean
    row_var = lax.optimization_barrier(jnp.mean(centred * centred, axis=-1, keepdims=True))
    return centred * lax.rsqrt(row_var + 1e-06) * gain_vec + bias_vec

def group_layer(weights, carried):
    gain_pair, shift_pair, router, wqkv, wout, win, wback = weights
    row_vals, routing, valid_rows = carried
    total_rows = row_vals.shape[0]
    images = total_rows // SEQ
    norm_one = low(layer_norm(row_vals, gain_pair[0], shift_pair[0]))
    qkv_rows = low(low_back(jnp.einsum('rd,cde->cre', norm_one, wqkv, precision=highest)))
    head_view = qkv_rows.reshape(3, images, SEQ, HEADS, HD)
    scores = low_back(HD ** (-0.5) * jnp.einsum('iqhd,ikhd->ihqk', head_view[0], head_view[1], precision=highest))
    key_keep = jnp.arange(SEQ) < LEN
    scores = jnp.where(key_keep, scores, -1e+30)
    attn_probs = jax.nn.softmax(scores, axis=-1)
    context = low(low_back(jnp.einsum('ihqk,ikhd->iqhd', low(attn_probs), head_view[2], precision=highest)))
    context = context.reshape(total_rows, D)
    attn_out = low_back(jnp.dot(context, wout, precision=highest))
    residual = row_vals + attn_out
    norm_two = low(layer_norm(residual, gain_pair[1], shift_pair[1]))
    router_probs = jax.nn.softmax(jnp.dot(norm_two, router, precision=highest), axis=-1)
    one_hot = routing[:, :, None] == jnp.arange(E)[None, None, :]
    gate_vals = lax.optimization_barrier(jnp.sum(jnp.where(one_hot, router_probs[:, None, :], 0.0), axis=-1))
    flat_pick = routing.reshape(-1)
    hot_int = (flat_pick[:, None] == jnp.arange(E)[None, :]).astype(jnp.int32)
    rank_in = lax.optimization_barrier(jnp.sum((jnp.cumsum(hot_int, axis=0) - hot_int) * hot_int, axis=1)).astype(jnp.int32)
    target = (flat_pick * SLOTS + rank_in).astype(jnp.int32)
    positions = jnp.full((E * SLOTS,), 2 * total_rows, jnp.int32).at[target].set(jnp.arange(2 * total_rows, dtype=jnp.int32))
    source = jnp.where(positions < 2 * total_rows, positions // 2, total_rows).astype(jnp.int32)
    padded = jnp.concatenate([norm_two, jnp.zeros((1, D), norm_two.dtype)], axis=0)
    arrived = padded[source].reshape(E, SLOTS, D)
    pre_act = low_back(jnp.einsum('esd,edf->esf', arrived, win, precision=highest))
    activation = low(jax.nn.gelu(pre_act, approximate=True))
    expert_rows = low(low_back(jnp.einsum('esf,edf->esd', activation, wback, precision=highest)))
    chosen = expert_rows.reshape(E * SLOTS, D)[target].reshape(total_rows, 2, D)
    expert_out = low_back(lax.optimization_barrier(jnp.sum(gate_vals[:, :, None] * chosen, axis=1)))
    result = residual + expert_out
    mask_col = valid_rows[:, None]
    stat_terms = jnp.stack([jnp.sum(mask_col * result * result), jnp.sum(mask_col * attn_out * attn_out), jnp.sum(mask_col * expert_out * expert_out)])
    return (result, stat_terms)

def forward(tokens, gains, biases, router, wqkv, wout, win, wback, routing, valid_rows):
    row_vals = tokens.reshape(N_DP, ROWS_GRP, D)
    gain_all = gains.reshape(LAYERS, 2, D)
    bias_all = biases.reshape(LAYERS, 2, D)
    router_all = router.reshape(LAYERS, D, E)
    layer_fn = jax.checkpoint(group_layer)
    totals = []
    for layer_idx in range(LAYERS):
        weights = (gain_all[layer_idx], bias_all[layer_idx], router_all[layer_idx], wqkv[layer_idx], wout[layer_idx], win[layer_idx], wback[layer_idx])
        row_vals, stat_terms = lax.map(lambda carried: layer_fn(weights, carried), (row_vals, routing[layer_idx], valid_rows))
        totals.append(lax.optimization_barrier(jnp.sum(stat_terms, axis=0)))
    return (row_vals.reshape(TOKENS, D), jnp.stack(totals))

def reference(tokens, counts, routes, norm_gain, norm_bias, w_router, w_qkv, w_out, w_in, w_back, cotangent):
    image_idx = jnp.arange(ROWS_GRP) // SEQ
    slot_idx = jnp.arange(ROWS_GRP) % SEQ
    valid_rows = ((image_idx[None, :] < counts[:, None]) & (slot_idx[None, :] < LEN)).astype(jnp.float32)
    routing = routes.reshape(LAYERS, N_DP, ROWS_GRP, 2)

    def run(tok, gains, biases, router, wqkv, wout, win, wback):
        return forward(tok, gains, biases, router, wqkv, wout, win, wback, routing, valid_rows)
    primals = tuple((a.astype(jnp.float32) for a in (tokens, norm_gain, norm_bias, w_router, w_qkv, w_out, w_in, w_back)))
    result, pull_back, totals = jax.vjp(run, *primals, has_aux=True)
    output_grad = cotangent.astype(jnp.float32) * valid_rows.reshape(TOKENS, 1)
    grads = pull_back(output_grad)
    denom = jnp.sum(counts).astype(jnp.float32) * (LEN * D)
    rms = jnp.sqrt(totals / denom)
    return (result, grads[0], grads[1], grads[2], grads[3], grads[4], grads[5], grads[6], grads[7], rms)
```

```python
from functools import partial
import math

import jax
import jax.numpy as jnp
from jax import lax
from jax.experimental import pallas as pl
from jax.experimental.pallas import tpu as pltpu
from jax.sharding import PartitionSpec as P

D = 768
HD = 64
LEN = 197
SEQ = 256
LAYERS = 2


eps_norm = 1e-06
far_negative = -1e30
highest = lax.Precision.HIGHEST


def norm_forward(row_vals, gain_vec, bias_vec):
    row_mean = jnp.mean(row_vals, axis=-1, keepdims=True)
    centred = row_vals - row_mean
    row_var = jnp.mean(centred * centred, axis=-1, keepdims=True)
    inv_std = lax.rsqrt(row_var + eps_norm)
    normed = centred * inv_std
    return (normed * gain_vec + bias_vec, normed, inv_std)


def norm_backward(grad_vals, normed, inv_std, gain_vec):
    gain_grad = jnp.sum(grad_vals * normed, axis=0)
    bias_grad = jnp.sum(grad_vals, axis=0)
    scaled = grad_vals * gain_vec
    mean_one = jnp.mean(scaled, axis=-1, keepdims=True)
    mean_two = jnp.mean(scaled * normed, axis=-1, keepdims=True)
    return (inv_std * (scaled - mean_one - normed * mean_two), gain_grad, bias_grad)


def gather_rows(row_vals):
    return lax.all_gather(row_vals, "tensor", axis=0, tiled=True)


def sum_rows(row_vals):
    return lax.psum_scatter(
        row_vals.astype(jnp.bfloat16), "tensor", scatter_dimension=0, tiled=True
    ).astype(jnp.float32)


def sum_slots(slot_vals):
    return lax.psum_scatter(
        slot_vals.astype(jnp.bfloat16), "tensor", scatter_dimension=1, tiled=True
    ).astype(jnp.float32)


def to_experts(make_rows, positions):
    return lax.all_to_all(make_rows(positions), "dp", split_axis=0, concat_axis=0, tiled=True)


def attend(block_in, key_keep, score_scale):
    query_heads, key_heads, value_heads = block_in
    scores = (
        jnp.einsum("iqhd,ikhd->ihqk", query_heads, key_heads, preferred_element_type=jnp.float32)
        * score_scale
    )
    scores = jnp.where(key_keep, scores, far_negative)
    row_max = jnp.max(scores, axis=-1, keepdims=True)
    exponent = jnp.exp(scores - row_max)
    row_total = jnp.sum(exponent, axis=-1, keepdims=True)
    weights = (exponent / row_total).astype(jnp.bfloat16)
    context = jnp.einsum(
        "ihqk,ikhd->iqhd", weights, value_heads, preferred_element_type=jnp.float32
    )
    return (context.astype(jnp.bfloat16), (row_max + jnp.log(row_total))[..., 0])


def attend_back(block_in, key_keep, score_scale):
    query_heads, key_heads, value_heads, d_context, log_total = block_in
    scores = (
        jnp.einsum("iqhd,ikhd->ihqk", query_heads, key_heads, preferred_element_type=jnp.float32)
        * score_scale
    )
    scores = jnp.where(key_keep, scores, far_negative)
    weights = jnp.exp(scores - log_total[..., None])
    d_values = jnp.einsum(
        "ihqk,iqhd->ikhd",
        weights.astype(jnp.bfloat16),
        d_context,
        preferred_element_type=jnp.float32,
    )
    d_weights = jnp.einsum(
        "iqhd,ikhd->ihqk", d_context, value_heads, preferred_element_type=jnp.float32
    )
    inner_sum = jnp.sum(weights * d_weights, axis=-1, keepdims=True)
    d_scores = (weights * (d_weights - inner_sum)).astype(jnp.bfloat16)
    d_queries = (
        jnp.einsum("ihqk,ikhd->iqhd", d_scores, key_heads, preferred_element_type=jnp.float32)
        * score_scale
    )
    d_keys = (
        jnp.einsum("ihqk,iqhd->ikhd", d_scores, query_heads, preferred_element_type=jnp.float32)
        * score_scale
    )
    return (
        d_queries.astype(jnp.bfloat16),
        d_keys.astype(jnp.bfloat16),
        d_values.astype(jnp.bfloat16),
    )


def contract_first(left_mat, right_mat):
    return lax.dot_general(
        left_mat, right_mat, (((0,), (0,)), ((), ())), preferred_element_type=jnp.float32
    )


def contract_last(left_mat, right_mat):
    return lax.dot_general(
        left_mat, right_mat, (((1,), (1,)), ((), ())), preferred_element_type=jnp.float32
    )


def per_device_general(
    tokens, counts, routes, norm_gain, norm_bias, w_router, w_qkv, w_out, w_in, w_back, cotangent
):
    groups = lax.axis_size("dp")
    parts = lax.axis_size("tensor")
    experts = groups // 2
    group_idx = lax.axis_index("dp")
    my_part = lax.axis_index("tensor")
    own_rows = tokens.shape[0]
    rows_all = own_rows * parts
    slot_count = 3 * rows_all // experts
    half_slots = slot_count // 2
    quarter = half_slots // parts
    score_scale = HD ** (-0.5)
    images = rows_all // SEQ
    per_block = math.gcd(images, max(1, 512 // SEQ))
    blocks = images // per_block
    head_cols = w_qkv.shape[-1]
    heads_here = head_cols // HD
    key_keep = jnp.arange(SEQ) < LEN
    gain_flat, bias_flat, router_flat = (
        lax.all_gather(norm_gain, ("dp", "tensor"), axis=0, tiled=True),
        lax.all_gather(norm_bias, ("dp", "tensor"), axis=0, tiled=True),
        lax.all_gather(w_router, ("dp", "tensor"), axis=0, tiled=True),
    )
    gains_all = gain_flat.astype(jnp.float32).reshape(LAYERS, 2, D)
    biases_all = bias_flat.astype(jnp.float32).reshape(LAYERS, 2, D)
    router_all = router_flat.reshape(LAYERS, D, experts)
    row_ids = my_part * own_rows + jnp.arange(own_rows, dtype=jnp.int32)
    image_count = lax.dynamic_index_in_dim(counts, group_idx, keepdims=False)
    valid_rows = ((row_ids // SEQ < image_count) & (row_ids % SEQ < LEN)).astype(jnp.float32)[
        :, None
    ]

    def split_heads(columns):
        return columns.reshape(blocks, per_block, SEQ, heads_here, HD)

    hidden = tokens.astype(jnp.float32)
    kept_layers = []
    stat_terms = []
    for layer_idx in range(LAYERS):
        gain_pair = gains_all[layer_idx]
        shift_pair = biases_all[layer_idx]
        wq_part, wo_part = (
            lax.all_gather(w_qkv[layer_idx], "dp", axis=1, tiled=True),
            lax.all_gather(w_out[layer_idx], "dp", axis=1, tiled=True),
        )
        w_cat = jnp.concatenate([wq_part[0], wq_part[1], wq_part[2]], axis=1)
        up_part, back_part = (
            lax.all_to_all(
                jnp.repeat(w_in[layer_idx], 2, axis=0),
                "dp",
                split_axis=0,
                concat_axis=0,
                tiled=True,
            ),
            lax.all_to_all(
                jnp.repeat(w_back[layer_idx], 2, axis=0),
                "dp",
                split_axis=0,
                concat_axis=0,
                tiled=True,
            ),
        )
        up_part = up_part.reshape(D, -1)
        back_part = back_part.reshape(D, -1)
        up_use, back_use = (up_part, back_part)
        norm_one, normed_one, inv_one = norm_forward(hidden, gain_pair[0], shift_pair[0])
        rows_one = gather_rows(norm_one.astype(jnp.bfloat16))
        qkv_rows = jnp.dot(rows_one, w_cat, preferred_element_type=jnp.float32).astype(jnp.bfloat16)
        query_heads = split_heads(qkv_rows[:, :head_cols])
        key_heads = split_heads(qkv_rows[:, head_cols : 2 * head_cols])
        value_heads = split_heads(qkv_rows[:, 2 * head_cols :])
        context, log_total = lax.map(
            partial(attend, key_keep=key_keep, score_scale=score_scale),
            (query_heads, key_heads, value_heads),
        )
        context = context.reshape(rows_all, head_cols)
        attn_out = sum_rows(jnp.dot(context, wo_part, preferred_element_type=jnp.float32))
        residual = hidden + attn_out
        norm_two, normed_two, inv_two = norm_forward(residual, gain_pair[1], shift_pair[1])
        rows_two = gather_rows(norm_two.astype(jnp.bfloat16))
        router = router_all[layer_idx]
        router_probs = jax.nn.softmax(
            jnp.dot(rows_two, router, preferred_element_type=jnp.float32), axis=-1
        )
        routing = routes[layer_idx]
        one_hot = routing[:, :, None] == jnp.arange(experts)[None, None, :]
        gate_vals = jnp.sum(jnp.where(one_hot, router_probs[:, None, :], 0.0), axis=-1)
        flat_pick = routing.reshape(-1)
        hot_int = (flat_pick[:, None] == jnp.arange(experts)[None, :]).astype(jnp.int32)
        rank_in = jnp.sum((jnp.cumsum(hot_int, axis=0) - hot_int) * hot_int, axis=1)
        target = flat_pick * slot_count + rank_in
        positions = (
            jnp.full((experts * slot_count,), 2 * rows_all, jnp.int32)
            .at[target]
            .set(jnp.arange(2 * rows_all, dtype=jnp.int32))
        )
        positions = positions.reshape(groups, half_slots)
        padded_two = jnp.concatenate([rows_two, jnp.zeros((1, D), jnp.bfloat16)], axis=0)

        def take_rows(slot_index):
            return padded_two[jnp.where(slot_index < 2 * rows_all, slot_index // 2, rows_all)]

        arrived = to_experts(take_rows, positions).reshape(-1, D)
        pre_act = jnp.dot(arrived, up_use, preferred_element_type=jnp.float32)
        activation = jax.nn.gelu(pre_act, approximate=True).astype(jnp.bfloat16)
        partial_out = contract_last(activation, back_use)
        summed = sum_slots(partial_out.reshape(groups, half_slots, D)).astype(jnp.bfloat16)
        returned = lax.all_to_all(summed, "dp", split_axis=0, concat_axis=0, tiled=True)
        slot_pair = target.reshape(rows_all, 2)
        owner = slot_pair // half_slots
        inside = slot_pair % half_slots
        in_quarter = inside // quarter == my_part
        pick_index = jnp.where(
            in_quarter, owner * quarter + inside - my_part * quarter, groups * quarter
        )
        padded_ret = jnp.concatenate(
            [returned.reshape(groups * quarter, D), jnp.zeros((1, D), jnp.bfloat16)], axis=0
        )
        chosen = padded_ret[pick_index]
        expert_out = sum_rows(jnp.sum(gate_vals[:, :, None] * chosen, axis=1))
        result = residual + expert_out
        stat_terms.append(
            jnp.stack(
                [
                    jnp.sum(valid_rows * result * result),
                    jnp.sum(valid_rows * attn_out * attn_out),
                    jnp.sum(valid_rows * expert_out * expert_out),
                ]
            )
        )
        kept_layers.append(
            (
                wo_part,
                w_cat,
                up_use,
                back_use,
                normed_one,
                inv_one,
                rows_one,
                query_heads,
                key_heads,
                value_heads,
                context,
                log_total,
                normed_two,
                inv_two,
                rows_two,
                router,
                router_probs,
                one_hot,
                gate_vals,
                positions,
                arrived,
                pre_act,
                activation,
                pick_index,
                chosen,
            )
        )
        hidden = result
    totals = lax.psum(jnp.stack(stat_terms), ("dp", "tensor"))
    denom = jnp.sum(counts).astype(jnp.float32) * (LEN * D)
    rms = jnp.sqrt(totals / denom)
    grad_rows = cotangent.astype(jnp.float32) * valid_rows
    gain_grads = [None] * LAYERS
    bias_grads = [None] * LAYERS
    router_grads = [None] * LAYERS
    qkv_grads = [None] * LAYERS
    out_grads = [None] * LAYERS
    up_grads = [None] * LAYERS
    back_grads = [None] * LAYERS
    for layer_idx in reversed(range(LAYERS)):
        (
            wo_part,
            w_cat,
            up_use,
            back_use,
            normed_one,
            inv_one,
            rows_one,
            query_heads,
            key_heads,
            value_heads,
            context,
            log_total,
            normed_two,
            inv_two,
            rows_two,
            router,
            router_probs,
            one_hot,
            gate_vals,
            positions,
            arrived,
            pre_act,
            activation,
            pick_index,
            chosen,
        ) = kept_layers[layer_idx]
        gain_pair = gains_all[layer_idx]
        grad_moe = gather_rows(grad_rows.astype(jnp.bfloat16))
        d_gates = jnp.einsum("rkd,rd->rk", chosen, grad_moe, preferred_element_type=jnp.float32)
        padded_down = jnp.concatenate([grad_moe, jnp.zeros((1, D), jnp.bfloat16)], axis=0)
        flat_gates = jnp.concatenate([gate_vals.reshape(-1), jnp.zeros((1,), jnp.float32)], axis=0)

        def scaled_rows(slot_index):
            filled = slot_index < 2 * rows_all
            row_index = jnp.where(filled, slot_index // 2, rows_all)
            gate_index = jnp.where(filled, slot_index, 2 * rows_all)
            return (flat_gates[gate_index][..., None] * padded_down[row_index]).astype(jnp.bfloat16)

        d_expert_rows = to_experts(scaled_rows, positions).reshape(-1, D)
        d_activation = jnp.dot(d_expert_rows, back_use, preferred_element_type=jnp.float32)
        back_grad = contract_first(d_expert_rows, activation)
        d_pre = jax.vjp(partial(jax.nn.gelu, approximate=True), pre_act)[1](d_activation)[0].astype(
            jnp.bfloat16
        )
        up_grad = contract_first(arrived, d_pre)
        d_arrived = contract_last(d_pre, up_use)
        d_slots = sum_slots(d_arrived.reshape(groups, half_slots, D))
        d_back_rows, up_pieces, back_pieces = (
            lax.all_to_all(
                d_slots.astype(jnp.bfloat16), "dp", split_axis=0, concat_axis=0, tiled=True
            ).astype(d_slots.dtype),
            lax.all_to_all(
                up_grad.reshape(groups, -1, up_grad.shape[1]).astype(jnp.bfloat16),
                "dp",
                split_axis=0,
                concat_axis=0,
                tiled=True,
            ).astype(jnp.float32),
            lax.all_to_all(
                back_grad.reshape(groups, -1, back_grad.shape[1]).astype(jnp.bfloat16),
                "dp",
                split_axis=0,
                concat_axis=0,
                tiled=True,
            ).astype(jnp.float32),
        )
        up_grads[layer_idx] = up_pieces.reshape(
            experts, 2, up_pieces.shape[1], up_pieces.shape[2]
        ).sum(axis=1)
        back_grads[layer_idx] = back_pieces.reshape(
            experts, 2, back_pieces.shape[1], back_pieces.shape[2]
        ).sum(axis=1)
        padded_back = jnp.concatenate(
            [d_back_rows.reshape(groups * quarter, D), jnp.zeros((1, D), jnp.float32)], axis=0
        )
        d_rows_two = jnp.sum(padded_back[pick_index], axis=1)
        d_probs = jnp.sum(jnp.where(one_hot, d_gates[:, :, None], 0.0), axis=1)
        d_logits = router_probs * (
            d_probs - jnp.sum(router_probs * d_probs, axis=-1, keepdims=True)
        )
        d_rows_two = d_rows_two + jnp.dot(d_logits, router.astype(jnp.float32).T, precision=highest)
        router_grads[layer_idx] = jnp.dot(
            rows_two.astype(jnp.float32).T, d_logits, precision=highest
        )
        d_second = sum_rows(d_rows_two)
        d_resid, gain_two, bias_two = norm_backward(d_second, normed_two, inv_two, gain_pair[1])
        grad_rows = grad_rows + d_resid
        grad_attn = gather_rows(grad_rows.astype(jnp.bfloat16))
        d_context = contract_last(grad_attn, wo_part).astype(jnp.bfloat16)
        out_grad = contract_first(context, grad_attn)
        d_queries, d_keys, d_values = lax.map(
            partial(attend_back, key_keep=key_keep, score_scale=score_scale),
            (query_heads, key_heads, value_heads, split_heads(d_context), log_total),
        )
        d_mixed = jnp.concatenate(
            [
                d_queries.reshape(rows_all, head_cols),
                d_keys.reshape(rows_all, head_cols),
                d_values.reshape(rows_all, head_cols),
            ],
            axis=1,
        )
        cat_grad = contract_first(rows_one, d_mixed)
        qkv_grad = jnp.stack(
            [
                cat_grad[:, :head_cols],
                cat_grad[:, head_cols : 2 * head_cols],
                cat_grad[:, 2 * head_cols :],
            ]
        )
        qkv_grads[layer_idx], out_grads[layer_idx] = (
            lax.psum_scatter(qkv_grad, "dp", scatter_dimension=1, tiled=True),
            lax.psum_scatter(out_grad, "dp", scatter_dimension=1, tiled=True),
        )
        d_first = sum_rows(contract_last(d_mixed, w_cat))
        d_hidden, gain_one, bias_one = norm_backward(d_first, normed_one, inv_one, gain_pair[0])
        grad_rows = grad_rows + d_hidden
        gain_grads[layer_idx] = jnp.stack([gain_one, gain_two])
        bias_grads[layer_idx] = jnp.stack([bias_one, bias_two])
    grad_gain, grad_bias, grad_router = (
        lax.psum_scatter(
            jnp.stack(gain_grads).reshape(-1), ("dp", "tensor"), scatter_dimension=0, tiled=True
        ),
        lax.psum_scatter(
            jnp.stack(bias_grads).reshape(-1), ("dp", "tensor"), scatter_dimension=0, tiled=True
        ),
        lax.psum_scatter(
            jnp.stack(router_grads).reshape(-1), ("dp", "tensor"), scatter_dimension=0, tiled=True
        ),
    )
    return (
        hidden,
        grad_rows,
        grad_gain,
        grad_bias,
        grad_router,
        jnp.stack(qkv_grads),
        jnp.stack(out_grads),
        jnp.stack(up_grads),
        jnp.stack(back_grads),
        rms,
    )


bf16 = jnp.bfloat16
f32 = jnp.float32
MESH = pl.DeviceIdType.MESH
VMEM_LIMIT = 60 * 1024 * 1024
EXPERTS = 4
HEADS_PART = 3
QKV = 3 * HEADS_PART * HD


def nn(left, right):
    return jnp.dot(left, right, preferred_element_type=f32)


def nt(left, right):
    return lax.dot_general(left, right, (((1,), (1,)), ((), ())), preferred_element_type=f32)


def tn(left, right):
    return lax.dot_general(left, right, (((0,), (0,)), ((), ())), preferred_element_type=f32)


def group_of(kind):
    dp, part = lax.axis_index("dp"), lax.axis_index("tensor")
    if kind == "plane":
        return dp // 2, 4, lambda place: (place * 2 + dp % 2, part)
    if kind == "column":
        return part, 4, lambda place: (dp, place)
    if kind == "chip":
        return dp % 2, 2, lambda place: (dp // 2 * 2 + place, part)
    return dp * 4 + part, 32, lambda place: (place // 4, place % 4)


def greet(devices):
    barrier = pltpu.get_barrier_semaphore()
    for device in devices:
        pl.semaphore_signal(barrier, inc=1, device_id=device, device_id_type=MESH)
    pl.semaphore_wait(barrier, len(devices))


def swap_kernel(kind, same, in_ref, out_ref, held, local_sem, send_sem, recv_sem):
    place, count, device = group_of(kind)
    others = [lax.rem(place + step, count) for step in range(1, count)]
    first = pltpu.make_async_copy(in_ref if same else in_ref.at[place], held, local_sem.at[0])
    first.start()
    greet([device(other) for other in others])
    copies = []
    for step, other in enumerate(others):
        copies.append(
            pltpu.make_async_remote_copy(
                src_ref=in_ref if same else in_ref.at[other],
                dst_ref=out_ref.at[place],
                send_sem=send_sem.at[step],
                recv_sem=recv_sem.at[step],
                device_id=device(other),
                device_id_type=MESH,
            )
        )
        copies[-1].start()
    first.wait()
    second = pltpu.make_async_copy(held, out_ref.at[place], local_sem.at[1])
    second.start()
    second.wait()
    for copy in copies:
        copy.wait()


def swap(array, kind, same, collective_id):
    count = {"plane": 4, "column": 4, "chip": 2, "all": 32}[kind]
    block = array.shape if same else array.shape[1:]
    any_spec = pl.BlockSpec(memory_space=pl.ANY)
    return pl.pallas_call(
        partial(swap_kernel, kind, same),
        out_shape=jax.ShapeDtypeStruct((count,) + block, array.dtype),
        in_specs=[any_spec],
        out_specs=any_spec,
        scratch_shapes=[
            pltpu.VMEM(block, array.dtype),
            pltpu.SemaphoreType.DMA((2,)),
            pltpu.SemaphoreType.DMA((count - 1,)),
            pltpu.SemaphoreType.DMA((count - 1,)),
        ],
        compiler_params=pltpu.CompilerParams(
            collective_id=collective_id, has_side_effects=True, vmem_limit_bytes=VMEM_LIMIT
        ),
        name=f"swap_{kind}_{collective_id}",
    )(array)


def spread_kernel(
    block_ref, small_ref, out_ref, small_out, local_sem, za_send, za_recv, yx_send, yx_recv, cc_send, cc_recv
):
    dp, part = lax.axis_index("dp"), lax.axis_index("tensor")
    place, core = dp // 2, dp % 2
    partner = (place * 2 + 1 - core, part)
    columns = [lax.rem(part + step, 4) for step in range(1, 4)]
    planes = [lax.rem(place + step, 4) for step in range(1, 4)]
    own = pltpu.make_async_copy(block_ref, out_ref.at[:, part, dp], local_sem.at[0])
    own_small = pltpu.make_async_copy(small_ref, small_out.at[part, dp], local_sem.at[1])
    own.start()
    own_small.start()
    greet(
        [(dp, other) for other in columns]
        + [(other * 2 + core, part) for other in planes]
        + [partner]
    )

    def send(src, dst, send_sem, recv_sem, device):
        copy = pltpu.make_async_remote_copy(
            src_ref=src, dst_ref=dst, send_sem=send_sem, recv_sem=recv_sem,
            device_id=device, device_id_type=MESH,
        )
        copy.start()
        return copy

    pairs = ((block_ref, out_ref), (small_ref, small_out))

    def slot(which, part_at, dp_at):
        return out_ref.at[:, part_at, dp_at] if which == 0 else small_out.at[part_at, dp_at]

    first = [
        [
            send(pairs[which][0], slot(which, part, dp), za_send.at[which, step], za_recv.at[which, step], (dp, other))
            for which in range(2)
        ]
        for step, other in enumerate(columns)
    ]
    own.wait()
    own_small.wait()
    second = [[], [], [], []]
    third = []
    for turn in range(4):
        part_at = lax.rem(part + 4 - turn, 4)
        if turn:
            for copy in first[turn - 1]:
                copy.wait()
        for step, other in enumerate(planes):
            for which in range(2):
                second[turn].append(
                    send(
                        slot(which, part_at, dp), slot(which, part_at, dp),
                        yx_send.at[turn, which, step], yx_recv.at[turn, which, step],
                        (other * 2 + core, part),
                    )
                )
        for which in range(2):
            third.append(
                send(
                    slot(which, part_at, dp), slot(which, part_at, dp),
                    cc_send.at[turn, which, 0], cc_recv.at[turn, which, 0], partner,
                )
            )
    for turn in range(4):
        part_at = lax.rem(part + 4 - turn, 4)
        for step in range(3):
            for which in range(2):
                second[turn][step * 2 + which].wait()
                dp_at = lax.rem(place + 3 - step, 4) * 2 + core
                third.append(
                    send(
                        slot(which, part_at, dp_at), slot(which, part_at, dp_at),
                        cc_send.at[turn, which, step + 1], cc_recv.at[turn, which, step + 1], partner,
                    )
                )
    for copy in third:
        copy.wait()


def spread(block, small):
    any_spec = pl.BlockSpec(memory_space=pl.ANY)
    vmem_spec = pl.BlockSpec(memory_space=pltpu.VMEM)
    dma = pltpu.SemaphoreType.DMA
    return pl.pallas_call(
        spread_kernel,
        out_shape=(
            jax.ShapeDtypeStruct((block.shape[0], 4, 8) + block.shape[1:], block.dtype),
            jax.ShapeDtypeStruct((4, 8) + small.shape, small.dtype),
        ),
        in_specs=[vmem_spec, vmem_spec],
        out_specs=(any_spec, any_spec),
        scratch_shapes=[
            dma((2,)), dma((2, 3)), dma((2, 3)), dma((4, 2, 3)), dma((4, 2, 3)), dma((4, 2, 4)), dma((4, 2, 4)),
        ],
        compiler_params=pltpu.CompilerParams(
            collective_id=1, has_side_effects=True, vmem_limit_bytes=VMEM_LIMIT
        ),
        name="spread",
    )(block, small)


def join_kernel(in_ref, out_ref, held, local_sem, send_sem, recv_sem):
    dp, part = lax.axis_index("dp"), lax.axis_index("tensor")
    core = dp % 2
    partner = (dp // 2 * 2 + 1 - core, part)
    loads = [
        pltpu.make_async_copy(in_ref.at[:, which], held.at[which], local_sem.at[0, which])
        for which in range(2)
    ]
    for load in loads:
        load.start()
    greet([partner])
    copies = [
        pltpu.make_async_remote_copy(
            src_ref=in_ref.at[:, which],
            dst_ref=out_ref.at[which, :, core],
            send_sem=send_sem.at[which],
            recv_sem=recv_sem.at[which],
            device_id=partner,
            device_id_type=MESH,
        )
        for which in range(2)
    ]
    for copy in copies:
        copy.start()
    stores = [
        pltpu.make_async_copy(held.at[which], out_ref.at[which, :, core], local_sem.at[1, which])
        for which in range(2)
    ]
    for which in range(2):
        loads[which].wait()
        stores[which].start()
    for copy in stores + copies:
        copy.wait()


def join(pieces):
    any_spec = pl.BlockSpec(memory_space=pl.ANY)
    dma = pltpu.SemaphoreType.DMA
    count, _, rows, width = pieces.shape
    return pl.pallas_call(
        join_kernel,
        out_shape=jax.ShapeDtypeStruct((2, count, 2, rows, width), pieces.dtype),
        in_specs=[any_spec],
        out_specs=any_spec,
        scratch_shapes=[
            pltpu.VMEM((2, count, rows, width), pieces.dtype), dma((2, 2)), dma((2,)), dma((2,)),
        ],
        compiler_params=pltpu.CompilerParams(
            collective_id=2, has_side_effects=True, vmem_limit_bytes=VMEM_LIMIT
        ),
        name="join",
    )(pieces)


def standard(rows):
    centred = rows - jnp.mean(rows, axis=-1, keepdims=True)
    inv_std = lax.rsqrt(jnp.mean(centred * centred, axis=-1, keepdims=True) + eps_norm)
    return centred * inv_std, inv_std


def lane_put(table, lane, column):
    lanes = lax.broadcasted_iota(jnp.int32, table.shape, 1)
    return jnp.where(lanes == lane, column, table)


def masked_scores(query, key):
    scores = nt(query, key) * (HD ** (-0.5))
    slots = lax.broadcasted_iota(jnp.int32, scores.shape, 1)
    return jnp.where(slots < LEN, scores, far_negative)


def attend_kernel(
    hidden_ref, weight_ref, vec_ref, router_ref,
    resid_ref, second_ref, saved_ref, table_ref, logs_ref, first_sc, attn_sc,
):
    turn = pl.program_id(0)
    images = hidden_ref.shape[0] // SEQ

    @pl.when(turn == 0)
    def _():
        normed, _ = standard(hidden_ref[...].astype(f32))
        first_sc[...] = (normed * vec_ref[0:1] + vec_ref[1:2]).astype(bf16)
        attn_sc[...] = jnp.zeros_like(attn_sc)

    for image in range(images):
        rows = pl.ds(image * SEQ, SEQ)
        mixed = nn(first_sc[rows, :], weight_ref[0, :, :QKV]).astype(bf16)
        logs = jnp.zeros((SEQ, 128), f32)
        contexts = []
        for head in range(HEADS_PART):
            query, key, value = [
                mixed[:, (kind * HEADS_PART + head) * HD : (kind * HEADS_PART + head + 1) * HD]
                for kind in range(3)
            ]
            scores = masked_scores(query, key)
            top = jnp.max(scores, axis=-1, keepdims=True)
            grown = jnp.exp(scores - top)
            total = jnp.sum(grown, axis=-1, keepdims=True)
            weights = (grown / total).astype(bf16)
            contexts.append(nn(weights, value).astype(bf16))
            logs = lane_put(logs, head, top + jnp.log(total))
        context = jnp.concatenate(contexts, axis=1)
        saved_ref[0, rows, :] = jnp.concatenate([mixed, context], axis=1)
        logs_ref[0, rows, :] = logs
        attn_sc[rows, :] += nt(context, weight_ref[0, :, QKV:])

    @pl.when(turn == pl.num_programs(0) - 1)
    def _():
        attn = attn_sc[...]
        resid = hidden_ref[...].astype(f32) + attn
        resid_ref[...] = resid
        normed, _ = standard(resid)
        second = (normed * vec_ref[2:3] + vec_ref[3:4]).astype(bf16)
        second_ref[...] = second
        logits = nn(second, router_ref[...])
        lanes = lax.broadcasted_iota(jnp.int32, logits.shape, 1)
        logits = jnp.where(lanes < EXPERTS, logits, far_negative)
        grown = jnp.exp(logits - jnp.max(logits, axis=-1, keepdims=True))
        probs = grown / jnp.sum(grown, axis=-1, keepdims=True)
        table_ref[...] = lane_put(probs, EXPERTS, jnp.sum(attn * attn, axis=-1, keepdims=True))


def attend_rows(hidden, weights, vecs, router):
    rows = hidden.shape[0]
    whole = lambda shape: pl.BlockSpec(shape, lambda turn: (0,) * len(shape))
    by_part = lambda shape: pl.BlockSpec((1,) + shape, lambda turn: (turn, 0, 0))
    return pl.pallas_call(
        attend_kernel,
        grid=(4,),
        in_specs=[whole((rows, D)), by_part((D, D)), whole((8, D)), whole((D, 128))],
        out_specs=(
            whole((rows, D)), whole((rows, D)), by_part((rows, D)), whole((rows, 128)), by_part((rows, 128)),
        ),
        out_shape=(
            jax.ShapeDtypeStruct((rows, D), f32),
            jax.ShapeDtypeStruct((rows, D), bf16),
            jax.ShapeDtypeStruct((4, rows, D), bf16),
            jax.ShapeDtypeStruct((rows, 128), f32),
            jax.ShapeDtypeStruct((4, rows, 128), f32),
        ),
        scratch_shapes=[pltpu.VMEM((rows, D), bf16), pltpu.VMEM((rows, D), f32)],
        compiler_params=pltpu.CompilerParams(vmem_limit_bytes=VMEM_LIMIT),
        name="attend_rows",
    )(hidden, weights, vecs, router)


def norm_pull(grad, normed, inv_std, gain):
    scaled = grad * gain
    one = jnp.mean(scaled, axis=-1, keepdims=True)
    two = jnp.mean(scaled * normed, axis=-1, keepdims=True)
    return inv_std * (scaled - one - normed * two)


def attend_pull_kernel(
    grad_ref, moved_ref, hidden_ref, resid_ref, saved_ref, table_ref, logs_ref, dprob_ref,
    weight_ref, vec_ref, router_ref,
    out_ref, wgrad_ref, small_ref, rgrad_ref,
    first_sc, grad_sc, low_sc, back_sc,
):
    turn = pl.program_id(0)
    rows_all = grad_ref.shape[0]
    images = rows_all // SEQ
    scale = HD ** (-0.5)

    @pl.when(turn == 0)
    def _():
        normed, inv_std = standard(resid_ref[...])
        second = (normed * vec_ref[2:3] + vec_ref[3:4]).astype(bf16)
        lanes = lax.broadcasted_iota(jnp.int32, (rows_all, 128), 1)
        probs = jnp.where(lanes < EXPERTS, table_ref[...], 0.0)
        dprobs = dprob_ref[...]
        dlogit = probs * (dprobs - jnp.sum(probs * dprobs, axis=-1, keepdims=True))
        high = dlogit.astype(bf16)
        low = (dlogit - high.astype(f32)).astype(bf16)
        rgrad_ref[...] = tn(second, high) + tn(second, low)
        dsecond = nt(high, router_ref[...]) + nt(low, router_ref[...])
        for expert in range(EXPERTS):
            dsecond = dsecond + moved_ref[expert].astype(f32)
        small_ref[2:3] = jnp.sum(dsecond * normed, axis=0, keepdims=True)
        small_ref[3:4] = jnp.sum(dsecond, axis=0, keepdims=True)
        grad = grad_ref[...] + norm_pull(dsecond, normed, inv_std, vec_ref[2:3])
        grad_sc[...] = grad
        low_sc[...] = grad.astype(bf16)
        normed, _ = standard(hidden_ref[...].astype(f32))
        first_sc[...] = (normed * vec_ref[0:1] + vec_ref[1:2]).astype(bf16)
        back_sc[...] = jnp.zeros_like(back_sc)

    mixed_grads = []
    for image in range(images):
        rows = pl.ds(image * SEQ, SEQ)
        saved = saved_ref[0, rows, :]
        dcontext = nn(low_sc[rows, :], weight_ref[0, :, QKV:]).astype(bf16)
        pieces = [[], [], []]
        for head in range(HEADS_PART):
            query, key, value = [
                saved[:, (kind * HEADS_PART + head) * HD : (kind * HEADS_PART + head + 1) * HD]
                for kind in range(3)
            ]
            dhead = dcontext[:, head * HD : (head + 1) * HD]
            weights = jnp.exp(masked_scores(query, key) - logs_ref[0, rows, head : head + 1])
            dvalue = tn(weights.astype(bf16), dhead)
            dweights = nt(dhead, value)
            inner = jnp.sum(weights * dweights, axis=-1, keepdims=True)
            dscores = (weights * (dweights - inner)).astype(bf16)
            pieces[0].append((nn(dscores, key) * scale).astype(bf16))
            pieces[1].append((tn(dscores, query) * scale).astype(bf16))
            pieces[2].append(dvalue.astype(bf16))
        mixed = jnp.concatenate(pieces[0] + pieces[1] + pieces[2], axis=1)
        back_sc[rows, :] += nt(mixed, weight_ref[0, :, :QKV])
        mixed_grads.append(mixed)
    mixed = jnp.concatenate(mixed_grads, axis=0)
    wgrad_ref[0, :, :QKV] = tn(first_sc[...], mixed).astype(bf16)
    wgrad_ref[0, :, QKV:] = tn(low_sc[...], saved_ref[0, :, QKV:]).astype(bf16)

    @pl.when(turn == pl.num_programs(0) - 1)
    def _():
        dfirst = back_sc[...]
        normed, inv_std = standard(hidden_ref[...].astype(f32))
        small_ref[0:1] = jnp.sum(dfirst * normed, axis=0, keepdims=True)
        small_ref[1:2] = jnp.sum(dfirst, axis=0, keepdims=True)
        small_ref[4:8] = jnp.zeros((4, D), f32)
        out_ref[...] = grad_sc[...] + norm_pull(dfirst, normed, inv_std, vec_ref[0:1])


def attend_pull(grad, moved, hidden, resid, saved, table, logs, dprob, weights, vecs, router):
    rows = grad.shape[0]
    whole = lambda shape: pl.BlockSpec(shape, lambda turn: (0,) * len(shape))
    by_part = lambda shape: pl.BlockSpec((1,) + shape, lambda turn: (turn, 0, 0))
    return pl.pallas_call(
        attend_pull_kernel,
        grid=(4,),
        in_specs=[
            whole((rows, D)), whole((EXPERTS, rows, D)), whole((rows, D)), whole((rows, D)),
            by_part((rows, D)), whole((rows, 128)), by_part((rows, 128)), whole((rows, 128)),
            by_part((D, D)), whole((8, D)), whole((D, 128)),
        ],
        out_specs=(whole((rows, D)), by_part((D, D)), whole((8, D)), whole((D, 128))),
        out_shape=(
            jax.ShapeDtypeStruct((rows, D), f32),
            jax.ShapeDtypeStruct((4, D, D), bf16),
            jax.ShapeDtypeStruct((8, D), f32),
            jax.ShapeDtypeStruct((D, 128), f32),
        ),
        scratch_shapes=[
            pltpu.VMEM((rows, D), bf16), pltpu.VMEM((rows, D), f32),
            pltpu.VMEM((rows, D), bf16), pltpu.VMEM((rows, D), f32),
        ],
        compiler_params=pltpu.CompilerParams(vmem_limit_bytes=VMEM_LIMIT),
        name="attend_pull",
    )(grad, moved, hidden, resid, saved, table, logs, dprob, weights, vecs, router)


GELU_C = math.sqrt(2.0 / math.pi)
GELU_K = 0.044715


def gelu_pair(pre):
    square = pre * pre
    bent = jnp.tanh(GELU_C * pre * (1.0 + GELU_K * square))
    half = 0.5 * (1.0 + bent)
    slope = half + (0.5 * GELU_C) * pre * (1.0 - bent * bent) * (1.0 + (3.0 * GELU_K) * square)
    return pre * half, slope


TILE = 256


def expert_kernel(rows_ref, weight_ref, out_ref, act_ref, slope_ref, sum_sc):
    turn = pl.program_id(1)
    for at in range(0, rows_ref.shape[1], TILE):
        tile = pl.ds(at, TILE)
        act, slope = gelu_pair(nn(rows_ref[0, tile, :], weight_ref[0, turn]))
        act = act.astype(bf16)
        act_ref[0, tile, :] = act
        slope_ref[0, tile, :] = slope.astype(bf16)
        part = nt(act, weight_ref[1, turn])
        sum_sc[tile, :] = jnp.where(turn == 0, part, sum_sc[tile, :] + part)

    @pl.when(turn == pl.num_programs(1) - 1)
    def _():
        out_ref[0] = sum_sc[...].astype(bf16)


def expert_rows(rows, weights):
    groups, count, _ = rows.shape
    return pl.pallas_call(
        expert_kernel,
        grid=(groups, 4),
        in_specs=[
            pl.BlockSpec((1, count, D), lambda at, turn: (at, 0, 0)),
            pl.BlockSpec((2, 4, D, D), lambda at, turn: (0, 0, 0, 0), pipeline_mode=pl.Buffered(1)),
        ],
        out_specs=(
            pl.BlockSpec((1, count, D), lambda at, turn: (at, 0, 0)),
            pl.BlockSpec((1, count, D), lambda at, turn: (turn, at, 0)),
            pl.BlockSpec((1, count, D), lambda at, turn: (turn, at, 0)),
        ),
        out_shape=(
            jax.ShapeDtypeStruct((groups, count, D), bf16),
            jax.ShapeDtypeStruct((4, groups * count, D), bf16),
            jax.ShapeDtypeStruct((4, groups * count, D), bf16),
        ),
        scratch_shapes=[pltpu.VMEM((count, D), f32)],
        compiler_params=pltpu.CompilerParams(vmem_limit_bytes=VMEM_LIMIT),
        name="expert_rows",
    )(rows, weights)


def expert_pull_kernel(rows_ref, grad_ref, act_ref, slope_ref, weight_ref, out_ref, wgrad_ref, sum_sc, pre_sc):
    step = pl.program_id(0)
    groups, count, _ = rows_ref.shape
    last = groups * 4

    @pl.when(step < last)
    def _():
        at, turn = step // 4, step % 4
        for place in range(0, count, TILE):
            tile = pl.ds(place, TILE)
            dact = nn(grad_ref[at, tile, :], weight_ref[1, turn])
            dpre = (slope_ref[0, tile, :].astype(f32) * dact).astype(bf16)
            pre_sc[turn, pl.ds(at * count + place, TILE), :] = dpre
            part = nt(dpre, weight_ref[0, turn])
            sum_sc[tile, :] = jnp.where(turn == 0, part, sum_sc[tile, :] + part)

        @pl.when(turn == 3)
        def _():
            out_ref[0] = sum_sc[...].astype(bf16)

    @pl.when(step >= last)
    def _():
        turn = step - last
        rows = rows_ref[...].reshape(groups * count, D)
        grads = grad_ref[...].reshape(groups * count, D)
        wgrad_ref[0, 0] = tn(rows, pre_sc[turn]).astype(bf16)
        wgrad_ref[1, 0] = tn(grads, act_ref[0]).astype(bf16)


def expert_pull(rows, grads, act, slope, weights):
    groups, count, _ = rows.shape
    last = groups * 4
    early = lambda step: jnp.minimum(step, last - 1)
    late = lambda step: jnp.maximum(step - last, 0)
    whole = lambda shape: pl.BlockSpec(
        shape, lambda step: (0,) * len(shape), pipeline_mode=pl.Buffered(1)
    )
    return pl.pallas_call(
        expert_pull_kernel,
        grid=(last + 4,),
        in_specs=[
            whole((groups, count, D)),
            whole((groups, count, D)),
            pl.BlockSpec((1, groups * count, D), lambda step: (late(step), 0, 0)),
            pl.BlockSpec((1, count, D), lambda step: (early(step) % 4, early(step) // 4, 0)),
            whole((2, 4, D, D)),
        ],
        out_specs=(
            pl.BlockSpec((1, count, D), lambda step: (early(step) // 4, 0, 0)),
            pl.BlockSpec((2, 1, D, D), lambda step: (0, late(step), 0, 0)),
        ),
        out_shape=(
            jax.ShapeDtypeStruct((groups, count, D), bf16),
            jax.ShapeDtypeStruct((2, 4, D, D), bf16),
        ),
        scratch_shapes=[
            pltpu.VMEM((count, D), f32),
            pltpu.VMEM((4, groups * count, D), bf16),
        ],
        compiler_params=pltpu.CompilerParams(vmem_limit_bytes=VMEM_LIMIT),
        name="expert_pull",
    )(rows, grads, act, slope, weights)


def add_up(pieces, own):
    return sum(pieces[at].astype(f32) for at in range(pieces.shape[0])).astype(own)


def per_device(
    tokens, counts, routes, norm_gain, norm_bias, w_router, w_qkv, w_out, w_in, w_back, cotangent
):
    dp, part = lax.axis_index("dp"), lax.axis_index("tensor")
    core = dp % 2
    own_rows = tokens.shape[0]
    slices = D // 8
    row_ids = part * own_rows + jnp.arange(own_rows, dtype=jnp.int32)
    image_count = lax.dynamic_index_in_dim(counts, dp, keepdims=False)
    valid = ((row_ids // SEQ < image_count) & (row_ids % SEQ < LEN)).astype(f32)[:, None]
    my_routes = lax.dynamic_slice_in_dim(routes, part * own_rows, own_rows, axis=1)
    chosen = (my_routes[:, :, :, None] == jnp.arange(EXPERTS)).any(axis=2)

    pieces = []
    for layer in range(LAYERS):
        packed = jnp.stack([w_in[layer], w_back[layer]], axis=1)
        arrived = swap(packed, "plane", False, 3)
        pieces.append(lax.all_gather(arrived, "tensor", axis=0, tiled=True))

    mixed_in = jnp.transpose(w_qkv, (0, 2, 1, 3)).reshape(LAYERS, slices, QKV)
    attn_block = jnp.concatenate([mixed_in, jnp.transpose(w_out, (0, 2, 1))], axis=2)
    small = jnp.concatenate([norm_gain, norm_bias, w_router])
    small = jnp.pad(small, (0, 2048 - small.shape[0])).reshape(16, 128)
    attn_all, small_all = spread(attn_block, small)
    attn_all = attn_all.reshape(LAYERS, 4, D, D)
    flat = jnp.transpose(small_all.reshape(4, 8, 2048), (1, 0, 2)).reshape(32, 2048)
    vec_count = LAYERS * 2 * D // 32
    gains = flat[:, :vec_count].reshape(LAYERS, 2, D).astype(f32)
    biases = flat[:, vec_count : 2 * vec_count].reshape(LAYERS, 2, D).astype(f32)
    routers = flat[:, 2 * vec_count : 2 * vec_count + LAYERS * D * EXPERTS // 32]
    routers = jnp.pad(routers.reshape(LAYERS, D, EXPERTS), ((0, 0), (0, 0), (0, 128 - EXPERTS)))
    vecs = jnp.pad(
        jnp.stack([gains[:, 0], biases[:, 0], gains[:, 1], biases[:, 1]], axis=1), ((0, 0), (0, 4), (0, 0))
    )

    hidden = tokens
    kept = []
    stats = []
    for layer in range(LAYERS):
        resid, second, saved, table, logs = attend_rows(hidden, attn_all[layer], vecs[layer], routers[layer])
        rows = swap(second, "plane", True, 4)
        weights = join(pieces[layer]).reshape(2, 4, D, D)
        made, act, slope = expert_rows(rows, weights)
        back = swap(made, "plane", False, 5)
        gates = jnp.where(chosen[layer], table[:, :EXPERTS], 0.0)
        moe = sum(gates[:, e : e + 1] * back[e].astype(f32) for e in range(EXPERTS))
        result = resid + moe
        stats.append(
            jnp.stack(
                [
                    jnp.sum(valid * result * result),
                    jnp.sum(valid[:, 0] * table[:, EXPERTS]),
                    jnp.sum(valid * moe * moe),
                ]
            )
        )
        kept.append((hidden, resid, saved, table, logs, rows, weights, act, slope, back, gates))
        hidden = result

    grad = cotangent.astype(f32) * valid
    attn_grads, expert_grads, small_grads, router_grads = [], [], [], []
    for layer in reversed(range(LAYERS)):
        before, resid, saved, table, logs, rows, weights, act, slope, back, gates = kept[layer]
        low = grad.astype(bf16)
        dgate = [jnp.sum(back[e].astype(f32) * low.astype(f32), axis=-1) for e in range(EXPERTS)]
        dprob = jnp.where(chosen[layer], jnp.stack(dgate, axis=1), 0.0)
        dprob = jnp.pad(dprob, ((0, 0), (0, 128 - EXPERTS)))
        sent = jnp.stack([(gates[:, e : e + 1] * low.astype(f32)).astype(bf16) for e in range(EXPERTS)])
        arrived = swap(sent, "plane", False, 5)
        drows, wgrad = expert_pull(rows, arrived, act, slope, weights)
        moved = swap(drows, "plane", False, 5)
        wgrad = wgrad.reshape(2, 4, 4, 2, slices, D)
        halves = jnp.transpose(wgrad, (3, 1, 2, 0, 4, 5))
        halves = add_up(swap(halves, "chip", False, 6), bf16)
        summed = lax.psum_scatter(halves, "tensor", scatter_dimension=0, tiled=False)
        expert_grads.append(summed)
        grad, attn_wgrad, small_grad, router_grad = attend_pull(
            grad, moved, before, resid, saved, table, logs, dprob, attn_all[layer], vecs[layer], routers[layer]
        )
        attn_wgrad = jnp.transpose(attn_wgrad.reshape(4, 4, 2, slices, D), (2, 1, 0, 3, 4))
        attn_wgrad = add_up(swap(attn_wgrad, "chip", False, 7), bf16)
        attn_wgrad = add_up(swap(attn_wgrad, "plane", False, 8), bf16)
        attn_wgrad = add_up(swap(attn_wgrad, "column", False, 9), f32)
        attn_grads.append(attn_wgrad)
        small_grads.append(small_grad[:4])
        router_grads.append(router_grad[:, :EXPERTS])
    owned = [swap(each, "plane", False, 10) for each in expert_grads]
    for listed in (attn_grads, owned, small_grads, router_grads):
        listed.reverse()

    vec_grads = jnp.stack(small_grads).reshape(LAYERS, 2, 2, D)
    packed = jnp.concatenate(
        [
            vec_grads[:, :, 0].reshape(32, -1),
            vec_grads[:, :, 1].reshape(32, -1),
            jnp.stack(router_grads).reshape(32, -1),
            jnp.broadcast_to(jnp.stack(stats).reshape(1, -1), (32, 3 * LAYERS)),
        ],
        axis=1,
    )
    packed = jnp.pad(packed, ((0, 0), (0, 1024 - packed.shape[1]))).reshape(32, 8, 128)
    total = jnp.sum(swap(packed, "all", False, 11), axis=0).reshape(-1)
    share = LAYERS * 2 * D // 32
    router_share = LAYERS * D * EXPERTS // 32
    at = 2 * share + router_share
    denom = jnp.sum(counts).astype(f32) * (LEN * D)
    rms = jnp.sqrt(total[at : at + 3 * LAYERS].reshape(LAYERS, 3) / denom)
    attn_grad = jnp.stack(attn_grads)
    qkv_grad = jnp.transpose(attn_grad[:, :, :QKV].reshape(LAYERS, slices, 3, QKV // 3), (0, 2, 1, 3))
    out_grad = jnp.transpose(attn_grad[:, :, QKV:], (0, 2, 1))
    expert_grad = jnp.stack(owned).astype(f32)
    return (
        hidden,
        grad,
        total[:share],
        total[share : 2 * share],
        total[2 * share : at],
        qkv_grad,
        out_grad,
        expert_grad[:, :, 0],
        expert_grad[:, :, 1],
        rms,
    )


def solution(mesh):
    return jax.shard_map(
        per_device if mesh.shape["dp"] == 8 else per_device_general,
        mesh=mesh,
        in_specs=(
            P(("dp", "tensor"), None),
            P(),
            P(None, "dp", None),
            P(("dp", "tensor")),
            P(("dp", "tensor")),
            P(("dp", "tensor")),
            P(None, None, "dp", "tensor"),
            P(None, "tensor", "dp"),
            P(None, None, "dp", "tensor"),
            P(None, None, "dp", "tensor"),
            P(("dp", "tensor"), None),
        ),
        out_specs=(
            P(("dp", "tensor"), None),
            P(("dp", "tensor"), None),
            P(("dp", "tensor")),
            P(("dp", "tensor")),
            P(("dp", "tensor")),
            P(None, None, "dp", "tensor"),
            P(None, "tensor", "dp"),
            P(None, None, "dp", "tensor"),
            P(None, None, "dp", "tensor"),
            P(),
        ),
        check_vma=False,
    )
```

```python
from functools import partial
import math

import jax
import jax.numpy as jnp
from jax import lax
from jax.experimental import pallas as pl
from jax.experimental.pallas import tpu as pltpu
from jax.sharding import PartitionSpec as P

D = 768
HD = 64
LEN = 197
SEQ = 256
LAYERS = 2


eps_norm = 1e-06
far_negative = -1e30
highest = lax.Precision.HIGHEST


def norm_forward(row_vals, gain_vec, bias_vec):
    row_mean = jnp.mean(row_vals, axis=-1, keepdims=True)
    centred = row_vals - row_mean
    row_var = jnp.mean(centred * centred, axis=-1, keepdims=True)
    inv_std = lax.rsqrt(row_var + eps_norm)
    normed = centred * inv_std
    return (normed * gain_vec + bias_vec, normed, inv_std)


def norm_backward(grad_vals, normed, inv_std, gain_vec):
    gain_grad = jnp.sum(grad_vals * normed, axis=0)
    bias_grad = jnp.sum(grad_vals, axis=0)
    scaled = grad_vals * gain_vec
    mean_one = jnp.mean(scaled, axis=-1, keepdims=True)
    mean_two = jnp.mean(scaled * normed, axis=-1, keepdims=True)
    return (inv_std * (scaled - mean_one - normed * mean_two), gain_grad, bias_grad)


def gather_rows(row_vals):
    return lax.all_gather(row_vals, "tensor", axis=0, tiled=True)


def sum_rows(row_vals):
    return lax.psum_scatter(
        row_vals.astype(jnp.bfloat16), "tensor", scatter_dimension=0, tiled=True
    ).astype(jnp.float32)


def sum_slots(slot_vals):
    return lax.psum_scatter(
        slot_vals.astype(jnp.bfloat16), "tensor", scatter_dimension=1, tiled=True
    ).astype(jnp.float32)


def to_experts(make_rows, positions):
    return lax.all_to_all(make_rows(positions), "dp", split_axis=0, concat_axis=0, tiled=True)


def attend(block_in, key_keep, score_scale):
    query_heads, key_heads, value_heads = block_in
    scores = (
        jnp.einsum("iqhd,ikhd->ihqk", query_heads, key_heads, preferred_element_type=jnp.float32)
        * score_scale
    )
    scores = jnp.where(key_keep, scores, far_negative)
    row_max = jnp.max(scores, axis=-1, keepdims=True)
    exponent = jnp.exp(scores - row_max)
    row_total = jnp.sum(exponent, axis=-1, keepdims=True)
    weights = (exponent / row_total).astype(jnp.bfloat16)
    context = jnp.einsum(
        "ihqk,ikhd->iqhd", weights, value_heads, preferred_element_type=jnp.float32
    )
    return (context.astype(jnp.bfloat16), (row_max + jnp.log(row_total))[..., 0])


def attend_back(block_in, key_keep, score_scale):
    query_heads, key_heads, value_heads, d_context, log_total = block_in
    scores = (
        jnp.einsum("iqhd,ikhd->ihqk", query_heads, key_heads, preferred_element_type=jnp.float32)
        * score_scale
    )
    scores = jnp.where(key_keep, scores, far_negative)
    weights = jnp.exp(scores - log_total[..., None])
    d_values = jnp.einsum(
        "ihqk,iqhd->ikhd",
        weights.astype(jnp.bfloat16),
        d_context,
        preferred_element_type=jnp.float32,
    )
    d_weights = jnp.einsum(
        "iqhd,ikhd->ihqk", d_context, value_heads, preferred_element_type=jnp.float32
    )
    inner_sum = jnp.sum(weights * d_weights, axis=-1, keepdims=True)
    d_scores = (weights * (d_weights - inner_sum)).astype(jnp.bfloat16)
    d_queries = (
        jnp.einsum("ihqk,ikhd->iqhd", d_scores, key_heads, preferred_element_type=jnp.float32)
        * score_scale
    )
    d_keys = (
        jnp.einsum("ihqk,iqhd->ikhd", d_scores, query_heads, preferred_element_type=jnp.float32)
        * score_scale
    )
    return (
        d_queries.astype(jnp.bfloat16),
        d_keys.astype(jnp.bfloat16),
        d_values.astype(jnp.bfloat16),
    )


def contract_first(left_mat, right_mat):
    return lax.dot_general(
        left_mat, right_mat, (((0,), (0,)), ((), ())), preferred_element_type=jnp.float32
    )


def contract_last(left_mat, right_mat):
    return lax.dot_general(
        left_mat, right_mat, (((1,), (1,)), ((), ())), preferred_element_type=jnp.float32
    )


def per_device_general(
    tokens, counts, routes, norm_gain, norm_bias, w_router, w_qkv, w_out, w_in, w_back, cotangent
):
    groups = lax.axis_size("dp")
    parts = lax.axis_size("tensor")
    experts = groups // 2
    group_idx = lax.axis_index("dp")
    my_part = lax.axis_index("tensor")
    own_rows = tokens.shape[0]
    rows_all = own_rows * parts
    slot_count = 3 * rows_all // experts
    half_slots = slot_count // 2
    quarter = half_slots // parts
    score_scale = HD ** (-0.5)
    images = rows_all // SEQ
    per_block = math.gcd(images, max(1, 512 // SEQ))
    blocks = images // per_block
    head_cols = w_qkv.shape[-1]
    heads_here = head_cols // HD
    key_keep = jnp.arange(SEQ) < LEN
    gain_flat, bias_flat, router_flat = (
        lax.all_gather(norm_gain, ("dp", "tensor"), axis=0, tiled=True),
        lax.all_gather(norm_bias, ("dp", "tensor"), axis=0, tiled=True),
        lax.all_gather(w_router, ("dp", "tensor"), axis=0, tiled=True),
    )
    gains_all = gain_flat.astype(jnp.float32).reshape(LAYERS, 2, D)
    biases_all = bias_flat.astype(jnp.float32).reshape(LAYERS, 2, D)
    router_all = router_flat.reshape(LAYERS, D, experts)
    row_ids = my_part * own_rows + jnp.arange(own_rows, dtype=jnp.int32)
    image_count = lax.dynamic_index_in_dim(counts, group_idx, keepdims=False)
    valid_rows = ((row_ids // SEQ < image_count) & (row_ids % SEQ < LEN)).astype(jnp.float32)[
        :, None
    ]

    def split_heads(columns):
        return columns.reshape(blocks, per_block, SEQ, heads_here, HD)

    hidden = tokens.astype(jnp.float32)
    kept_layers = []
    stat_terms = []
    for layer_idx in range(LAYERS):
        gain_pair = gains_all[layer_idx]
        shift_pair = biases_all[layer_idx]
        wq_part, wo_part = (
            lax.all_gather(w_qkv[layer_idx], "dp", axis=1, tiled=True),
            lax.all_gather(w_out[layer_idx], "dp", axis=1, tiled=True),
        )
        w_cat = jnp.concatenate([wq_part[0], wq_part[1], wq_part[2]], axis=1)
        up_part, back_part = (
            lax.all_to_all(
                jnp.repeat(w_in[layer_idx], 2, axis=0),
                "dp",
                split_axis=0,
                concat_axis=0,
                tiled=True,
            ),
            lax.all_to_all(
                jnp.repeat(w_back[layer_idx], 2, axis=0),
                "dp",
                split_axis=0,
                concat_axis=0,
                tiled=True,
            ),
        )
        up_part = up_part.reshape(D, -1)
        back_part = back_part.reshape(D, -1)
        up_use, back_use = (up_part, back_part)
        norm_one, normed_one, inv_one = norm_forward(hidden, gain_pair[0], shift_pair[0])
        rows_one = gather_rows(norm_one.astype(jnp.bfloat16))
        qkv_rows = jnp.dot(rows_one, w_cat, preferred_element_type=jnp.float32).astype(jnp.bfloat16)
        query_heads = split_heads(qkv_rows[:, :head_cols])
        key_heads = split_heads(qkv_rows[:, head_cols : 2 * head_cols])
        value_heads = split_heads(qkv_rows[:, 2 * head_cols :])
        context, log_total = lax.map(
            partial(attend, key_keep=key_keep, score_scale=score_scale),
            (query_heads, key_heads, value_heads),
        )
        context = context.reshape(rows_all, head_cols)
        attn_out = sum_rows(jnp.dot(context, wo_part, preferred_element_type=jnp.float32))
        residual = hidden + attn_out
        norm_two, normed_two, inv_two = norm_forward(residual, gain_pair[1], shift_pair[1])
        rows_two = gather_rows(norm_two.astype(jnp.bfloat16))
        router = router_all[layer_idx]
        router_probs = jax.nn.softmax(
            jnp.dot(rows_two, router, preferred_element_type=jnp.float32), axis=-1
        )
        routing = routes[layer_idx]
        one_hot = routing[:, :, None] == jnp.arange(experts)[None, None, :]
        gate_vals = jnp.sum(jnp.where(one_hot, router_probs[:, None, :], 0.0), axis=-1)
        flat_pick = routing.reshape(-1)
        hot_int = (flat_pick[:, None] == jnp.arange(experts)[None, :]).astype(jnp.int32)
        rank_in = jnp.sum((jnp.cumsum(hot_int, axis=0) - hot_int) * hot_int, axis=1)
        target = flat_pick * slot_count + rank_in
        positions = (
            jnp.full((experts * slot_count,), 2 * rows_all, jnp.int32)
            .at[target]
            .set(jnp.arange(2 * rows_all, dtype=jnp.int32))
        )
        positions = positions.reshape(groups, half_slots)
        padded_two = jnp.concatenate([rows_two, jnp.zeros((1, D), jnp.bfloat16)], axis=0)

        def take_rows(slot_index):
            return padded_two[jnp.where(slot_index < 2 * rows_all, slot_index // 2, rows_all)]

        arrived = to_experts(take_rows, positions).reshape(-1, D)
        pre_act = jnp.dot(arrived, up_use, preferred_element_type=jnp.float32)
        activation = jax.nn.gelu(pre_act, approximate=True).astype(jnp.bfloat16)
        partial_out = contract_last(activation, back_use)
        summed = sum_slots(partial_out.reshape(groups, half_slots, D)).astype(jnp.bfloat16)
        returned = lax.all_to_all(summed, "dp", split_axis=0, concat_axis=0, tiled=True)
        slot_pair = target.reshape(rows_all, 2)
        owner = slot_pair // half_slots
        inside = slot_pair % half_slots
        in_quarter = inside // quarter == my_part
        pick_index = jnp.where(
            in_quarter, owner * quarter + inside - my_part * quarter, groups * quarter
        )
        padded_ret = jnp.concatenate(
            [returned.reshape(groups * quarter, D), jnp.zeros((1, D), jnp.bfloat16)], axis=0
        )
        chosen = padded_ret[pick_index]
        expert_out = sum_rows(jnp.sum(gate_vals[:, :, None] * chosen, axis=1))
        result = residual + expert_out
        stat_terms.append(
            jnp.stack(
                [
                    jnp.sum(valid_rows * result * result),
                    jnp.sum(valid_rows * attn_out * attn_out),
                    jnp.sum(valid_rows * expert_out * expert_out),
                ]
            )
        )
        kept_layers.append(
            (
                wo_part,
                w_cat,
                up_use,
                back_use,
                normed_one,
                inv_one,
                rows_one,
                query_heads,
                key_heads,
                value_heads,
                context,
                log_total,
                normed_two,
                inv_two,
                rows_two,
                router,
                router_probs,
                one_hot,
                gate_vals,
                positions,
                arrived,
                pre_act,
                activation,
                pick_index,
                chosen,
            )
        )
        hidden = result
    totals = lax.psum(jnp.stack(stat_terms), ("dp", "tensor"))
    denom = jnp.sum(counts).astype(jnp.float32) * (LEN * D)
    rms = jnp.sqrt(totals / denom)
    grad_rows = cotangent.astype(jnp.float32) * valid_rows
    gain_grads = [None] * LAYERS
    bias_grads = [None] * LAYERS
    router_grads = [None] * LAYERS
    qkv_grads = [None] * LAYERS
    out_grads = [None] * LAYERS
    up_grads = [None] * LAYERS
    back_grads = [None] * LAYERS
    for layer_idx in reversed(range(LAYERS)):
        (
            wo_part,
            w_cat,
            up_use,
            back_use,
            normed_one,
            inv_one,
            rows_one,
            query_heads,
            key_heads,
            value_heads,
            context,
            log_total,
            normed_two,
            inv_two,
            rows_two,
            router,
            router_probs,
            one_hot,
            gate_vals,
            positions,
            arrived,
            pre_act,
            activation,
            pick_index,
            chosen,
        ) = kept_layers[layer_idx]
        gain_pair = gains_all[layer_idx]
        grad_moe = gather_rows(grad_rows.astype(jnp.bfloat16))
        d_gates = jnp.einsum("rkd,rd->rk", chosen, grad_moe, preferred_element_type=jnp.float32)
        padded_down = jnp.concatenate([grad_moe, jnp.zeros((1, D), jnp.bfloat16)], axis=0)
        flat_gates = jnp.concatenate([gate_vals.reshape(-1), jnp.zeros((1,), jnp.float32)], axis=0)

        def scaled_rows(slot_index):
            filled = slot_index < 2 * rows_all
            row_index = jnp.where(filled, slot_index // 2, rows_all)
            gate_index = jnp.where(filled, slot_index, 2 * rows_all)
            return (flat_gates[gate_index][..., None] * padded_down[row_index]).astype(jnp.bfloat16)

        d_expert_rows = to_experts(scaled_rows, positions).reshape(-1, D)
        d_activation = jnp.dot(d_expert_rows, back_use, preferred_element_type=jnp.float32)
        back_grad = contract_first(d_expert_rows, activation)
        d_pre = jax.vjp(partial(jax.nn.gelu, approximate=True), pre_act)[1](d_activation)[0].astype(
            jnp.bfloat16
        )
        up_grad = contract_first(arrived, d_pre)
        d_arrived = contract_last(d_pre, up_use)
        d_slots = sum_slots(d_arrived.reshape(groups, half_slots, D))
        d_back_rows, up_pieces, back_pieces = (
            lax.all_to_all(
                d_slots.astype(jnp.bfloat16), "dp", split_axis=0, concat_axis=0, tiled=True
            ).astype(d_slots.dtype),
            lax.all_to_all(
                up_grad.reshape(groups, -1, up_grad.shape[1]).astype(jnp.bfloat16),
                "dp",
                split_axis=0,
                concat_axis=0,
                tiled=True,
            ).astype(jnp.float32),
            lax.all_to_all(
                back_grad.reshape(groups, -1, back_grad.shape[1]).astype(jnp.bfloat16),
                "dp",
                split_axis=0,
                concat_axis=0,
                tiled=True,
            ).astype(jnp.float32),
        )
        up_grads[layer_idx] = up_pieces.reshape(
            experts, 2, up_pieces.shape[1], up_pieces.shape[2]
        ).sum(axis=1)
        back_grads[layer_idx] = back_pieces.reshape(
            experts, 2, back_pieces.shape[1], back_pieces.shape[2]
        ).sum(axis=1)
        padded_back = jnp.concatenate(
            [d_back_rows.reshape(groups * quarter, D), jnp.zeros((1, D), jnp.float32)], axis=0
        )
        d_rows_two = jnp.sum(padded_back[pick_index], axis=1)
        d_probs = jnp.sum(jnp.where(one_hot, d_gates[:, :, None], 0.0), axis=1)
        d_logits = router_probs * (
            d_probs - jnp.sum(router_probs * d_probs, axis=-1, keepdims=True)
        )
        d_rows_two = d_rows_two + jnp.dot(d_logits, router.astype(jnp.float32).T, precision=highest)
        router_grads[layer_idx] = jnp.dot(
            rows_two.astype(jnp.float32).T, d_logits, precision=highest
        )
        d_second = sum_rows(d_rows_two)
        d_resid, gain_two, bias_two = norm_backward(d_second, normed_two, inv_two, gain_pair[1])
        grad_rows = grad_rows + d_resid
        grad_attn = gather_rows(grad_rows.astype(jnp.bfloat16))
        d_context = contract_last(grad_attn, wo_part).astype(jnp.bfloat16)
        out_grad = contract_first(context, grad_attn)
        d_queries, d_keys, d_values = lax.map(
            partial(attend_back, key_keep=key_keep, score_scale=score_scale),
            (query_heads, key_heads, value_heads, split_heads(d_context), log_total),
        )
        d_mixed = jnp.concatenate(
            [
                d_queries.reshape(rows_all, head_cols),
                d_keys.reshape(rows_all, head_cols),
                d_values.reshape(rows_all, head_cols),
            ],
            axis=1,
        )
        cat_grad = contract_first(rows_one, d_mixed)
        qkv_grad = jnp.stack(
            [
                cat_grad[:, :head_cols],
                cat_grad[:, head_cols : 2 * head_cols],
                cat_grad[:, 2 * head_cols :],
            ]
        )
        qkv_grads[layer_idx], out_grads[layer_idx] = (
            lax.psum_scatter(qkv_grad, "dp", scatter_dimension=1, tiled=True),
            lax.psum_scatter(out_grad, "dp", scatter_dimension=1, tiled=True),
        )
        d_first = sum_rows(contract_last(d_mixed, w_cat))
        d_hidden, gain_one, bias_one = norm_backward(d_first, normed_one, inv_one, gain_pair[0])
        grad_rows = grad_rows + d_hidden
        gain_grads[layer_idx] = jnp.stack([gain_one, gain_two])
        bias_grads[layer_idx] = jnp.stack([bias_one, bias_two])
    grad_gain, grad_bias, grad_router = (
        lax.psum_scatter(
            jnp.stack(gain_grads).reshape(-1), ("dp", "tensor"), scatter_dimension=0, tiled=True
        ),
        lax.psum_scatter(
            jnp.stack(bias_grads).reshape(-1), ("dp", "tensor"), scatter_dimension=0, tiled=True
        ),
        lax.psum_scatter(
            jnp.stack(router_grads).reshape(-1), ("dp", "tensor"), scatter_dimension=0, tiled=True
        ),
    )
    return (
        hidden,
        grad_rows,
        grad_gain,
        grad_bias,
        grad_router,
        jnp.stack(qkv_grads),
        jnp.stack(out_grads),
        jnp.stack(up_grads),
        jnp.stack(back_grads),
        rms,
    )


bf16 = jnp.bfloat16
f32 = jnp.float32
MESH = pl.DeviceIdType.MESH
VMEM_LIMIT = 63 * 1024 * 1024
EXPERTS = 4
HEADS_PART = 3
QKV = 3 * HEADS_PART * HD


def nn(left, right):
    return jnp.dot(left, right, preferred_element_type=f32)


def nt(left, right):
    return lax.dot_general(left, right, (((1,), (1,)), ((), ())), preferred_element_type=f32)


def tn(left, right):
    return lax.dot_general(left, right, (((0,), (0,)), ((), ())), preferred_element_type=f32)


def group_of(kind):
    dp, part = lax.axis_index("dp"), lax.axis_index("tensor")
    if kind == "plane":
        return dp // 2, 4, lambda place: (place * 2 + dp % 2, part)
    if kind == "column":
        return part, 4, lambda place: (dp, place)
    if kind == "chip":
        return dp % 2, 2, lambda place: (dp // 2 * 2 + place, part)
    return dp * 4 + part, 32, lambda place: (place // 4, place % 4)


def greet(devices):
    barrier = pltpu.get_barrier_semaphore()
    for device in devices:
        pl.semaphore_signal(barrier, inc=1, device_id=device, device_id_type=MESH)
    pl.semaphore_wait(barrier, len(devices))


def swap_kernel(kind, same, in_ref, out_ref, held, local_sem, send_sem, recv_sem):
    place, count, device = group_of(kind)
    others = [lax.rem(place + step, count) for step in range(1, count)]
    first = pltpu.make_async_copy(in_ref if same else in_ref.at[place], held, local_sem.at[0])
    first.start()
    greet([device(other) for other in others])
    copies = []
    for step, other in enumerate(others):
        copies.append(
            pltpu.make_async_remote_copy(
                src_ref=in_ref if same else in_ref.at[other],
                dst_ref=out_ref.at[place],
                send_sem=send_sem.at[step],
                recv_sem=recv_sem.at[step],
                device_id=device(other),
                device_id_type=MESH,
            )
        )
        copies[-1].start()
    first.wait()
    second = pltpu.make_async_copy(held, out_ref.at[place], local_sem.at[1])
    second.start()
    second.wait()
    for copy in copies:
        copy.wait()


def swap(array, kind, same, collective_id):
    count = {"plane": 4, "column": 4, "chip": 2, "all": 32}[kind]
    block = array.shape if same else array.shape[1:]
    any_spec = pl.BlockSpec(memory_space=pl.ANY)
    return pl.pallas_call(
        partial(swap_kernel, kind, same),
        out_shape=jax.ShapeDtypeStruct((count,) + block, array.dtype),
        in_specs=[any_spec],
        out_specs=any_spec,
        scratch_shapes=[
            pltpu.VMEM(block, array.dtype),
            pltpu.SemaphoreType.DMA((2,)),
            pltpu.SemaphoreType.DMA((count - 1,)),
            pltpu.SemaphoreType.DMA((count - 1,)),
        ],
        compiler_params=pltpu.CompilerParams(
            collective_id=collective_id, has_side_effects=True, vmem_limit_bytes=VMEM_LIMIT
        ),
        name=f"swap_{kind}_{collective_id}",
    )(array)


def relatives():
    dp, part = lax.axis_index("dp"), lax.axis_index("tensor")
    place, core = dp // 2, dp % 2
    row, col = place // 2, place % 2
    near = (row * 2 + 1 - col, (1 - row) * 2 + col, (1 - row) * 2 + 1 - col)
    return place, core, part, [None] + [(at * 2 + core, part) for at in near], (place * 2 + 1 - core, part)


def push(src, dst, send_sem, recv_sem, device):
    return pltpu.make_async_remote_copy(
        src_ref=src, dst_ref=dst, send_sem=send_sem, recv_sem=recv_sem, device_id=device, device_id_type=MESH
    )


def comm_params(collective_id):
    return pltpu.CompilerParams(
        collective_id=collective_id, has_side_effects=True, vmem_limit_bytes=VMEM_LIMIT
    )


ANY_SPEC = pl.BlockSpec(memory_space=pl.ANY)
DMA = pltpu.SemaphoreType.DMA


def spread_kernel(
    block_ref, small_ref, out_ref, small_out, local_sem, za_send, za_recv, yx_send, yx_recv, cc_send, cc_recv
):
    place, core, part, near, partner = relatives()
    dp = place * 2 + core
    columns = [lax.rem(part + step, 4) for step in range(1, 4)]
    pairs = ((block_ref, out_ref), (small_ref, small_out))
    locals_ = [
        pltpu.make_async_copy(src, dst.at[dp, part], local_sem.at[which])
        for which, (src, dst) in enumerate(pairs)
    ]
    for copy in locals_:
        copy.start()
    greet([(dp, other) for other in columns] + near[1:] + [partner])
    first = [
        [
            push(src, dst.at[dp, part], za_send.at[which, step], za_recv.at[which, step], (dp, other))
            for which, (src, dst) in enumerate(pairs)
        ]
        for step, other in enumerate(columns)
    ]
    for listed in first:
        for copy in listed:
            copy.start()
    for copy in locals_:
        copy.wait()
    second = [[], [], [], []]
    third = []

    def start(listed, copy):
        copy.start()
        listed.append(copy)

    for turn in range(4):
        part_at = lax.rem(part + 4 - turn, 4)
        if turn:
            for copy in first[turn - 1]:
                copy.wait()
        for which, (_, dst) in enumerate(pairs):
            spot = dst.at[dp, part_at]
            for step in range(3):
                start(
                    second[turn],
                    push(spot, spot, yx_send.at[turn, which, step], yx_recv.at[turn, which, step], near[step + 1]),
                )
            start(third, push(spot, spot, cc_send.at[turn, which, 0], cc_recv.at[turn, which, 0], partner))
    for turn in range(4):
        part_at = lax.rem(part + 4 - turn, 4)
        for which, (_, dst) in enumerate(pairs):
            for step in range(3):
                second[turn][which * 3 + step].wait()
                spot = dst.at[near[step + 1][0], part_at]
                start(
                    third,
                    push(spot, spot, cc_send.at[turn, which, step + 1], cc_recv.at[turn, which, step + 1], partner),
                )
    for copy in third:
        copy.wait()


def spread(block, small):
    vmem_spec = pl.BlockSpec(memory_space=pltpu.VMEM)
    return pl.pallas_call(
        spread_kernel,
        out_shape=(
            jax.ShapeDtypeStruct((8, 4) + block.shape, block.dtype),
            jax.ShapeDtypeStruct((8, 4) + small.shape, small.dtype),
        ),
        in_specs=[vmem_spec, vmem_spec],
        out_specs=(ANY_SPEC, ANY_SPEC),
        scratch_shapes=[
            DMA((2,)), DMA((2, 3)), DMA((2, 3)), DMA((4, 2, 3)), DMA((4, 2, 3)), DMA((4, 2, 4)), DMA((4, 2, 4)),
        ],
        compiler_params=comm_params(1),
        name="spread",
    )(block, small)


def gather_sums_kernel(
    large_ref, small_ref, large_out, small_out,
    own_a, own_b, chip_a, chip_b, sum_a, sum_b, near_a, near_b, col_a, col_b, part_a, part_b,
    local_sem, chip_send, chip_recv, near_send, near_recv, col_send, col_recv,
):
    place, core, part, near, partner = relatives()
    dp = place * 2 + core
    columns = [lax.rem(part + step, 4) for step in range(1, 4)]
    spots = [place] + [near[step][0] // 2 for step in range(1, 4)]
    order = (3, 1, 2, 0)
    sets = (
        (large_ref, own_a, chip_a, sum_a, near_a, col_a, part_a),
        (small_ref, own_b, chip_b, sum_b, near_b, col_b, part_b),
    )
    loads = {}
    for step in order:
        for which, (src, own, *_) in enumerate(sets):
            loads[which, step] = pltpu.make_async_copy(
                src.at[spots[step], core], own.at[step], local_sem.at[which, step]
            )
            loads[which, step].start()
    greet([(dp, other) for other in columns] + near[1:] + [partner])
    chips, nears, cols = {}, {}, {}
    for step in order:
        for which, (src, own, chip, *_) in enumerate(sets):
            chips[which, step] = push(
                src.at[spots[step], 1 - core], chip.at[step],
                chip_send.at[which, step], chip_recv.at[which, step], partner,
            )
            chips[which, step].start()
    for step in order:
        for which, (src, own, chip, total, arrived, *_) in enumerate(sets):
            loads[which, step].wait()
            chips[which, step].wait()
            total[step] = (own[step].astype(f32) + chip[step].astype(f32)).astype(total.dtype)
            if step:
                nears[which, step] = push(
                    total.at[step], arrived.at[step - 1],
                    near_send.at[which, step - 1], near_recv.at[which, step - 1], near[step],
                )
                nears[which, step].start()
    for which, (src, own, chip, total, arrived, column, partial_sum) in enumerate(sets):
        for step in order[:3]:
            nears[which, step].wait()
        partial_sum[...] = (
            total[0].astype(f32)
            + arrived[0].astype(f32)
            + arrived[1].astype(f32)
            + arrived[2].astype(f32)
        ).astype(partial_sum.dtype)
        for step, other in enumerate(columns):
            cols[which, step] = push(
                partial_sum.at[other], column.at[step],
                col_send.at[which, step], col_recv.at[which, step], (dp, other),
            )
            cols[which, step].start()
    for which, out in enumerate((large_out, small_out)):
        _, _, _, _, _, column, partial_sum = sets[which]
        for step in range(3):
            cols[which, step].wait()
        out[...] = (
            partial_sum[part].astype(f32)
            + column[0].astype(f32)
            + column[1].astype(f32)
            + column[2].astype(f32)
        )


def gather_sums(large, small):
    blocks = (large.shape[2:], small.shape[2:])
    kinds = (large.dtype, small.dtype)
    two = lambda lead: [pltpu.VMEM(lead(block), kind) for block, kind in zip(blocks, kinds)]
    vmem_spec = pl.BlockSpec(memory_space=pltpu.VMEM)
    return pl.pallas_call(
        gather_sums_kernel,
        out_shape=tuple(jax.ShapeDtypeStruct(block[1:], f32) for block in blocks),
        in_specs=[ANY_SPEC, ANY_SPEC],
        out_specs=(vmem_spec, vmem_spec),
        scratch_shapes=two(lambda block: (4,) + block)
        + two(lambda block: (4,) + block)
        + two(lambda block: (4,) + block)
        + two(lambda block: (3,) + block)
        + two(lambda block: (3,) + block[1:])
        + two(lambda block: block)
        + [DMA((2, 4)), DMA((2, 4)), DMA((2, 4)), DMA((2, 3)), DMA((2, 3)), DMA((2, 3)), DMA((2, 3))],
        compiler_params=comm_params(2),
        name="gather_sums",
    )(large, small)


def standard(rows):
    centred = rows - jnp.mean(rows, axis=-1, keepdims=True)
    inv_std = lax.rsqrt(jnp.mean(centred * centred, axis=-1, keepdims=True) + eps_norm)
    return centred * inv_std, inv_std


def lane_put(table, lane, column):
    lanes = lax.broadcasted_iota(jnp.int32, table.shape, 1)
    return jnp.where(lanes == lane, column, table)


def masked_scores(query, key):
    scores = nt(query, key) * (HD ** (-0.5))
    slots = lax.broadcasted_iota(jnp.int32, scores.shape, 1)
    return jnp.where(slots < LEN, scores, far_negative)


WEIGHT_SPEC = pl.BlockSpec((8, 1, D // 8, D), lambda turn: (0, turn, 0, 0))


def attend_kernel(
    hidden_ref, weight_ref, vec_ref, router_ref,
    resid_ref, second_ref, saved_ref, table_ref, logs_ref, first_sc, attn_sc,
):
    turn = pl.program_id(0)
    images = hidden_ref.shape[0] // SEQ
    weight = weight_ref[:, 0].reshape(D, D)

    @pl.when(turn == 0)
    def _():
        normed, _ = standard(hidden_ref[...].astype(f32))
        first_sc[...] = (normed * vec_ref[0:1] + vec_ref[1:2]).astype(bf16)
        attn_sc[...] = jnp.zeros_like(attn_sc)

    for image in range(images):
        rows = pl.ds(image * SEQ, SEQ)
        mixed = nn(first_sc[rows, :], weight[:, :QKV]).astype(bf16)
        logs = jnp.zeros((SEQ, 128), f32)
        contexts = []
        for head in range(HEADS_PART):
            query, key, value = [
                mixed[:, (kind * HEADS_PART + head) * HD : (kind * HEADS_PART + head + 1) * HD]
                for kind in range(3)
            ]
            scores = masked_scores(query, key)
            top = jnp.max(scores, axis=-1, keepdims=True)
            grown = jnp.exp(scores - top)
            total = jnp.sum(grown, axis=-1, keepdims=True)
            weights = (grown / total).astype(bf16)
            contexts.append(nn(weights, value).astype(bf16))
            logs = lane_put(logs, head, top + jnp.log(total))
        context = jnp.concatenate(contexts, axis=1)
        saved_ref[0, rows, :] = jnp.concatenate([mixed, context], axis=1)
        logs_ref[0, rows, :] = logs
        attn_sc[rows, :] += nt(context, weight[:, QKV:])

    @pl.when(turn == pl.num_programs(0) - 1)
    def _():
        attn = attn_sc[...]
        resid = hidden_ref[...].astype(f32) + attn
        resid_ref[...] = resid
        normed, _ = standard(resid)
        second = (normed * vec_ref[2:3] + vec_ref[3:4]).astype(bf16)
        second_ref[...] = second
        logits = nn(second, router_ref[...])
        lanes = lax.broadcasted_iota(jnp.int32, logits.shape, 1)
        logits = jnp.where(lanes < EXPERTS, logits, far_negative)
        grown = jnp.exp(logits - jnp.max(logits, axis=-1, keepdims=True))
        probs = grown / jnp.sum(grown, axis=-1, keepdims=True)
        table_ref[...] = lane_put(probs, EXPERTS, jnp.sum(attn * attn, axis=-1, keepdims=True))


def attend_rows(hidden, weights, vecs, router):
    rows = hidden.shape[0]
    whole = lambda shape: pl.BlockSpec(shape, lambda turn: (0,) * len(shape))
    by_part = lambda shape: pl.BlockSpec((1,) + shape, lambda turn: (turn, 0, 0))
    return pl.pallas_call(
        attend_kernel,
        grid=(4,),
        in_specs=[whole((rows, D)), WEIGHT_SPEC, whole((8, D)), whole((D, 128))],
        out_specs=(
            whole((rows, D)), whole((rows, D)), by_part((rows, D)), whole((rows, 128)), by_part((rows, 128)),
        ),
        out_shape=(
            jax.ShapeDtypeStruct((rows, D), f32),
            jax.ShapeDtypeStruct((rows, D), bf16),
            jax.ShapeDtypeStruct((4, rows, D), bf16),
            jax.ShapeDtypeStruct((rows, 128), f32),
            jax.ShapeDtypeStruct((4, rows, 128), f32),
        ),
        scratch_shapes=[pltpu.VMEM((rows, D), bf16), pltpu.VMEM((rows, D), f32)],
        compiler_params=pltpu.CompilerParams(vmem_limit_bytes=VMEM_LIMIT),
        name="attend_rows",
    )(hidden, weights, vecs, router)


def norm_pull(grad, normed, inv_std, gain):
    scaled = grad * gain
    one = jnp.mean(scaled, axis=-1, keepdims=True)
    two = jnp.mean(scaled * normed, axis=-1, keepdims=True)
    return inv_std * (scaled - one - normed * two)


def attend_pull_kernel(
    grad_ref, moved_ref, hidden_ref, resid_ref, saved_ref, table_ref, logs_ref, dprob_ref,
    weight_ref, vec_ref, router_ref,
    out_ref, wgrad_ref, small_ref, rgrad_ref,
    first_sc, grad_sc, low_sc, back_sc,
):
    turn = pl.program_id(0)
    rows_all = grad_ref.shape[0]
    images = rows_all // SEQ
    weight = weight_ref[:, 0].reshape(D, D)
    scale = HD ** (-0.5)

    @pl.when(turn == 0)
    def _():
        normed, inv_std = standard(resid_ref[...])
        second = (normed * vec_ref[2:3] + vec_ref[3:4]).astype(bf16)
        lanes = lax.broadcasted_iota(jnp.int32, (rows_all, 128), 1)
        probs = jnp.where(lanes < EXPERTS, table_ref[...], 0.0)
        dprobs = dprob_ref[...]
        dlogit = probs * (dprobs - jnp.sum(probs * dprobs, axis=-1, keepdims=True))
        high = dlogit.astype(bf16)
        low = (dlogit - high.astype(f32)).astype(bf16)
        rgrad_ref[...] = tn(second, high) + tn(second, low)
        dsecond = nt(high, router_ref[...]) + nt(low, router_ref[...])
        for expert in range(EXPERTS):
            dsecond = dsecond + moved_ref[expert].astype(f32)
        small_ref[2:3] = jnp.sum(dsecond * normed, axis=0, keepdims=True)
        small_ref[3:4] = jnp.sum(dsecond, axis=0, keepdims=True)
        grad = grad_ref[...] + norm_pull(dsecond, normed, inv_std, vec_ref[2:3])
        grad_sc[...] = grad
        low_sc[...] = grad.astype(bf16)
        normed, _ = standard(hidden_ref[...].astype(f32))
        first_sc[...] = (normed * vec_ref[0:1] + vec_ref[1:2]).astype(bf16)
        back_sc[...] = jnp.zeros_like(back_sc)

    mixed_grads = []
    for image in range(images):
        rows = pl.ds(image * SEQ, SEQ)
        saved = saved_ref[0, rows, :]
        dcontext = nn(low_sc[rows, :], weight[:, QKV:]).astype(bf16)
        pieces = [[], [], []]
        for head in range(HEADS_PART):
            query, key, value = [
                saved[:, (kind * HEADS_PART + head) * HD : (kind * HEADS_PART + head + 1) * HD]
                for kind in range(3)
            ]
            dhead = dcontext[:, head * HD : (head + 1) * HD]
            weights = jnp.exp(masked_scores(query, key) - logs_ref[0, rows, head : head + 1])
            dvalue = tn(weights.astype(bf16), dhead)
            dweights = nt(dhead, value)
            inner = jnp.sum(weights * dweights, axis=-1, keepdims=True)
            dscores = (weights * (dweights - inner)).astype(bf16)
            pieces[0].append((nn(dscores, key) * scale).astype(bf16))
            pieces[1].append((tn(dscores, query) * scale).astype(bf16))
            pieces[2].append(dvalue.astype(bf16))
        mixed = jnp.concatenate(pieces[0] + pieces[1] + pieces[2], axis=1)
        back_sc[rows, :] += nt(mixed, weight[:, :QKV])
        mixed_grads.append(mixed)
    mixed = jnp.concatenate(mixed_grads, axis=0)
    wgrad = jnp.concatenate([tn(first_sc[...], mixed), tn(low_sc[...], saved_ref[0, :, QKV:])], axis=1)
    wgrad_ref[:, 0] = wgrad.astype(bf16).reshape(8, D // 8, D)

    @pl.when(turn == pl.num_programs(0) - 1)
    def _():
        dfirst = back_sc[...]
        normed, inv_std = standard(hidden_ref[...].astype(f32))
        small_ref[0:1] = jnp.sum(dfirst * normed, axis=0, keepdims=True)
        small_ref[1:2] = jnp.sum(dfirst, axis=0, keepdims=True)
        small_ref[4:8] = jnp.zeros((4, D), f32)
        out_ref[...] = grad_sc[...] + norm_pull(dfirst, normed, inv_std, vec_ref[0:1])


def attend_pull(grad, moved, hidden, resid, saved, table, logs, dprob, weights, vecs, router):
    rows = grad.shape[0]
    whole = lambda shape: pl.BlockSpec(shape, lambda turn: (0,) * len(shape))
    by_part = lambda shape: pl.BlockSpec((1,) + shape, lambda turn: (turn, 0, 0))
    return pl.pallas_call(
        attend_pull_kernel,
        grid=(4,),
        in_specs=[
            whole((rows, D)), whole((EXPERTS, rows, D)), whole((rows, D)), whole((rows, D)),
            by_part((rows, D)), whole((rows, 128)), by_part((rows, 128)), whole((rows, 128)),
            WEIGHT_SPEC, whole((8, D)), whole((D, 128)),
        ],
        out_specs=(whole((rows, D)), WEIGHT_SPEC, whole((8, D)), whole((D, 128))),
        out_shape=(
            jax.ShapeDtypeStruct((rows, D), f32),
            jax.ShapeDtypeStruct((8, 4, D // 8, D), bf16),
            jax.ShapeDtypeStruct((8, D), f32),
            jax.ShapeDtypeStruct((D, 128), f32),
        ),
        scratch_shapes=[
            pltpu.VMEM((rows, D), bf16), pltpu.VMEM((rows, D), f32),
            pltpu.VMEM((rows, D), bf16), pltpu.VMEM((rows, D), f32),
        ],
        compiler_params=pltpu.CompilerParams(vmem_limit_bytes=VMEM_LIMIT),
        name="attend_pull",
    )(grad, moved, hidden, resid, saved, table, logs, dprob, weights, vecs, router)


GELU_C = math.sqrt(2.0 / math.pi)
GELU_K = 0.044715


def gelu_pair(pre):
    square = pre * pre
    bent = jnp.tanh(GELU_C * pre * (1.0 + GELU_K * square))
    half = 0.5 * (1.0 + bent)
    slope = half + (0.5 * GELU_C) * pre * (1.0 - bent * bent) * (1.0 + (3.0 * GELU_K) * square)
    return pre * half, slope


TILE = 256


def weight_of(held, which, turn):
    return held[which, pl.ds(turn * 4, 4)].reshape(D, D)


def expert_kernel(
    second_ref, pieces_ref, rows_out, back_out, weights_out, act_out, slope_out,
    held, weights, made, acts, slopes, total,
    load_sem, join_send, join_recv, row_send, row_recv, pass_send, pass_recv, back_send, back_recv, out_sem, save_sem,
):
    _, core, _, near, partner = relatives()
    count = second_ref.shape[0]
    half = count // 2
    load = pltpu.make_async_copy(second_ref, held.at[0], load_sem.at[2])
    load.start()
    joins = []
    for which in range(2):
        src, dst = pieces_ref.at[:, which], weights.at[which, :, core]
        joins.append(pltpu.make_async_copy(src, dst, load_sem.at[which]))
        joins[-1].start()
    greet(near[1:] + [partner])
    for which in range(2):
        src, dst = pieces_ref.at[:, which], weights.at[which, :, core]
        joins.append(push(src, dst, join_send.at[which], join_recv.at[which], partner))
        joins[-1].start()
    rows = [
        push(second_ref, held.at[step], row_send.at[step - 1], row_recv.at[step - 1], near[step])
        for step in (1, 2)
    ]
    for copy in rows:
        copy.start()
    low, high = pl.ds(0, half), pl.ds(half, half)
    passed = [
        push(held.at[1, low], held.at[3, low], pass_send.at[0], pass_recv.at[0], near[2]),
        push(held.at[2, high], held.at[3, high], pass_send.at[1], pass_recv.at[1], near[1]),
    ]
    backs = [pltpu.make_async_copy(made.at[0], back_out.at[0], save_sem.at[2])] + [
        push(made.at[step], back_out.at[step], back_send.at[step - 1], back_recv.at[step - 1], near[step])
        for step in (1, 2, 3)
    ]
    save_rows = pltpu.make_async_copy(held, rows_out, save_sem.at[0])
    save_weights = pltpu.make_async_copy(weights, weights_out, save_sem.at[1])
    load.wait()
    for copy in joins:
        copy.wait()
    save_weights.start()

    def outs(slot, step, turn):
        place = pl.ds(pl.multiple_of(step * count, count), count)
        return (
            pltpu.make_async_copy(acts.at[slot], act_out.at[turn, place], out_sem.at[0, slot]),
            pltpu.make_async_copy(slopes.at[slot], slope_out.at[turn, place], out_sem.at[1, slot]),
        )

    def chunk(step, carry):
        @pl.when(step == 1)
        def _():
            for copy in rows:
                copy.wait()
            for copy in passed:
                copy.start()

        @pl.when(step == 3)
        def _():
            for copy in passed:
                copy.wait()
            save_rows.start()

        def part(turn, carry):
            slot = lax.rem(turn, 2)

            @pl.when(step * 4 + turn >= 2)
            def _():
                for copy in outs(slot, step, turn):
                    copy.wait()

            for at in range(0, count, TILE):
                tile = pl.ds(at, TILE)
                act, slope = gelu_pair(nn(held[step, tile, :], weight_of(weights, 0, turn)))
                act = act.astype(bf16)
                acts[slot, tile, :] = act
                slopes[slot, tile, :] = slope.astype(bf16)
                product = nt(act, weight_of(weights, 1, turn))
                total[tile, :] = jnp.where(turn == 0, product, total[tile, :] + product)
            for copy in outs(slot, step, turn):
                copy.start()
            return carry

        lax.fori_loop(0, 4, part, 0)
        made[step] = total[...].astype(bf16)
        for at in range(4):

            @pl.when(step == at)
            def _():
                backs[at].start()

        return carry

    lax.fori_loop(0, 4, chunk, 0)
    for slot in range(2):
        for copy in outs(slot, 3, 2 + slot):
            copy.wait()
    save_rows.wait()
    save_weights.wait()
    for copy in backs:
        copy.wait()


def expert_rows(second, pieces):
    count = second.shape[0]
    block = (count, D)
    weight_shape = (2, 16, 2, D // 8, D)
    return pl.pallas_call(
        expert_kernel,
        in_specs=[ANY_SPEC, ANY_SPEC],
        out_specs=(ANY_SPEC,) * 5,
        out_shape=(
            jax.ShapeDtypeStruct((4,) + block, bf16),
            jax.ShapeDtypeStruct((4,) + block, bf16),
            jax.ShapeDtypeStruct(weight_shape, bf16),
            jax.ShapeDtypeStruct((4, 4 * count, D), bf16),
            jax.ShapeDtypeStruct((4, 4 * count, D), bf16),
        ),
        scratch_shapes=[
            pltpu.VMEM((4,) + block, bf16),
            pltpu.VMEM(weight_shape, bf16),
            pltpu.VMEM((4,) + block, bf16),
            pltpu.VMEM((2,) + block, bf16),
            pltpu.VMEM((2,) + block, bf16),
            pltpu.VMEM(block, f32),
            DMA((3,)), DMA((2,)), DMA((2,)), DMA((2,)), DMA((2,)), DMA((2,)), DMA((2,)),
            DMA((3,)), DMA((3,)), DMA((2, 2)), DMA((3,)),
        ],
        compiler_params=comm_params(4),
        name="expert_rows",
    )(second, pieces)


def expert_pull_kernel(
    sent_ref, rows_ref, act_ref, slope_ref, weights_ref, moved_out, wgrad_out,
    grads, rows, weights, pres, made, slopes, acts, total, halves, arrived,
    load_sem, row_send, row_recv, back_send, back_recv, slope_sem, act_sem, chip_send, chip_recv, save_sem,
):
    _, core, _, near, partner = relatives()
    count = sent_ref.shape[1]
    own = pltpu.make_async_copy(sent_ref.at[0], grads.at[0], load_sem.at[0])
    load_weights = pltpu.make_async_copy(weights_ref, weights, load_sem.at[1])
    load_rows = pltpu.make_async_copy(rows_ref, rows, load_sem.at[2])

    def slope_load(step, turn, slot):
        place = pl.ds(pl.multiple_of(step * count, count), count)
        return pltpu.make_async_copy(slope_ref.at[turn, place], slopes.at[slot], slope_sem.at[slot])

    def act_load(turn, slot):
        return pltpu.make_async_copy(act_ref.at[turn], acts.at[slot], act_sem.at[slot])

    own.start()
    load_weights.start()
    for slot in range(2):
        slope_load(0, slot, slot).start()
    load_rows.start()
    for slot in range(2):
        act_load(slot, slot).start()
    greet(near[1:] + [partner])
    sends = [None] + [
        push(sent_ref.at[step], grads.at[step], row_send.at[step - 1], row_recv.at[step - 1], near[step])
        for step in (1, 2, 3)
    ]
    sends[1].start()
    sends[2].start()
    backs = [pltpu.make_async_copy(made.at[0], moved_out.at[0], load_sem.at[3])] + [
        push(made.at[step], moved_out.at[step], back_send.at[step - 1], back_recv.at[step - 1], near[step])
        for step in (1, 2, 3)
    ]
    own.wait()
    load_weights.wait()

    def chunk(step, carry):
        @pl.when(step == 1)
        def _():
            sends[3].start()

        for at in (1, 2, 3):

            @pl.when(step == at)
            def _():
                sends[at].wait()

        def part(turn, carry):
            slot = lax.rem(turn, 2)
            slope_load(step, turn, slot).wait()
            for at in range(0, count, TILE):
                tile = pl.ds(at, TILE)
                dact = nn(grads[step, tile, :], weight_of(weights, 1, turn))
                dpre = (slopes[slot, tile, :].astype(f32) * dact).astype(bf16)
                pres[turn, step, tile, :] = dpre
                product = nt(dpre, weight_of(weights, 0, turn))
                total[tile, :] = jnp.where(turn == 0, product, total[tile, :] + product)

            @pl.when(step * 4 + turn < 14)
            def _():
                after = step * 4 + turn + 2
                slope_load(after // 4, after % 4, slot).start()

            return carry

        lax.fori_loop(0, 4, part, 0)
        made[step] = total[...].astype(bf16)
        for at in range(4):

            @pl.when(step == at)
            def _():
                backs[at].start()

        return carry

    lax.fori_loop(0, 4, chunk, 0)
    load_rows.wait()

    def chip_copy(which, turn):
        return push(
            halves.at[which, turn, :, 1 - core], arrived.at[which, turn],
            chip_send.at[which, turn], chip_recv.at[which, turn], partner,
        )

    def save(which, turn):
        return pltpu.make_async_copy(arrived.at[which, turn], wgrad_out.at[turn, :, which], save_sem.at[which, turn])

    def finish(turn):
        for which in range(2):
            chip_copy(which, turn).wait()
            arrived[which, turn] = (
                halves[which, turn, :, core].astype(f32) + arrived[which, turn].astype(f32)
            ).astype(bf16)
            save(which, turn).start()

    def wgrad(turn, carry):
        slot = lax.rem(turn, 2)
        flat = (4 * count, D)
        act_load(turn, slot).wait()
        first = tn(rows[...].reshape(flat), pres[turn].reshape(flat))
        halves[0, turn] = first.astype(bf16).reshape(4, 2, D // 8, D)
        chip_copy(0, turn).start()
        second = tn(grads[...].reshape(flat), acts[slot])
        halves[1, turn] = second.astype(bf16).reshape(4, 2, D // 8, D)
        chip_copy(1, turn).start()

        @pl.when(turn < 2)
        def _():
            act_load(turn + 2, slot).start()

        @pl.when(turn > 0)
        def _():
            finish(turn - 1)

        return carry

    lax.fori_loop(0, 4, wgrad, 0)
    finish(3)
    for turn in range(4):
        for which in range(2):
            save(which, turn).wait()
    for copy in backs:
        copy.wait()


def expert_pull(sent, rows, act, slope, weights):
    count = sent.shape[1]
    block = (count, D)
    slices = D // 8
    return pl.pallas_call(
        expert_pull_kernel,
        in_specs=[ANY_SPEC] * 5,
        out_specs=(ANY_SPEC, ANY_SPEC),
        out_shape=(
            jax.ShapeDtypeStruct((4,) + block, bf16),
            jax.ShapeDtypeStruct((4, 4, 2, slices, D), bf16),
        ),
        scratch_shapes=[
            pltpu.VMEM((4,) + block, bf16),
            pltpu.VMEM((4,) + block, bf16),
            pltpu.VMEM(weights.shape, bf16),
            pltpu.VMEM((4, 4) + block, bf16),
            pltpu.VMEM((4,) + block, bf16),
            pltpu.VMEM((2,) + block, bf16),
            pltpu.VMEM((2, 4 * count, D), bf16),
            pltpu.VMEM(block, f32),
            pltpu.VMEM((2, 4, 4, 2, slices, D), bf16),
            pltpu.VMEM((2, 4, 4, slices, D), bf16),
            DMA((4,)), DMA((3,)), DMA((3,)), DMA((3,)), DMA((3,)), DMA((2,)), DMA((2,)),
            DMA((2, 4)), DMA((2, 4)), DMA((2, 4)),
        ],
        compiler_params=comm_params(5),
        name="expert_pull",
    )(sent, rows, act, slope, weights)


def per_device(
    tokens, counts, routes, norm_gain, norm_bias, w_router, w_qkv, w_out, w_in, w_back, cotangent
):
    dp, part = lax.axis_index("dp"), lax.axis_index("tensor")
    place = dp // 2
    own_rows = tokens.shape[0]
    slices = D // 8
    row_ids = part * own_rows + jnp.arange(own_rows, dtype=jnp.int32)
    image_count = lax.dynamic_index_in_dim(counts, dp, keepdims=False)
    valid = ((row_ids // SEQ < image_count) & (row_ids % SEQ < LEN)).astype(f32)[:, None]
    my_routes = lax.dynamic_slice_in_dim(routes, part * own_rows, own_rows, axis=1)
    row, col = place // 2, place % 2
    served = jnp.stack([place, row * 2 + 1 - col, (1 - row) * 2 + col, (1 - row) * 2 + 1 - col])
    expert_of = served[:, None] == jnp.arange(EXPERTS)[None, :]
    chosen = (my_routes[:, :, :, None] == served).any(axis=2)

    def by_place(table):
        return jnp.sum(jnp.where(expert_of[None], table[:, None, :], 0.0), axis=-1)

    attn_blocks = jnp.concatenate(
        [
            jnp.transpose(w_qkv, (0, 2, 1, 3)).reshape(LAYERS, slices, QKV),
            jnp.transpose(w_out, (0, 2, 1)),
        ],
        axis=2,
    )
    small = jnp.concatenate([norm_gain, norm_bias, w_router])
    small = jnp.pad(small, (0, 2048 - small.shape[0])).reshape(16, 128)

    def expert_pieces(layer, after):
        packed = jnp.stack([w_in[layer], w_back[layer]], axis=1)
        packed, _ = lax.optimization_barrier((packed, after))
        arrived = swap(packed, "plane", False, 3)
        return lax.all_gather(arrived, "tensor", axis=0, tiled=True)

    pieces = [expert_pieces(0, small), None]
    attn_first, small_all = spread(attn_blocks[0], small)
    attn_later = [
        lax.all_gather(attn_blocks[layer], ("dp", "tensor"), axis=0, tiled=False) for layer in range(1, LAYERS)
    ]
    attn_all = [attn_first] + [each.reshape(8, 4, slices, D) for each in attn_later]
    flat = small_all.reshape(32, 2048)
    vec_count = LAYERS * 2 * D // 32
    gains = flat[:, :vec_count].reshape(LAYERS, 2, D).astype(f32)
    biases = flat[:, vec_count : 2 * vec_count].reshape(LAYERS, 2, D).astype(f32)
    routers = flat[:, 2 * vec_count : 2 * vec_count + LAYERS * D * EXPERTS // 32]
    routers = jnp.pad(routers.reshape(LAYERS, D, EXPERTS), ((0, 0), (0, 0), (0, 128 - EXPERTS)))
    vecs = jnp.pad(
        jnp.stack([gains[:, 0], biases[:, 0], gains[:, 1], biases[:, 1]], axis=1), ((0, 0), (0, 4), (0, 0))
    )

    hidden = tokens
    kept = []
    stats = []
    for layer in range(LAYERS):
        resid, second, saved, table, logs = attend_rows(hidden, attn_all[layer], vecs[layer], routers[layer])
        if layer + 1 < LAYERS:
            pieces[layer + 1] = expert_pieces(layer + 1, second[:8, :128])
        rows, back, weights, act, slope = expert_rows(second, pieces[layer])
        gates = jnp.where(chosen[layer], by_place(table[:, :EXPERTS]), 0.0)
        moe = sum(gates[:, at : at + 1] * back[at].astype(f32) for at in range(EXPERTS))
        result = resid + moe
        stats.append(
            jnp.stack(
                [
                    jnp.sum(valid * result * result),
                    jnp.sum(valid[:, 0] * table[:, EXPERTS]),
                    jnp.sum(valid * moe * moe),
                ]
            )
        )
        kept.append((hidden, resid, saved, table, logs, rows, weights, act, slope, back, gates))
        hidden = result

    grad = cotangent.astype(f32) * valid
    attn_grads, owned, small_grads, router_grads = [], [], [], []
    for layer in reversed(range(LAYERS)):
        before, resid, saved, table, logs, rows, weights, act, slope, back, gates = kept[layer]
        low = grad.astype(bf16)
        dgate = [jnp.sum(back[at].astype(f32) * low.astype(f32), axis=-1) for at in range(EXPERTS)]
        dprob = by_place(jnp.where(chosen[layer], jnp.stack(dgate, axis=1), 0.0))
        dprob = jnp.pad(dprob, ((0, 0), (0, 128 - EXPERTS)))
        sent = jnp.stack([(gates[:, at : at + 1] * low.astype(f32)).astype(bf16) for at in range(EXPERTS)])
        moved, wgrad = expert_pull(sent, rows, act, slope, weights)
        summed = lax.psum_scatter(wgrad, "tensor", scatter_dimension=0, tiled=False)
        owned.append(summed)
        grad, attn_wgrad, small_grad, router_grad = attend_pull(
            grad, moved, before, resid, saved, table, logs, dprob, attn_all[layer], vecs[layer], routers[layer]
        )
        if layer:
            attn_wgrad = lax.psum_scatter(
                attn_wgrad.reshape(32, slices, D), ("dp", "tensor"), scatter_dimension=0, tiled=False
            ).astype(f32)
        attn_grads.append(attn_wgrad)
        small_grads.append(small_grad[:4])
        router_grads.append(router_grad[:, :EXPERTS])
    for listed in (small_grads, router_grads, owned):
        listed.reverse()

    vec_grads = jnp.stack(small_grads).reshape(LAYERS, 2, 2, D)
    packed = jnp.concatenate(
        [
            vec_grads[:, :, 0].reshape(32, -1),
            vec_grads[:, :, 1].reshape(32, -1),
            jnp.stack(router_grads).reshape(32, -1),
            jnp.broadcast_to(jnp.stack(stats).reshape(1, -1), (32, 3 * LAYERS)),
        ],
        axis=1,
    )
    packed = jnp.pad(packed, ((0, 0), (0, 1024 - packed.shape[1]))).reshape(4, 2, 4, 8, 128)
    last, total = gather_sums(attn_grads.pop().reshape(4, 2, 4, slices, D), packed)
    attn_grad = jnp.stack([last] + attn_grads)
    total = total.reshape(-1)
    share = LAYERS * 2 * D // 32
    router_share = LAYERS * D * EXPERTS // 32
    at = 2 * share + router_share
    denom = jnp.sum(counts).astype(f32) * (LEN * D)
    rms = jnp.sqrt(total[at : at + 3 * LAYERS].reshape(LAYERS, 3) / denom)
    qkv_grad = jnp.transpose(attn_grad[:, :, :QKV].reshape(LAYERS, slices, 3, QKV // 3), (0, 2, 1, 3))
    out_grad = jnp.transpose(attn_grad[:, :, QKV:], (0, 2, 1))
    expert_grad = swap(jnp.stack(owned, axis=1), "plane", False, 6).astype(f32)
    expert_grad = jnp.transpose(expert_grad, (2, 1, 0, 3, 4))
    return (
        hidden,
        grad,
        total[:share],
        total[share : 2 * share],
        total[2 * share : at],
        qkv_grad,
        out_grad,
        expert_grad[0],
        expert_grad[1],
        rms,
    )


def solution(mesh):
    return jax.shard_map(
        per_device if mesh.shape["dp"] == 8 else per_device_general,
        mesh=mesh,
        in_specs=(
            P(("dp", "tensor"), None),
            P(),
            P(None, "dp", None),
            P(("dp", "tensor")),
            P(("dp", "tensor")),
            P(("dp", "tensor")),
            P(None, None, "dp", "tensor"),
            P(None, "tensor", "dp"),
            P(None, None, "dp", "tensor"),
            P(None, None, "dp", "tensor"),
            P(("dp", "tensor"), None),
        ),
        out_specs=(
            P(("dp", "tensor"), None),
            P(("dp", "tensor"), None),
            P(("dp", "tensor")),
            P(("dp", "tensor")),
            P(("dp", "tensor")),
            P(None, None, "dp", "tensor"),
            P(None, "tensor", "dp"),
            P(None, None, "dp", "tensor"),
            P(None, None, "dp", "tensor"),
            P(),
        ),
        check_vma=False,
    )
```

```python
from functools import partial
import math

import jax
import jax.numpy as jnp
from jax import lax
from jax.experimental import pallas as pl
from jax.experimental.pallas import tpu as pltpu
from jax.sharding import PartitionSpec as P

D = 768
HD = 64
LEN = 197
SEQ = 256
LAYERS = 2


eps_norm = 1e-06
far_negative = -1e30
highest = lax.Precision.HIGHEST


def norm_forward(row_vals, gain_vec, bias_vec):
    row_mean = jnp.mean(row_vals, axis=-1, keepdims=True)
    centred = row_vals - row_mean
    row_var = jnp.mean(centred * centred, axis=-1, keepdims=True)
    inv_std = lax.rsqrt(row_var + eps_norm)
    normed = centred * inv_std
    return (normed * gain_vec + bias_vec, normed, inv_std)


def norm_backward(grad_vals, normed, inv_std, gain_vec):
    gain_grad = jnp.sum(grad_vals * normed, axis=0)
    bias_grad = jnp.sum(grad_vals, axis=0)
    scaled = grad_vals * gain_vec
    mean_one = jnp.mean(scaled, axis=-1, keepdims=True)
    mean_two = jnp.mean(scaled * normed, axis=-1, keepdims=True)
    return (inv_std * (scaled - mean_one - normed * mean_two), gain_grad, bias_grad)


def gather_rows(row_vals):
    return lax.all_gather(row_vals, "tensor", axis=0, tiled=True)


def sum_rows(row_vals):
    return lax.psum_scatter(
        row_vals.astype(jnp.bfloat16), "tensor", scatter_dimension=0, tiled=True
    ).astype(jnp.float32)


def sum_slots(slot_vals):
    return lax.psum_scatter(
        slot_vals.astype(jnp.bfloat16), "tensor", scatter_dimension=1, tiled=True
    ).astype(jnp.float32)


def to_experts(make_rows, positions):
    return lax.all_to_all(make_rows(positions), "dp", split_axis=0, concat_axis=0, tiled=True)


def attend(block_in, key_keep, score_scale):
    query_heads, key_heads, value_heads = block_in
    scores = (
        jnp.einsum("iqhd,ikhd->ihqk", query_heads, key_heads, preferred_element_type=jnp.float32)
        * score_scale
    )
    scores = jnp.where(key_keep, scores, far_negative)
    row_max = jnp.max(scores, axis=-1, keepdims=True)
    exponent = jnp.exp(scores - row_max)
    row_total = jnp.sum(exponent, axis=-1, keepdims=True)
    weights = (exponent / row_total).astype(jnp.bfloat16)
    context = jnp.einsum(
        "ihqk,ikhd->iqhd", weights, value_heads, preferred_element_type=jnp.float32
    )
    return (context.astype(jnp.bfloat16), (row_max + jnp.log(row_total))[..., 0])


def attend_back(block_in, key_keep, score_scale):
    query_heads, key_heads, value_heads, d_context, log_total = block_in
    scores = (
        jnp.einsum("iqhd,ikhd->ihqk", query_heads, key_heads, preferred_element_type=jnp.float32)
        * score_scale
    )
    scores = jnp.where(key_keep, scores, far_negative)
    weights = jnp.exp(scores - log_total[..., None])
    d_values = jnp.einsum(
        "ihqk,iqhd->ikhd",
        weights.astype(jnp.bfloat16),
        d_context,
        preferred_element_type=jnp.float32,
    )
    d_weights = jnp.einsum(
        "iqhd,ikhd->ihqk", d_context, value_heads, preferred_element_type=jnp.float32
    )
    inner_sum = jnp.sum(weights * d_weights, axis=-1, keepdims=True)
    d_scores = (weights * (d_weights - inner_sum)).astype(jnp.bfloat16)
    d_queries = (
        jnp.einsum("ihqk,ikhd->iqhd", d_scores, key_heads, preferred_element_type=jnp.float32)
        * score_scale
    )
    d_keys = (
        jnp.einsum("ihqk,iqhd->ikhd", d_scores, query_heads, preferred_element_type=jnp.float32)
        * score_scale
    )
    return (
        d_queries.astype(jnp.bfloat16),
        d_keys.astype(jnp.bfloat16),
        d_values.astype(jnp.bfloat16),
    )


def contract_first(left_mat, right_mat):
    return lax.dot_general(
        left_mat, right_mat, (((0,), (0,)), ((), ())), preferred_element_type=jnp.float32
    )


def contract_last(left_mat, right_mat):
    return lax.dot_general(
        left_mat, right_mat, (((1,), (1,)), ((), ())), preferred_element_type=jnp.float32
    )


def per_device_general(
    tokens, counts, routes, norm_gain, norm_bias, w_router, w_qkv, w_out, w_in, w_back, cotangent
):
    groups = lax.axis_size("dp")
    parts = lax.axis_size("tensor")
    experts = groups // 2
    group_idx = lax.axis_index("dp")
    my_part = lax.axis_index("tensor")
    own_rows = tokens.shape[0]
    rows_all = own_rows * parts
    slot_count = 3 * rows_all // experts
    half_slots = slot_count // 2
    quarter = half_slots // parts
    score_scale = HD ** (-0.5)
    images = rows_all // SEQ
    per_block = math.gcd(images, max(1, 512 // SEQ))
    blocks = images // per_block
    head_cols = w_qkv.shape[-1]
    heads_here = head_cols // HD
    key_keep = jnp.arange(SEQ) < LEN
    gain_flat, bias_flat, router_flat = (
        lax.all_gather(norm_gain, ("dp", "tensor"), axis=0, tiled=True),
        lax.all_gather(norm_bias, ("dp", "tensor"), axis=0, tiled=True),
        lax.all_gather(w_router, ("dp", "tensor"), axis=0, tiled=True),
    )
    gains_all = gain_flat.astype(jnp.float32).reshape(LAYERS, 2, D)
    biases_all = bias_flat.astype(jnp.float32).reshape(LAYERS, 2, D)
    router_all = router_flat.reshape(LAYERS, D, experts)
    row_ids = my_part * own_rows + jnp.arange(own_rows, dtype=jnp.int32)
    image_count = lax.dynamic_index_in_dim(counts, group_idx, keepdims=False)
    valid_rows = ((row_ids // SEQ < image_count) & (row_ids % SEQ < LEN)).astype(jnp.float32)[
        :, None
    ]

    def split_heads(columns):
        return columns.reshape(blocks, per_block, SEQ, heads_here, HD)

    hidden = tokens.astype(jnp.float32)
    kept_layers = []
    stat_terms = []
    for layer_idx in range(LAYERS):
        gain_pair = gains_all[layer_idx]
        shift_pair = biases_all[layer_idx]
        wq_part, wo_part = (
            lax.all_gather(w_qkv[layer_idx], "dp", axis=1, tiled=True),
            lax.all_gather(w_out[layer_idx], "dp", axis=1, tiled=True),
        )
        w_cat = jnp.concatenate([wq_part[0], wq_part[1], wq_part[2]], axis=1)
        up_part, back_part = (
            lax.all_to_all(
                jnp.repeat(w_in[layer_idx], 2, axis=0),
                "dp",
                split_axis=0,
                concat_axis=0,
                tiled=True,
            ),
            lax.all_to_all(
                jnp.repeat(w_back[layer_idx], 2, axis=0),
                "dp",
                split_axis=0,
                concat_axis=0,
                tiled=True,
            ),
        )
        up_part = up_part.reshape(D, -1)
        back_part = back_part.reshape(D, -1)
        up_use, back_use = (up_part, back_part)
        norm_one, normed_one, inv_one = norm_forward(hidden, gain_pair[0], shift_pair[0])
        rows_one = gather_rows(norm_one.astype(jnp.bfloat16))
        qkv_rows = jnp.dot(rows_one, w_cat, preferred_element_type=jnp.float32).astype(jnp.bfloat16)
        query_heads = split_heads(qkv_rows[:, :head_cols])
        key_heads = split_heads(qkv_rows[:, head_cols : 2 * head_cols])
        value_heads = split_heads(qkv_rows[:, 2 * head_cols :])
        context, log_total = lax.map(
            partial(attend, key_keep=key_keep, score_scale=score_scale),
            (query_heads, key_heads, value_heads),
        )
        context = context.reshape(rows_all, head_cols)
        attn_out = sum_rows(jnp.dot(context, wo_part, preferred_element_type=jnp.float32))
        residual = hidden + attn_out
        norm_two, normed_two, inv_two = norm_forward(residual, gain_pair[1], shift_pair[1])
        rows_two = gather_rows(norm_two.astype(jnp.bfloat16))
        router = router_all[layer_idx]
        router_probs = jax.nn.softmax(
            jnp.dot(rows_two, router, preferred_element_type=jnp.float32), axis=-1
        )
        routing = routes[layer_idx]
        one_hot = routing[:, :, None] == jnp.arange(experts)[None, None, :]
        gate_vals = jnp.sum(jnp.where(one_hot, router_probs[:, None, :], 0.0), axis=-1)
        flat_pick = routing.reshape(-1)
        hot_int = (flat_pick[:, None] == jnp.arange(experts)[None, :]).astype(jnp.int32)
        rank_in = jnp.sum((jnp.cumsum(hot_int, axis=0) - hot_int) * hot_int, axis=1)
        target = flat_pick * slot_count + rank_in
        positions = (
            jnp.full((experts * slot_count,), 2 * rows_all, jnp.int32)
            .at[target]
            .set(jnp.arange(2 * rows_all, dtype=jnp.int32))
        )
        positions = positions.reshape(groups, half_slots)
        padded_two = jnp.concatenate([rows_two, jnp.zeros((1, D), jnp.bfloat16)], axis=0)

        def take_rows(slot_index):
            return padded_two[jnp.where(slot_index < 2 * rows_all, slot_index // 2, rows_all)]

        arrived = to_experts(take_rows, positions).reshape(-1, D)
        pre_act = jnp.dot(arrived, up_use, preferred_element_type=jnp.float32)
        activation = jax.nn.gelu(pre_act, approximate=True).astype(jnp.bfloat16)
        partial_out = contract_last(activation, back_use)
        summed = sum_slots(partial_out.reshape(groups, half_slots, D)).astype(jnp.bfloat16)
        returned = lax.all_to_all(summed, "dp", split_axis=0, concat_axis=0, tiled=True)
        slot_pair = target.reshape(rows_all, 2)
        owner = slot_pair // half_slots
        inside = slot_pair % half_slots
        in_quarter = inside // quarter == my_part
        pick_index = jnp.where(
            in_quarter, owner * quarter + inside - my_part * quarter, groups * quarter
        )
        padded_ret = jnp.concatenate(
            [returned.reshape(groups * quarter, D), jnp.zeros((1, D), jnp.bfloat16)], axis=0
        )
        chosen = padded_ret[pick_index]
        expert_out = sum_rows(jnp.sum(gate_vals[:, :, None] * chosen, axis=1))
        result = residual + expert_out
        stat_terms.append(
            jnp.stack(
                [
                    jnp.sum(valid_rows * result * result),
                    jnp.sum(valid_rows * attn_out * attn_out),
                    jnp.sum(valid_rows * expert_out * expert_out),
                ]
            )
        )
        kept_layers.append(
            (
                wo_part,
                w_cat,
                up_use,
                back_use,
                normed_one,
                inv_one,
                rows_one,
                query_heads,
                key_heads,
                value_heads,
                context,
                log_total,
                normed_two,
                inv_two,
                rows_two,
                router,
                router_probs,
                one_hot,
                gate_vals,
                positions,
                arrived,
                pre_act,
                activation,
                pick_index,
                chosen,
            )
        )
        hidden = result
    totals = lax.psum(jnp.stack(stat_terms), ("dp", "tensor"))
    denom = jnp.sum(counts).astype(jnp.float32) * (LEN * D)
    rms = jnp.sqrt(totals / denom)
    grad_rows = cotangent.astype(jnp.float32) * valid_rows
    gain_grads = [None] * LAYERS
    bias_grads = [None] * LAYERS
    router_grads = [None] * LAYERS
    qkv_grads = [None] * LAYERS
    out_grads = [None] * LAYERS
    up_grads = [None] * LAYERS
    back_grads = [None] * LAYERS
    for layer_idx in reversed(range(LAYERS)):
        (
            wo_part,
            w_cat,
            up_use,
            back_use,
            normed_one,
            inv_one,
            rows_one,
            query_heads,
            key_heads,
            value_heads,
            context,
            log_total,
            normed_two,
            inv_two,
            rows_two,
            router,
            router_probs,
            one_hot,
            gate_vals,
            positions,
            arrived,
            pre_act,
            activation,
            pick_index,
            chosen,
        ) = kept_layers[layer_idx]
        gain_pair = gains_all[layer_idx]
        grad_moe = gather_rows(grad_rows.astype(jnp.bfloat16))
        d_gates = jnp.einsum("rkd,rd->rk", chosen, grad_moe, preferred_element_type=jnp.float32)
        padded_down = jnp.concatenate([grad_moe, jnp.zeros((1, D), jnp.bfloat16)], axis=0)
        flat_gates = jnp.concatenate([gate_vals.reshape(-1), jnp.zeros((1,), jnp.float32)], axis=0)

        def scaled_rows(slot_index):
            filled = slot_index < 2 * rows_all
            row_index = jnp.where(filled, slot_index // 2, rows_all)
            gate_index = jnp.where(filled, slot_index, 2 * rows_all)
            return (flat_gates[gate_index][..., None] * padded_down[row_index]).astype(jnp.bfloat16)

        d_expert_rows = to_experts(scaled_rows, positions).reshape(-1, D)
        d_activation = jnp.dot(d_expert_rows, back_use, preferred_element_type=jnp.float32)
        back_grad = contract_first(d_expert_rows, activation)
        d_pre = jax.vjp(partial(jax.nn.gelu, approximate=True), pre_act)[1](d_activation)[0].astype(
            jnp.bfloat16
        )
        up_grad = contract_first(arrived, d_pre)
        d_arrived = contract_last(d_pre, up_use)
        d_slots = sum_slots(d_arrived.reshape(groups, half_slots, D))
        d_back_rows, up_pieces, back_pieces = (
            lax.all_to_all(
                d_slots.astype(jnp.bfloat16), "dp", split_axis=0, concat_axis=0, tiled=True
            ).astype(d_slots.dtype),
            lax.all_to_all(
                up_grad.reshape(groups, -1, up_grad.shape[1]).astype(jnp.bfloat16),
                "dp",
                split_axis=0,
                concat_axis=0,
                tiled=True,
            ).astype(jnp.float32),
            lax.all_to_all(
                back_grad.reshape(groups, -1, back_grad.shape[1]).astype(jnp.bfloat16),
                "dp",
                split_axis=0,
                concat_axis=0,
                tiled=True,
            ).astype(jnp.float32),
        )
        up_grads[layer_idx] = up_pieces.reshape(
            experts, 2, up_pieces.shape[1], up_pieces.shape[2]
        ).sum(axis=1)
        back_grads[layer_idx] = back_pieces.reshape(
            experts, 2, back_pieces.shape[1], back_pieces.shape[2]
        ).sum(axis=1)
        padded_back = jnp.concatenate(
            [d_back_rows.reshape(groups * quarter, D), jnp.zeros((1, D), jnp.float32)], axis=0
        )
        d_rows_two = jnp.sum(padded_back[pick_index], axis=1)
        d_probs = jnp.sum(jnp.where(one_hot, d_gates[:, :, None], 0.0), axis=1)
        d_logits = router_probs * (
            d_probs - jnp.sum(router_probs * d_probs, axis=-1, keepdims=True)
        )
        d_rows_two = d_rows_two + jnp.dot(d_logits, router.astype(jnp.float32).T, precision=highest)
        router_grads[layer_idx] = jnp.dot(
            rows_two.astype(jnp.float32).T, d_logits, precision=highest
        )
        d_second = sum_rows(d_rows_two)
        d_resid, gain_two, bias_two = norm_backward(d_second, normed_two, inv_two, gain_pair[1])
        grad_rows = grad_rows + d_resid
        grad_attn = gather_rows(grad_rows.astype(jnp.bfloat16))
        d_context = contract_last(grad_attn, wo_part).astype(jnp.bfloat16)
        out_grad = contract_first(context, grad_attn)
        d_queries, d_keys, d_values = lax.map(
            partial(attend_back, key_keep=key_keep, score_scale=score_scale),
            (query_heads, key_heads, value_heads, split_heads(d_context), log_total),
        )
        d_mixed = jnp.concatenate(
            [
                d_queries.reshape(rows_all, head_cols),
                d_keys.reshape(rows_all, head_cols),
                d_values.reshape(rows_all, head_cols),
            ],
            axis=1,
        )
        cat_grad = contract_first(rows_one, d_mixed)
        qkv_grad = jnp.stack(
            [
                cat_grad[:, :head_cols],
                cat_grad[:, head_cols : 2 * head_cols],
                cat_grad[:, 2 * head_cols :],
            ]
        )
        qkv_grads[layer_idx], out_grads[layer_idx] = (
            lax.psum_scatter(qkv_grad, "dp", scatter_dimension=1, tiled=True),
            lax.psum_scatter(out_grad, "dp", scatter_dimension=1, tiled=True),
        )
        d_first = sum_rows(contract_last(d_mixed, w_cat))
        d_hidden, gain_one, bias_one = norm_backward(d_first, normed_one, inv_one, gain_pair[0])
        grad_rows = grad_rows + d_hidden
        gain_grads[layer_idx] = jnp.stack([gain_one, gain_two])
        bias_grads[layer_idx] = jnp.stack([bias_one, bias_two])
    grad_gain, grad_bias, grad_router = (
        lax.psum_scatter(
            jnp.stack(gain_grads).reshape(-1), ("dp", "tensor"), scatter_dimension=0, tiled=True
        ),
        lax.psum_scatter(
            jnp.stack(bias_grads).reshape(-1), ("dp", "tensor"), scatter_dimension=0, tiled=True
        ),
        lax.psum_scatter(
            jnp.stack(router_grads).reshape(-1), ("dp", "tensor"), scatter_dimension=0, tiled=True
        ),
    )
    return (
        hidden,
        grad_rows,
        grad_gain,
        grad_bias,
        grad_router,
        jnp.stack(qkv_grads),
        jnp.stack(out_grads),
        jnp.stack(up_grads),
        jnp.stack(back_grads),
        rms,
    )


bf16 = jnp.bfloat16
f32 = jnp.float32
MESH = pl.DeviceIdType.MESH
VMEM_LIMIT = 63 * 1024 * 1024
EXPERTS = 4
HEADS_PART = 3
QKV = 3 * HEADS_PART * HD


def nn(left, right):
    return jnp.dot(left, right, preferred_element_type=f32)


def nt(left, right):
    return lax.dot_general(left, right, (((1,), (1,)), ((), ())), preferred_element_type=f32)


def tn(left, right):
    return lax.dot_general(left, right, (((0,), (0,)), ((), ())), preferred_element_type=f32)


def group_of(kind):
    dp, part = lax.axis_index("dp"), lax.axis_index("tensor")
    if kind == "plane":
        return dp // 2, 4, lambda place: (place * 2 + dp % 2, part)
    if kind == "column":
        return part, 4, lambda place: (dp, place)
    if kind == "chip":
        return dp % 2, 2, lambda place: (dp // 2 * 2 + place, part)
    return dp * 4 + part, 32, lambda place: (place // 4, place % 4)


def greet(devices):
    barrier = pltpu.get_barrier_semaphore()
    for device in devices:
        pl.semaphore_signal(barrier, inc=1, device_id=device, device_id_type=MESH)
    pl.semaphore_wait(barrier, len(devices))


def swap_kernel(kind, same, in_ref, after_ref, out_ref, held, local_sem, send_sem, recv_sem):
    place, count, device = group_of(kind)
    others = [lax.rem(place + step, count) for step in range(1, count)]
    first = pltpu.make_async_copy(in_ref if same else in_ref.at[place], held, local_sem.at[0])
    first.start()
    greet([device(other) for other in others])
    copies = []
    for step, other in enumerate(others):
        copies.append(
            pltpu.make_async_remote_copy(
                src_ref=in_ref if same else in_ref.at[other],
                dst_ref=out_ref.at[place],
                send_sem=send_sem.at[step],
                recv_sem=recv_sem.at[step],
                device_id=device(other),
                device_id_type=MESH,
            )
        )
        copies[-1].start()
    first.wait()
    second = pltpu.make_async_copy(held, out_ref.at[place], local_sem.at[1])
    second.start()
    second.wait()
    for copy in copies:
        copy.wait()


def swap(array, kind, same, collective_id, after):
    count = {"plane": 4, "column": 4, "chip": 2, "all": 32}[kind]
    block = array.shape if same else array.shape[1:]
    any_spec = pl.BlockSpec(memory_space=pl.ANY)
    return pl.pallas_call(
        partial(swap_kernel, kind, same),
        out_shape=jax.ShapeDtypeStruct((count,) + block, array.dtype),
        in_specs=[any_spec, any_spec],
        out_specs=any_spec,
        scratch_shapes=[
            pltpu.VMEM(block, array.dtype),
            pltpu.SemaphoreType.DMA((2,)),
            pltpu.SemaphoreType.DMA((count - 1,)),
            pltpu.SemaphoreType.DMA((count - 1,)),
        ],
        compiler_params=pltpu.CompilerParams(
            collective_id=collective_id, has_side_effects=True, vmem_limit_bytes=VMEM_LIMIT
        ),
        name=f"swap_{kind}_{collective_id}",
    )(array, after)


def relatives():
    dp, part = lax.axis_index("dp"), lax.axis_index("tensor")
    place, core = dp // 2, dp % 2
    row, col = place // 2, place % 2
    near = (row * 2 + 1 - col, (1 - row) * 2 + col, (1 - row) * 2 + 1 - col)
    return place, core, part, [None] + [(at * 2 + core, part) for at in near], (place * 2 + 1 - core, part)


def push(src, dst, send_sem, recv_sem, device):
    return pltpu.make_async_remote_copy(
        src_ref=src, dst_ref=dst, send_sem=send_sem, recv_sem=recv_sem, device_id=device, device_id_type=MESH
    )


def comm_params(collective_id):
    return pltpu.CompilerParams(
        collective_id=collective_id, has_side_effects=True, vmem_limit_bytes=VMEM_LIMIT
    )


ANY_SPEC = pl.BlockSpec(memory_space=pl.ANY)
DMA = pltpu.SemaphoreType.DMA


def spread_kernel(
    block_ref, small_ref, out_ref, small_out, local_sem, za_send, za_recv, yx_send, yx_recv, cc_send, cc_recv
):
    place, core, part, near, partner = relatives()
    dp = place * 2 + core
    columns = [lax.rem(part + step, 4) for step in range(1, 4)]
    pairs = ((block_ref, out_ref), (small_ref, small_out))
    locals_ = [
        pltpu.make_async_copy(src, dst.at[dp, part], local_sem.at[which])
        for which, (src, dst) in enumerate(pairs)
    ]
    for copy in locals_:
        copy.start()
    greet([(dp, other) for other in columns] + near[1:] + [partner])
    first = [
        [
            push(src, dst.at[dp, part], za_send.at[which, step], za_recv.at[which, step], (dp, other))
            for which, (src, dst) in enumerate(pairs)
        ]
        for step, other in enumerate(columns)
    ]
    for listed in first:
        for copy in listed:
            copy.start()
    for copy in locals_:
        copy.wait()
    second = [[], [], [], []]
    third = []

    def start(listed, copy):
        copy.start()
        listed.append(copy)

    for turn in range(4):
        part_at = lax.rem(part + 4 - turn, 4)
        if turn:
            for copy in first[turn - 1]:
                copy.wait()
        for which, (_, dst) in enumerate(pairs):
            spot = dst.at[dp, part_at]
            for step in range(3):
                start(
                    second[turn],
                    push(spot, spot, yx_send.at[turn, which, step], yx_recv.at[turn, which, step], near[step + 1]),
                )
            start(third, push(spot, spot, cc_send.at[turn, which, 0], cc_recv.at[turn, which, 0], partner))
    for turn in range(4):
        part_at = lax.rem(part + 4 - turn, 4)
        for which, (_, dst) in enumerate(pairs):
            for step in range(3):
                second[turn][which * 3 + step].wait()
                spot = dst.at[near[step + 1][0], part_at]
                start(
                    third,
                    push(spot, spot, cc_send.at[turn, which, step + 1], cc_recv.at[turn, which, step + 1], partner),
                )
    for copy in third:
        copy.wait()


def spread(block, small):
    vmem_spec = pl.BlockSpec(memory_space=pltpu.VMEM)
    return pl.pallas_call(
        spread_kernel,
        out_shape=(
            jax.ShapeDtypeStruct((8, 4) + block.shape, block.dtype),
            jax.ShapeDtypeStruct((8, 4) + small.shape, small.dtype),
        ),
        in_specs=[vmem_spec, vmem_spec],
        out_specs=(ANY_SPEC, ANY_SPEC),
        scratch_shapes=[
            DMA((2,)), DMA((2, 3)), DMA((2, 3)), DMA((4, 2, 3)), DMA((4, 2, 3)), DMA((4, 2, 4)), DMA((4, 2, 4)),
        ],
        compiler_params=comm_params(1),
        name="spread",
    )(block, small)


def gather_sums_kernel(count, *refs):
    ins, moved_ref, refs = refs[:count], refs[count], refs[count + 1 :]
    outs, swapped, refs = refs[:count], refs[count], refs[count + 1 :]
    sets = [(ins[which],) + refs[6 * which : 6 * which + 6] for which in range(count)]
    held, *sems = refs[6 * count :]
    local_sem, chip_send, chip_recv, near_send, near_recv, col_send, col_recv, held_sem, swap_send, swap_recv = sems
    place, core, part, near, partner = relatives()
    dp = place * 2 + core
    columns = [lax.rem(part + step, 4) for step in range(1, 4)]
    spots = [place] + [near[step][0] // 2 for step in range(1, 4)]
    order = (3, 1, 2, 0)
    loads = {}
    for which, (src, own, *_) in enumerate(sets):
        for step in order:
            loads[which, step] = pltpu.make_async_copy(
                src.at[spots[step], core], own.at[step], local_sem.at[which, step]
            )
            loads[which, step].start()
    bring = pltpu.make_async_copy(moved_ref.at[place], held, held_sem.at[0])
    bring.start()
    greet([(dp, other) for other in columns] + near[1:] + [partner])
    chips, nears, cols = {}, {}, {}
    for which, (src, own, chip, *_) in enumerate(sets):
        for step in order:
            chips[which, step] = push(
                src.at[spots[step], 1 - core], chip.at[step],
                chip_send.at[which, step], chip_recv.at[which, step], partner,
            )
            chips[which, step].start()
    swaps = [
        push(
            moved_ref.at[spots[step]], swapped.at[place], swap_send.at[step - 1], swap_recv.at[step - 1], near[step]
        )
        for step in (1, 2, 3)
    ]
    for copy in swaps:
        copy.start()
    bring.wait()
    keep = pltpu.make_async_copy(held, swapped.at[place], held_sem.at[1])
    keep.start()
    for which, (src, own, chip, total, arrived, *_) in enumerate(sets):
        for step in order:
            loads[which, step].wait()
            chips[which, step].wait()
            total[step] = (own[step].astype(f32) + chip[step].astype(f32)).astype(total.dtype)
            if step:
                nears[which, step] = push(
                    total.at[step], arrived.at[step - 1],
                    near_send.at[which, step - 1], near_recv.at[which, step - 1], near[step],
                )
                nears[which, step].start()
    for which, (src, own, chip, total, arrived, column, partial_sum) in enumerate(sets):
        for step in order[:3]:
            nears[which, step].wait()
        partial_sum[...] = (
            total[0].astype(f32)
            + arrived[0].astype(f32)
            + arrived[1].astype(f32)
            + arrived[2].astype(f32)
        ).astype(partial_sum.dtype)
        for step, other in enumerate(columns):
            cols[which, step] = push(
                partial_sum.at[other], column.at[step],
                col_send.at[which, step], col_recv.at[which, step], (dp, other),
            )
            cols[which, step].start()
    for which, out in enumerate(outs):
        _, _, _, _, _, column, partial_sum = sets[which]
        for step in range(3):
            cols[which, step].wait()
        out[...] = (
            partial_sum[part].astype(f32)
            + column[0].astype(f32)
            + column[1].astype(f32)
            + column[2].astype(f32)
        )
    keep.wait()
    for copy in swaps:
        copy.wait()


def gather_sums(arrays, moved):
    count = len(arrays)
    scratch = []
    for array in arrays:
        block = array.shape[2:]
        for shape in ((4,) + block, (4,) + block, (4,) + block, (3,) + block, (3,) + block[1:], block):
            scratch.append(pltpu.VMEM(shape, array.dtype))
    vmem_spec = pl.BlockSpec(memory_space=pltpu.VMEM)
    return pl.pallas_call(
        partial(gather_sums_kernel, count),
        out_shape=tuple(jax.ShapeDtypeStruct(array.shape[3:], f32) for array in arrays)
        + (jax.ShapeDtypeStruct(moved.shape, moved.dtype),),
        in_specs=[ANY_SPEC] * (count + 1),
        out_specs=(vmem_spec,) * count + (ANY_SPEC,),
        scratch_shapes=scratch
        + [pltpu.VMEM(moved.shape[1:], moved.dtype)]
        + [DMA((count, 4))] * 3 + [DMA((count, 3))] * 4 + [DMA((2,)), DMA((3,)), DMA((3,))],
        compiler_params=comm_params(2),
        name="gather_sums",
    )(*arrays, moved)


def standard(rows):
    centred = rows - jnp.mean(rows, axis=-1, keepdims=True)
    inv_std = lax.rsqrt(jnp.mean(centred * centred, axis=-1, keepdims=True) + eps_norm)
    return centred * inv_std, inv_std


def lane_put(table, lane, column):
    lanes = lax.broadcasted_iota(jnp.int32, table.shape, 1)
    return jnp.where(lanes == lane, column, table)


def masked_scores(query, key):
    scores = nt(query, key) * (HD ** (-0.5))
    slots = lax.broadcasted_iota(jnp.int32, scores.shape, 1)
    return jnp.where(slots < LEN, scores, far_negative)


WGRAD_SPEC = pl.BlockSpec((8, 1, D // 8, D), lambda turn: (0, turn, 0, 0))


def weight_spec(layer):
    return pl.BlockSpec((8, 1, 1, D // 8, D), lambda turn: (0, turn, layer, 0, 0))


def attend_kernel(
    hidden_ref, weight_ref, vec_ref, router_ref,
    resid_ref, second_ref, saved_ref, table_ref, logs_ref, first_sc, attn_sc,
):
    turn = pl.program_id(0)
    images = hidden_ref.shape[0] // SEQ
    weight = weight_ref[:, 0, 0].reshape(D, D)

    @pl.when(turn == 0)
    def _():
        normed, _ = standard(hidden_ref[...].astype(f32))
        first_sc[...] = (normed * vec_ref[0:1] + vec_ref[1:2]).astype(bf16)
        attn_sc[...] = jnp.zeros_like(attn_sc)

    for image in range(images):
        rows = pl.ds(image * SEQ, SEQ)
        mixed = nn(first_sc[rows, :], weight[:, :QKV]).astype(bf16)
        logs = jnp.zeros((SEQ, 128), f32)
        contexts = []
        for head in range(HEADS_PART):
            query, key, value = [
                mixed[:, (kind * HEADS_PART + head) * HD : (kind * HEADS_PART + head + 1) * HD]
                for kind in range(3)
            ]
            scores = masked_scores(query, key)
            top = jnp.max(scores, axis=-1, keepdims=True)
            grown = jnp.exp(scores - top)
            total = jnp.sum(grown, axis=-1, keepdims=True)
            weights = (grown / total).astype(bf16)
            contexts.append(nn(weights, value).astype(bf16))
            logs = lane_put(logs, head, top + jnp.log(total))
        context = jnp.concatenate(contexts, axis=1)
        saved_ref[0, rows, :] = jnp.concatenate([mixed, context], axis=1)
        logs_ref[0, rows, :] = logs
        attn_sc[rows, :] += nt(context, weight[:, QKV:])

    @pl.when(turn == pl.num_programs(0) - 1)
    def _():
        attn = attn_sc[...]
        resid = hidden_ref[...].astype(f32) + attn
        resid_ref[...] = resid
        normed, _ = standard(resid)
        second = (normed * vec_ref[2:3] + vec_ref[3:4]).astype(bf16)
        second_ref[...] = second
        logits = nn(second, router_ref[...])
        lanes = lax.broadcasted_iota(jnp.int32, logits.shape, 1)
        logits = jnp.where(lanes < EXPERTS, logits, far_negative)
        grown = jnp.exp(logits - jnp.max(logits, axis=-1, keepdims=True))
        probs = grown / jnp.sum(grown, axis=-1, keepdims=True)
        table_ref[...] = lane_put(probs, EXPERTS, jnp.sum(attn * attn, axis=-1, keepdims=True))


def attend_rows(hidden, weights, vecs, router, layer):
    rows = hidden.shape[0]
    whole = lambda shape: pl.BlockSpec(shape, lambda turn: (0,) * len(shape))
    by_part = lambda shape: pl.BlockSpec((1,) + shape, lambda turn: (turn, 0, 0))
    return pl.pallas_call(
        attend_kernel,
        grid=(4,),
        in_specs=[whole((rows, D)), weight_spec(layer), whole((8, D)), whole((D, 128))],
        out_specs=(
            whole((rows, D)), whole((rows, D)), by_part((rows, D)), whole((rows, 128)), by_part((rows, 128)),
        ),
        out_shape=(
            jax.ShapeDtypeStruct((rows, D), f32),
            jax.ShapeDtypeStruct((rows, D), bf16),
            jax.ShapeDtypeStruct((4, rows, D), bf16),
            jax.ShapeDtypeStruct((rows, 128), f32),
            jax.ShapeDtypeStruct((4, rows, 128), f32),
        ),
        scratch_shapes=[pltpu.VMEM((rows, D), bf16), pltpu.VMEM((rows, D), f32)],
        compiler_params=pltpu.CompilerParams(vmem_limit_bytes=VMEM_LIMIT),
        name="attend_rows",
    )(hidden, weights, vecs, router)


def norm_pull(grad, normed, inv_std, gain):
    scaled = grad * gain
    one = jnp.mean(scaled, axis=-1, keepdims=True)
    two = jnp.mean(scaled * normed, axis=-1, keepdims=True)
    return inv_std * (scaled - one - normed * two)


def attend_pull_kernel(
    grad_ref, moved_ref, hidden_ref, resid_ref, saved_ref, table_ref, logs_ref, dprob_ref,
    weight_ref, vec_ref, router_ref,
    out_ref, wgrad_ref, small_ref, rgrad_ref,
    first_sc, grad_sc, low_sc, back_sc,
):
    turn = pl.program_id(0)
    rows_all = grad_ref.shape[0]
    images = rows_all // SEQ
    weight = weight_ref[:, 0, 0].reshape(D, D)
    scale = HD ** (-0.5)

    @pl.when(turn == 0)
    def _():
        normed, inv_std = standard(resid_ref[...])
        second = (normed * vec_ref[2:3] + vec_ref[3:4]).astype(bf16)
        lanes = lax.broadcasted_iota(jnp.int32, (rows_all, 128), 1)
        probs = jnp.where(lanes < EXPERTS, table_ref[...], 0.0)
        dprobs = dprob_ref[...]
        dlogit = probs * (dprobs - jnp.sum(probs * dprobs, axis=-1, keepdims=True))
        high = dlogit.astype(bf16)
        low = (dlogit - high.astype(f32)).astype(bf16)
        rgrad_ref[...] = tn(second, high) + tn(second, low)
        dsecond = nt(high, router_ref[...]) + nt(low, router_ref[...])
        for expert in range(EXPERTS):
            dsecond = dsecond + moved_ref[expert].astype(f32)
        small_ref[2:3] = jnp.sum(dsecond * normed, axis=0, keepdims=True)
        small_ref[3:4] = jnp.sum(dsecond, axis=0, keepdims=True)
        grad = grad_ref[...] + norm_pull(dsecond, normed, inv_std, vec_ref[2:3])
        grad_sc[...] = grad
        low_sc[...] = grad.astype(bf16)
        normed, _ = standard(hidden_ref[...].astype(f32))
        first_sc[...] = (normed * vec_ref[0:1] + vec_ref[1:2]).astype(bf16)
        back_sc[...] = jnp.zeros_like(back_sc)

    mixed_grads = []
    for image in range(images):
        rows = pl.ds(image * SEQ, SEQ)
        saved = saved_ref[0, rows, :]
        dcontext = nn(low_sc[rows, :], weight[:, QKV:]).astype(bf16)
        pieces = [[], [], []]
        for head in range(HEADS_PART):
            query, key, value = [
                saved[:, (kind * HEADS_PART + head) * HD : (kind * HEADS_PART + head + 1) * HD]
                for kind in range(3)
            ]
            dhead = dcontext[:, head * HD : (head + 1) * HD]
            weights = jnp.exp(masked_scores(query, key) - logs_ref[0, rows, head : head + 1])
            dvalue = tn(weights.astype(bf16), dhead)
            dweights = nt(dhead, value)
            inner = jnp.sum(weights * dweights, axis=-1, keepdims=True)
            dscores = (weights * (dweights - inner)).astype(bf16)
            pieces[0].append((nn(dscores, key) * scale).astype(bf16))
            pieces[1].append((tn(dscores, query) * scale).astype(bf16))
            pieces[2].append(dvalue.astype(bf16))
        mixed = jnp.concatenate(pieces[0] + pieces[1] + pieces[2], axis=1)
        back_sc[rows, :] += nt(mixed, weight[:, :QKV])
        mixed_grads.append(mixed)
    mixed = jnp.concatenate(mixed_grads, axis=0)
    wgrad = jnp.concatenate([tn(first_sc[...], mixed), tn(low_sc[...], saved_ref[0, :, QKV:])], axis=1)
    wgrad_ref[:, 0] = wgrad.astype(bf16).reshape(8, D // 8, D)

    @pl.when(turn == pl.num_programs(0) - 1)
    def _():
        dfirst = back_sc[...]
        normed, inv_std = standard(hidden_ref[...].astype(f32))
        small_ref[0:1] = jnp.sum(dfirst * normed, axis=0, keepdims=True)
        small_ref[1:2] = jnp.sum(dfirst, axis=0, keepdims=True)
        small_ref[4:8] = jnp.zeros((4, D), f32)
        out_ref[...] = grad_sc[...] + norm_pull(dfirst, normed, inv_std, vec_ref[0:1])


def attend_pull(grad, moved, hidden, resid, saved, table, logs, dprob, weights, vecs, router, layer):
    rows = grad.shape[0]
    whole = lambda shape: pl.BlockSpec(shape, lambda turn: (0,) * len(shape))
    by_part = lambda shape: pl.BlockSpec((1,) + shape, lambda turn: (turn, 0, 0))
    return pl.pallas_call(
        attend_pull_kernel,
        grid=(4,),
        in_specs=[
            whole((rows, D)), whole((EXPERTS, rows, D)), whole((rows, D)), whole((rows, D)),
            by_part((rows, D)), whole((rows, 128)), by_part((rows, 128)), whole((rows, 128)),
            weight_spec(layer), whole((8, D)), whole((D, 128)),
        ],
        out_specs=(whole((rows, D)), WGRAD_SPEC, whole((8, D)), whole((D, 128))),
        out_shape=(
            jax.ShapeDtypeStruct((rows, D), f32),
            jax.ShapeDtypeStruct((8, 4, D // 8, D), bf16),
            jax.ShapeDtypeStruct((8, D), f32),
            jax.ShapeDtypeStruct((D, 128), f32),
        ),
        scratch_shapes=[
            pltpu.VMEM((rows, D), bf16), pltpu.VMEM((rows, D), f32),
            pltpu.VMEM((rows, D), bf16), pltpu.VMEM((rows, D), f32),
        ],
        compiler_params=pltpu.CompilerParams(vmem_limit_bytes=VMEM_LIMIT),
        name="attend_pull",
    )(grad, moved, hidden, resid, saved, table, logs, dprob, weights, vecs, router)


GELU_C = math.sqrt(2.0 / math.pi)
GELU_K = 0.044715


def gelu_pair(pre):
    square = pre * pre
    bent = jnp.tanh(GELU_C * pre * (1.0 + GELU_K * square))
    half = 0.5 * (1.0 + bent)
    slope = half + (0.5 * GELU_C) * pre * (1.0 - bent * bent) * (1.0 + (3.0 * GELU_K) * square)
    return pre * half, slope


TILE = 256


def weight_of(held, which, turn):
    return held[which, pl.ds(turn * 4, 4)].reshape(D, D)


def expert_kernel(
    second_ref, pieces_ref, after_ref, rows_out, back_out, weights_out, act_out, slope_out,
    held, weights, made, acts, slopes, total,
    load_sem, join_send, join_recv, row_send, row_recv, pass_send, pass_recv, back_send, back_recv, out_sem, save_sem,
):
    _, core, _, near, partner = relatives()
    count = second_ref.shape[0]
    half = count // 2
    load = pltpu.make_async_copy(second_ref, held.at[0], load_sem.at[2])
    load.start()
    joins = []
    for which in range(2):
        src, dst = pieces_ref.at[:, which], weights.at[which, :, core]
        joins.append(pltpu.make_async_copy(src, dst, load_sem.at[which]))
        joins[-1].start()
    greet(near[1:] + [partner])
    for which in range(2):
        src, dst = pieces_ref.at[:, which], weights.at[which, :, core]
        joins.append(push(src, dst, join_send.at[which], join_recv.at[which], partner))
        joins[-1].start()
    rows = [
        push(second_ref, held.at[step], row_send.at[step - 1], row_recv.at[step - 1], near[step])
        for step in (1, 2)
    ]
    for copy in rows:
        copy.start()
    low, high = pl.ds(0, half), pl.ds(half, half)
    passed = [
        push(held.at[1, low], held.at[3, low], pass_send.at[0], pass_recv.at[0], near[2]),
        push(held.at[2, high], held.at[3, high], pass_send.at[1], pass_recv.at[1], near[1]),
    ]
    backs = [pltpu.make_async_copy(made.at[0], back_out.at[0], save_sem.at[2])] + [
        push(made.at[step], back_out.at[step], back_send.at[step - 1], back_recv.at[step - 1], near[step])
        for step in (1, 2, 3)
    ]
    save_rows = pltpu.make_async_copy(held, rows_out, save_sem.at[0])
    save_weights = pltpu.make_async_copy(weights, weights_out, save_sem.at[1])
    load.wait()
    for copy in joins:
        copy.wait()
    save_weights.start()

    def outs(slot, step, turn):
        place = pl.ds(pl.multiple_of(step * count, count), count)
        return (
            pltpu.make_async_copy(acts.at[slot], act_out.at[turn, place], out_sem.at[0, slot]),
            pltpu.make_async_copy(slopes.at[slot], slope_out.at[turn, place], out_sem.at[1, slot]),
        )

    def chunk(step, carry):
        @pl.when(step == 1)
        def _():
            for copy in rows:
                copy.wait()
            for copy in passed:
                copy.start()

        @pl.when(step == 3)
        def _():
            for copy in passed:
                copy.wait()
            save_rows.start()

        def part(turn, carry):
            slot = lax.rem(turn, 2)

            @pl.when(step * 4 + turn >= 2)
            def _():
                for copy in outs(slot, step, turn):
                    copy.wait()

            for at in range(0, count, TILE):
                tile = pl.ds(at, TILE)
                act, slope = gelu_pair(nn(held[step, tile, :], weight_of(weights, 0, turn)))
                act = act.astype(bf16)
                acts[slot, tile, :] = act
                slopes[slot, tile, :] = slope.astype(bf16)
                product = nt(act, weight_of(weights, 1, turn))
                total[tile, :] = jnp.where(turn == 0, product, total[tile, :] + product)
            for copy in outs(slot, step, turn):
                copy.start()
            return carry

        lax.fori_loop(0, 4, part, 0)
        made[step] = total[...].astype(bf16)
        for at in range(4):

            @pl.when(step == at)
            def _():
                backs[at].start()

        return carry

    lax.fori_loop(0, 4, chunk, 0)
    for slot in range(2):
        for copy in outs(slot, 3, 2 + slot):
            copy.wait()
    save_rows.wait()
    save_weights.wait()
    for copy in backs:
        copy.wait()


def expert_rows(second, pieces, after):
    count = second.shape[0]
    block = (count, D)
    weight_shape = (2, 16, 2, D // 8, D)
    return pl.pallas_call(
        expert_kernel,
        in_specs=[ANY_SPEC] * 3,
        out_specs=(ANY_SPEC,) * 5,
        out_shape=(
            jax.ShapeDtypeStruct((4,) + block, bf16),
            jax.ShapeDtypeStruct((4,) + block, bf16),
            jax.ShapeDtypeStruct(weight_shape, bf16),
            jax.ShapeDtypeStruct((4, 4 * count, D), bf16),
            jax.ShapeDtypeStruct((4, 4 * count, D), bf16),
        ),
        scratch_shapes=[
            pltpu.VMEM((4,) + block, bf16),
            pltpu.VMEM(weight_shape, bf16),
            pltpu.VMEM((4,) + block, bf16),
            pltpu.VMEM((2,) + block, bf16),
            pltpu.VMEM((2,) + block, bf16),
            pltpu.VMEM(block, f32),
            DMA((3,)), DMA((2,)), DMA((2,)), DMA((2,)), DMA((2,)), DMA((2,)), DMA((2,)),
            DMA((3,)), DMA((3,)), DMA((2, 2)), DMA((3,)),
        ],
        compiler_params=comm_params(4),
        name="expert_rows",
    )(second, pieces, after)


def expert_pull_kernel(
    sent_ref, rows_ref, act_ref, slope_ref, weights_ref, moved_out, wgrad_out,
    grads, rows, weights, pres, made, slopes, acts, total, halves, arrived,
    load_sem, row_send, row_recv, back_send, back_recv, slope_sem, act_sem, chip_send, chip_recv, save_sem,
):
    _, core, _, near, partner = relatives()
    count = sent_ref.shape[1]
    own = pltpu.make_async_copy(sent_ref.at[0], grads.at[0], load_sem.at[0])
    load_weights = pltpu.make_async_copy(weights_ref, weights, load_sem.at[1])
    load_rows = pltpu.make_async_copy(rows_ref, rows, load_sem.at[2])

    def slope_load(step, turn, slot):
        place = pl.ds(pl.multiple_of(step * count, count), count)
        return pltpu.make_async_copy(slope_ref.at[turn, place], slopes.at[slot], slope_sem.at[slot])

    def act_load(turn, slot):
        return pltpu.make_async_copy(act_ref.at[turn], acts.at[slot], act_sem.at[slot])

    own.start()
    load_weights.start()
    for slot in range(2):
        slope_load(0, slot, slot).start()
    load_rows.start()
    for slot in range(2):
        act_load(slot, slot).start()
    greet(near[1:] + [partner])
    sends = [None] + [
        push(sent_ref.at[step], grads.at[step], row_send.at[step - 1], row_recv.at[step - 1], near[step])
        for step in (1, 2, 3)
    ]
    sends[1].start()
    sends[2].start()
    backs = [pltpu.make_async_copy(made.at[0], moved_out.at[0], load_sem.at[3])] + [
        push(made.at[step], moved_out.at[step], back_send.at[step - 1], back_recv.at[step - 1], near[step])
        for step in (1, 2, 3)
    ]
    own.wait()
    load_weights.wait()

    def chunk(step, carry):
        @pl.when(step == 1)
        def _():
            sends[3].start()

        for at in (1, 2, 3):

            @pl.when(step == at)
            def _():
                sends[at].wait()

        def part(turn, carry):
            slot = lax.rem(turn, 2)
            slope_load(step, turn, slot).wait()
            for at in range(0, count, TILE):
                tile = pl.ds(at, TILE)
                dact = nn(grads[step, tile, :], weight_of(weights, 1, turn))
                dpre = (slopes[slot, tile, :].astype(f32) * dact).astype(bf16)
                pres[turn, step, tile, :] = dpre
                product = nt(dpre, weight_of(weights, 0, turn))
                total[tile, :] = jnp.where(turn == 0, product, total[tile, :] + product)

            @pl.when(step * 4 + turn < 14)
            def _():
                after = step * 4 + turn + 2
                slope_load(after // 4, after % 4, slot).start()

            return carry

        lax.fori_loop(0, 4, part, 0)
        made[step] = total[...].astype(bf16)
        for at in range(4):

            @pl.when(step == at)
            def _():
                backs[at].start()

        return carry

    lax.fori_loop(0, 4, chunk, 0)
    load_rows.wait()

    def chip_copy(which, turn):
        return push(
            halves.at[which, turn, :, 1 - core], arrived.at[which, turn],
            chip_send.at[which, turn], chip_recv.at[which, turn], partner,
        )

    def save(which, turn):
        return pltpu.make_async_copy(arrived.at[which, turn], wgrad_out.at[turn, :, which], save_sem.at[which, turn])

    def finish(turn):
        for which in range(2):
            chip_copy(which, turn).wait()
            arrived[which, turn] = (
                halves[which, turn, :, core].astype(f32) + arrived[which, turn].astype(f32)
            ).astype(bf16)
            save(which, turn).start()

    def wgrad(turn, carry):
        slot = lax.rem(turn, 2)
        flat = (4 * count, D)
        act_load(turn, slot).wait()
        first = tn(rows[...].reshape(flat), pres[turn].reshape(flat))
        halves[0, turn] = first.astype(bf16).reshape(4, 2, D // 8, D)
        chip_copy(0, turn).start()
        second = tn(grads[...].reshape(flat), acts[slot])
        halves[1, turn] = second.astype(bf16).reshape(4, 2, D // 8, D)
        chip_copy(1, turn).start()

        @pl.when(turn < 2)
        def _():
            act_load(turn + 2, slot).start()

        @pl.when(turn > 0)
        def _():
            finish(turn - 1)

        return carry

    lax.fori_loop(0, 4, wgrad, 0)
    finish(3)
    for turn in range(4):
        for which in range(2):
            save(which, turn).wait()
    for copy in backs:
        copy.wait()


def expert_pull(sent, rows, act, slope, weights):
    count = sent.shape[1]
    block = (count, D)
    slices = D // 8
    return pl.pallas_call(
        expert_pull_kernel,
        in_specs=[ANY_SPEC] * 5,
        out_specs=(ANY_SPEC, ANY_SPEC),
        out_shape=(
            jax.ShapeDtypeStruct((4,) + block, bf16),
            jax.ShapeDtypeStruct((4, 4, 2, slices, D), bf16),
        ),
        scratch_shapes=[
            pltpu.VMEM((4,) + block, bf16),
            pltpu.VMEM((4,) + block, bf16),
            pltpu.VMEM(weights.shape, bf16),
            pltpu.VMEM((4, 4) + block, bf16),
            pltpu.VMEM((4,) + block, bf16),
            pltpu.VMEM((2,) + block, bf16),
            pltpu.VMEM((2, 4 * count, D), bf16),
            pltpu.VMEM(block, f32),
            pltpu.VMEM((2, 4, 4, 2, slices, D), bf16),
            pltpu.VMEM((2, 4, 4, slices, D), bf16),
            DMA((4,)), DMA((3,)), DMA((3,)), DMA((3,)), DMA((3,)), DMA((2,)), DMA((2,)),
            DMA((2, 4)), DMA((2, 4)), DMA((2, 4)),
        ],
        compiler_params=comm_params(5),
        name="expert_pull",
    )(sent, rows, act, slope, weights)


def per_device(
    tokens, counts, routes, norm_gain, norm_bias, w_router, w_qkv, w_out, w_in, w_back, cotangent
):
    dp, part = lax.axis_index("dp"), lax.axis_index("tensor")
    place = dp // 2
    own_rows = tokens.shape[0]
    slices = D // 8
    row_ids = part * own_rows + jnp.arange(own_rows, dtype=jnp.int32)
    image_count = lax.dynamic_index_in_dim(counts, dp, keepdims=False)
    valid = ((row_ids // SEQ < image_count) & (row_ids % SEQ < LEN)).astype(f32)[:, None]
    my_routes = lax.dynamic_slice_in_dim(routes, part * own_rows, own_rows, axis=1)
    row, col = place // 2, place % 2
    served = jnp.stack([place, row * 2 + 1 - col, (1 - row) * 2 + col, (1 - row) * 2 + 1 - col])
    expert_of = served[:, None] == jnp.arange(EXPERTS)[None, :]
    chosen = (my_routes[:, :, :, None] == served).any(axis=2)

    def by_place(table):
        return jnp.sum(jnp.where(expert_of[None], table[:, None, :], 0.0), axis=-1)

    attn_blocks = jnp.concatenate(
        [
            jnp.transpose(w_qkv, (0, 2, 1, 3)).reshape(LAYERS, slices, QKV),
            jnp.transpose(w_out, (0, 2, 1)),
        ],
        axis=2,
    )
    small = jnp.concatenate([norm_gain, norm_bias, w_router])
    small = jnp.pad(small, (0, 2048 - small.shape[0])).reshape(16, 128)

    def expert_pieces(layer, after):
        packed = jnp.stack([w_in[layer], w_back[layer]], axis=1)
        arrived = swap(packed, "plane", False, 3 + 4 * layer, after)
        return arrived, lax.all_gather(arrived, "tensor", axis=0, tiled=True)

    pieces = [expert_pieces(0, small), None]
    attn_all, small_all = spread(attn_blocks, small)
    flat = small_all.reshape(32, 2048)
    vec_count = LAYERS * 2 * D // 32
    gains = flat[:, :vec_count].reshape(LAYERS, 2, D).astype(f32)
    biases = flat[:, vec_count : 2 * vec_count].reshape(LAYERS, 2, D).astype(f32)
    routers = flat[:, 2 * vec_count : 2 * vec_count + LAYERS * D * EXPERTS // 32]
    routers = jnp.pad(routers.reshape(LAYERS, D, EXPERTS), ((0, 0), (0, 0), (0, 128 - EXPERTS)))
    vecs = jnp.pad(
        jnp.stack([gains[:, 0], biases[:, 0], gains[:, 1], biases[:, 1]], axis=1), ((0, 0), (0, 4), (0, 0))
    )

    hidden = tokens
    kept = []
    stats = []
    for layer in range(LAYERS):
        resid, second, saved, table, logs = attend_rows(hidden, attn_all, vecs[layer], routers[layer], layer)
        if layer + 1 < LAYERS:
            pieces[layer + 1] = expert_pieces(layer + 1, second)
        after = pieces[min(layer + 1, LAYERS - 1)][0]
        rows, back, weights, act, slope = expert_rows(second, pieces[layer][1], after)
        gates = jnp.where(chosen[layer], by_place(table[:, :EXPERTS]), 0.0)
        moe = sum(gates[:, at : at + 1] * back[at].astype(f32) for at in range(EXPERTS))
        result = resid + moe
        stats.append(
            jnp.stack(
                [
                    jnp.sum(valid * result * result),
                    jnp.sum(valid[:, 0] * table[:, EXPERTS]),
                    jnp.sum(valid * moe * moe),
                ]
            )
        )
        kept.append((hidden, resid, saved, table, logs, rows, weights, act, slope, back, gates))
        hidden = result

    grad = cotangent.astype(f32) * valid
    attn_grads, owned, small_grads, router_grads = [], [], [], []
    for layer in reversed(range(LAYERS)):
        before, resid, saved, table, logs, rows, weights, act, slope, back, gates = kept[layer]
        low = grad.astype(bf16)
        dgate = [jnp.sum(back[at].astype(f32) * low.astype(f32), axis=-1) for at in range(EXPERTS)]
        dprob = by_place(jnp.where(chosen[layer], jnp.stack(dgate, axis=1), 0.0))
        dprob = jnp.pad(dprob, ((0, 0), (0, 128 - EXPERTS)))
        sent = jnp.stack([(gates[:, at : at + 1] * low.astype(f32)).astype(bf16) for at in range(EXPERTS)])
        moved, wgrad = expert_pull(sent, rows, act, slope, weights)
        summed = lax.psum_scatter(wgrad, "tensor", scatter_dimension=0, tiled=False)
        owned.append(summed)
        grad, attn_wgrad, small_grad, router_grad = attend_pull(
            grad, moved, before, resid, saved, table, logs, dprob, attn_all, vecs[layer], routers[layer], layer
        )
        attn_grads.append(attn_wgrad.reshape(4, 2, 4, slices, D))
        small_grads.append(small_grad[:4])
        router_grads.append(router_grad[:, :EXPERTS])
    for listed in (small_grads, router_grads, owned):
        listed.reverse()

    vec_grads = jnp.stack(small_grads).reshape(LAYERS, 2, 2, D)
    packed = jnp.concatenate(
        [
            vec_grads[:, :, 0].reshape(32, -1),
            vec_grads[:, :, 1].reshape(32, -1),
            jnp.stack(router_grads).reshape(32, -1),
            jnp.broadcast_to(jnp.stack(stats).reshape(1, -1), (32, 3 * LAYERS)),
        ],
        axis=1,
    )
    packed = jnp.pad(packed, ((0, 0), (0, 1024 - packed.shape[1]))).reshape(4, 2, 4, 8, 128)
    *attn_grads, total, moved_later = gather_sums(attn_grads + [packed], owned[1])
    attn_grad = jnp.stack(attn_grads[::-1])
    total = total.reshape(-1)
    share = LAYERS * 2 * D // 32
    router_share = LAYERS * D * EXPERTS // 32
    at = 2 * share + router_share
    denom = jnp.sum(counts).astype(f32) * (LEN * D)
    rms = jnp.sqrt(total[at : at + 3 * LAYERS].reshape(LAYERS, 3) / denom)
    qkv_grad = jnp.transpose(attn_grad[:, :, :QKV].reshape(LAYERS, slices, 3, QKV // 3), (0, 2, 1, 3))
    out_grad = jnp.transpose(attn_grad[:, :, QKV:], (0, 2, 1))
    moved_first = swap(owned[0], "plane", False, 6, moved_later)
    expert_grad = jnp.stack([moved_first, moved_later], axis=1).astype(f32)
    expert_grad = jnp.transpose(expert_grad, (2, 1, 0, 3, 4))
    return (
        hidden,
        grad,
        total[:share],
        total[share : 2 * share],
        total[2 * share : at],
        qkv_grad,
        out_grad,
        expert_grad[0],
        expert_grad[1],
        rms,
    )


def solution(mesh):
    return jax.shard_map(
        per_device if mesh.shape["dp"] == 8 else per_device_general,
        mesh=mesh,
        in_specs=(
            P(("dp", "tensor"), None),
            P(),
            P(None, "dp", None),
            P(("dp", "tensor")),
            P(("dp", "tensor")),
            P(("dp", "tensor")),
            P(None, None, "dp", "tensor"),
            P(None, "tensor", "dp"),
            P(None, None, "dp", "tensor"),
            P(None, None, "dp", "tensor"),
            P(("dp", "tensor"), None),
        ),
        out_specs=(
            P(("dp", "tensor"), None),
            P(("dp", "tensor"), None),
            P(("dp", "tensor")),
            P(("dp", "tensor")),
            P(("dp", "tensor")),
            P(None, None, "dp", "tensor"),
            P(None, "tensor", "dp"),
            P(None, None, "dp", "tensor"),
            P(None, None, "dp", "tensor"),
            P(),
        ),
        check_vma=False,
    )
```

```python
from functools import partial
import math

import jax
import jax.numpy as jnp
from jax import lax
from jax.experimental import pallas as pl
from jax.experimental.pallas import tpu as pltpu
from jax.sharding import PartitionSpec as P

D = 768
HD = 64
LEN = 197
SEQ = 256
LAYERS = 2


eps_norm = 1e-06
far_negative = -1e30
highest = lax.Precision.HIGHEST


def norm_forward(row_vals, gain_vec, bias_vec):
    row_mean = jnp.mean(row_vals, axis=-1, keepdims=True)
    centred = row_vals - row_mean
    row_var = jnp.mean(centred * centred, axis=-1, keepdims=True)
    inv_std = lax.rsqrt(row_var + eps_norm)
    normed = centred * inv_std
    return (normed * gain_vec + bias_vec, normed, inv_std)


def norm_backward(grad_vals, normed, inv_std, gain_vec):
    gain_grad = jnp.sum(grad_vals * normed, axis=0)
    bias_grad = jnp.sum(grad_vals, axis=0)
    scaled = grad_vals * gain_vec
    mean_one = jnp.mean(scaled, axis=-1, keepdims=True)
    mean_two = jnp.mean(scaled * normed, axis=-1, keepdims=True)
    return (inv_std * (scaled - mean_one - normed * mean_two), gain_grad, bias_grad)


def gather_rows(row_vals):
    return lax.all_gather(row_vals, "tensor", axis=0, tiled=True)


def sum_rows(row_vals):
    return lax.psum_scatter(
        row_vals.astype(jnp.bfloat16), "tensor", scatter_dimension=0, tiled=True
    ).astype(jnp.float32)


def sum_slots(slot_vals):
    return lax.psum_scatter(
        slot_vals.astype(jnp.bfloat16), "tensor", scatter_dimension=1, tiled=True
    ).astype(jnp.float32)


def to_experts(make_rows, positions):
    return lax.all_to_all(make_rows(positions), "dp", split_axis=0, concat_axis=0, tiled=True)


def attend(block_in, key_keep, score_scale):
    query_heads, key_heads, value_heads = block_in
    scores = (
        jnp.einsum("iqhd,ikhd->ihqk", query_heads, key_heads, preferred_element_type=jnp.float32)
        * score_scale
    )
    scores = jnp.where(key_keep, scores, far_negative)
    row_max = jnp.max(scores, axis=-1, keepdims=True)
    exponent = jnp.exp(scores - row_max)
    row_total = jnp.sum(exponent, axis=-1, keepdims=True)
    weights = (exponent / row_total).astype(jnp.bfloat16)
    context = jnp.einsum(
        "ihqk,ikhd->iqhd", weights, value_heads, preferred_element_type=jnp.float32
    )
    return (context.astype(jnp.bfloat16), (row_max + jnp.log(row_total))[..., 0])


def attend_back(block_in, key_keep, score_scale):
    query_heads, key_heads, value_heads, d_context, log_total = block_in
    scores = (
        jnp.einsum("iqhd,ikhd->ihqk", query_heads, key_heads, preferred_element_type=jnp.float32)
        * score_scale
    )
    scores = jnp.where(key_keep, scores, far_negative)
    weights = jnp.exp(scores - log_total[..., None])
    d_values = jnp.einsum(
        "ihqk,iqhd->ikhd",
        weights.astype(jnp.bfloat16),
        d_context,
        preferred_element_type=jnp.float32,
    )
    d_weights = jnp.einsum(
        "iqhd,ikhd->ihqk", d_context, value_heads, preferred_element_type=jnp.float32
    )
    inner_sum = jnp.sum(weights * d_weights, axis=-1, keepdims=True)
    d_scores = (weights * (d_weights - inner_sum)).astype(jnp.bfloat16)
    d_queries = (
        jnp.einsum("ihqk,ikhd->iqhd", d_scores, key_heads, preferred_element_type=jnp.float32)
        * score_scale
    )
    d_keys = (
        jnp.einsum("ihqk,iqhd->ikhd", d_scores, query_heads, preferred_element_type=jnp.float32)
        * score_scale
    )
    return (
        d_queries.astype(jnp.bfloat16),
        d_keys.astype(jnp.bfloat16),
        d_values.astype(jnp.bfloat16),
    )


def contract_first(left_mat, right_mat):
    return lax.dot_general(
        left_mat, right_mat, (((0,), (0,)), ((), ())), preferred_element_type=jnp.float32
    )


def contract_last(left_mat, right_mat):
    return lax.dot_general(
        left_mat, right_mat, (((1,), (1,)), ((), ())), preferred_element_type=jnp.float32
    )


def per_device_general(
    tokens, counts, routes, norm_gain, norm_bias, w_router, w_qkv, w_out, w_in, w_back, cotangent
):
    groups = lax.axis_size("dp")
    parts = lax.axis_size("tensor")
    experts = groups // 2
    group_idx = lax.axis_index("dp")
    my_part = lax.axis_index("tensor")
    own_rows = tokens.shape[0]
    rows_all = own_rows * parts
    slot_count = 3 * rows_all // experts
    half_slots = slot_count // 2
    quarter = half_slots // parts
    score_scale = HD ** (-0.5)
    images = rows_all // SEQ
    per_block = math.gcd(images, max(1, 512 // SEQ))
    blocks = images // per_block
    head_cols = w_qkv.shape[-1]
    heads_here = head_cols // HD
    key_keep = jnp.arange(SEQ) < LEN
    gain_flat, bias_flat, router_flat = (
        lax.all_gather(norm_gain, ("dp", "tensor"), axis=0, tiled=True),
        lax.all_gather(norm_bias, ("dp", "tensor"), axis=0, tiled=True),
        lax.all_gather(w_router, ("dp", "tensor"), axis=0, tiled=True),
    )
    gains_all = gain_flat.astype(jnp.float32).reshape(LAYERS, 2, D)
    biases_all = bias_flat.astype(jnp.float32).reshape(LAYERS, 2, D)
    router_all = router_flat.reshape(LAYERS, D, experts)
    row_ids = my_part * own_rows + jnp.arange(own_rows, dtype=jnp.int32)
    image_count = lax.dynamic_index_in_dim(counts, group_idx, keepdims=False)
    valid_rows = ((row_ids // SEQ < image_count) & (row_ids % SEQ < LEN)).astype(jnp.float32)[
        :, None
    ]

    def split_heads(columns):
        return columns.reshape(blocks, per_block, SEQ, heads_here, HD)

    hidden = tokens.astype(jnp.float32)
    kept_layers = []
    stat_terms = []
    for layer_idx in range(LAYERS):
        gain_pair = gains_all[layer_idx]
        shift_pair = biases_all[layer_idx]
        wq_part, wo_part = (
            lax.all_gather(w_qkv[layer_idx], "dp", axis=1, tiled=True),
            lax.all_gather(w_out[layer_idx], "dp", axis=1, tiled=True),
        )
        w_cat = jnp.concatenate([wq_part[0], wq_part[1], wq_part[2]], axis=1)
        up_part, back_part = (
            lax.all_to_all(
                jnp.repeat(w_in[layer_idx], 2, axis=0),
                "dp",
                split_axis=0,
                concat_axis=0,
                tiled=True,
            ),
            lax.all_to_all(
                jnp.repeat(w_back[layer_idx], 2, axis=0),
                "dp",
                split_axis=0,
                concat_axis=0,
                tiled=True,
            ),
        )
        up_part = up_part.reshape(D, -1)
        back_part = back_part.reshape(D, -1)
        up_use, back_use = (up_part, back_part)
        norm_one, normed_one, inv_one = norm_forward(hidden, gain_pair[0], shift_pair[0])
        rows_one = gather_rows(norm_one.astype(jnp.bfloat16))
        qkv_rows = jnp.dot(rows_one, w_cat, preferred_element_type=jnp.float32).astype(jnp.bfloat16)
        query_heads = split_heads(qkv_rows[:, :head_cols])
        key_heads = split_heads(qkv_rows[:, head_cols : 2 * head_cols])
        value_heads = split_heads(qkv_rows[:, 2 * head_cols :])
        context, log_total = lax.map(
            partial(attend, key_keep=key_keep, score_scale=score_scale),
            (query_heads, key_heads, value_heads),
        )
        context = context.reshape(rows_all, head_cols)
        attn_out = sum_rows(jnp.dot(context, wo_part, preferred_element_type=jnp.float32))
        residual = hidden + attn_out
        norm_two, normed_two, inv_two = norm_forward(residual, gain_pair[1], shift_pair[1])
        rows_two = gather_rows(norm_two.astype(jnp.bfloat16))
        router = router_all[layer_idx]
        router_probs = jax.nn.softmax(
            jnp.dot(rows_two, router, preferred_element_type=jnp.float32), axis=-1
        )
        routing = routes[layer_idx]
        one_hot = routing[:, :, None] == jnp.arange(experts)[None, None, :]
        gate_vals = jnp.sum(jnp.where(one_hot, router_probs[:, None, :], 0.0), axis=-1)
        flat_pick = routing.reshape(-1)
        hot_int = (flat_pick[:, None] == jnp.arange(experts)[None, :]).astype(jnp.int32)
        rank_in = jnp.sum((jnp.cumsum(hot_int, axis=0) - hot_int) * hot_int, axis=1)
        target = flat_pick * slot_count + rank_in
        positions = (
            jnp.full((experts * slot_count,), 2 * rows_all, jnp.int32)
            .at[target]
            .set(jnp.arange(2 * rows_all, dtype=jnp.int32))
        )
        positions = positions.reshape(groups, half_slots)
        padded_two = jnp.concatenate([rows_two, jnp.zeros((1, D), jnp.bfloat16)], axis=0)

        def take_rows(slot_index):
            return padded_two[jnp.where(slot_index < 2 * rows_all, slot_index // 2, rows_all)]

        arrived = to_experts(take_rows, positions).reshape(-1, D)
        pre_act = jnp.dot(arrived, up_use, preferred_element_type=jnp.float32)
        activation = jax.nn.gelu(pre_act, approximate=True).astype(jnp.bfloat16)
        partial_out = contract_last(activation, back_use)
        summed = sum_slots(partial_out.reshape(groups, half_slots, D)).astype(jnp.bfloat16)
        returned = lax.all_to_all(summed, "dp", split_axis=0, concat_axis=0, tiled=True)
        slot_pair = target.reshape(rows_all, 2)
        owner = slot_pair // half_slots
        inside = slot_pair % half_slots
        in_quarter = inside // quarter == my_part
        pick_index = jnp.where(
            in_quarter, owner * quarter + inside - my_part * quarter, groups * quarter
        )
        padded_ret = jnp.concatenate(
            [returned.reshape(groups * quarter, D), jnp.zeros((1, D), jnp.bfloat16)], axis=0
        )
        chosen = padded_ret[pick_index]
        expert_out = sum_rows(jnp.sum(gate_vals[:, :, None] * chosen, axis=1))
        result = residual + expert_out
        stat_terms.append(
            jnp.stack(
                [
                    jnp.sum(valid_rows * result * result),
                    jnp.sum(valid_rows * attn_out * attn_out),
                    jnp.sum(valid_rows * expert_out * expert_out),
                ]
            )
        )
        kept_layers.append(
            (
                wo_part,
                w_cat,
                up_use,
                back_use,
                normed_one,
                inv_one,
                rows_one,
                query_heads,
                key_heads,
                value_heads,
                context,
                log_total,
                normed_two,
                inv_two,
                rows_two,
                router,
                router_probs,
                one_hot,
                gate_vals,
                positions,
                arrived,
                pre_act,
                activation,
                pick_index,
                chosen,
            )
        )
        hidden = result
    totals = lax.psum(jnp.stack(stat_terms), ("dp", "tensor"))
    denom = jnp.sum(counts).astype(jnp.float32) * (LEN * D)
    rms = jnp.sqrt(totals / denom)
    grad_rows = cotangent.astype(jnp.float32) * valid_rows
    gain_grads = [None] * LAYERS
    bias_grads = [None] * LAYERS
    router_grads = [None] * LAYERS
    qkv_grads = [None] * LAYERS
    out_grads = [None] * LAYERS
    up_grads = [None] * LAYERS
    back_grads = [None] * LAYERS
    for layer_idx in reversed(range(LAYERS)):
        (
            wo_part,
            w_cat,
            up_use,
            back_use,
            normed_one,
            inv_one,
            rows_one,
            query_heads,
            key_heads,
            value_heads,
            context,
            log_total,
            normed_two,
            inv_two,
            rows_two,
            router,
            router_probs,
            one_hot,
            gate_vals,
            positions,
            arrived,
            pre_act,
            activation,
            pick_index,
            chosen,
        ) = kept_layers[layer_idx]
        gain_pair = gains_all[layer_idx]
        grad_moe = gather_rows(grad_rows.astype(jnp.bfloat16))
        d_gates = jnp.einsum("rkd,rd->rk", chosen, grad_moe, preferred_element_type=jnp.float32)
        padded_down = jnp.concatenate([grad_moe, jnp.zeros((1, D), jnp.bfloat16)], axis=0)
        flat_gates = jnp.concatenate([gate_vals.reshape(-1), jnp.zeros((1,), jnp.float32)], axis=0)

        def scaled_rows(slot_index):
            filled = slot_index < 2 * rows_all
            row_index = jnp.where(filled, slot_index // 2, rows_all)
            gate_index = jnp.where(filled, slot_index, 2 * rows_all)
            return (flat_gates[gate_index][..., None] * padded_down[row_index]).astype(jnp.bfloat16)

        d_expert_rows = to_experts(scaled_rows, positions).reshape(-1, D)
        d_activation = jnp.dot(d_expert_rows, back_use, preferred_element_type=jnp.float32)
        back_grad = contract_first(d_expert_rows, activation)
        d_pre = jax.vjp(partial(jax.nn.gelu, approximate=True), pre_act)[1](d_activation)[0].astype(
            jnp.bfloat16
        )
        up_grad = contract_first(arrived, d_pre)
        d_arrived = contract_last(d_pre, up_use)
        d_slots = sum_slots(d_arrived.reshape(groups, half_slots, D))
        d_back_rows, up_pieces, back_pieces = (
            lax.all_to_all(
                d_slots.astype(jnp.bfloat16), "dp", split_axis=0, concat_axis=0, tiled=True
            ).astype(d_slots.dtype),
            lax.all_to_all(
                up_grad.reshape(groups, -1, up_grad.shape[1]).astype(jnp.bfloat16),
                "dp",
                split_axis=0,
                concat_axis=0,
                tiled=True,
            ).astype(jnp.float32),
            lax.all_to_all(
                back_grad.reshape(groups, -1, back_grad.shape[1]).astype(jnp.bfloat16),
                "dp",
                split_axis=0,
                concat_axis=0,
                tiled=True,
            ).astype(jnp.float32),
        )
        up_grads[layer_idx] = up_pieces.reshape(
            experts, 2, up_pieces.shape[1], up_pieces.shape[2]
        ).sum(axis=1)
        back_grads[layer_idx] = back_pieces.reshape(
            experts, 2, back_pieces.shape[1], back_pieces.shape[2]
        ).sum(axis=1)
        padded_back = jnp.concatenate(
            [d_back_rows.reshape(groups * quarter, D), jnp.zeros((1, D), jnp.float32)], axis=0
        )
        d_rows_two = jnp.sum(padded_back[pick_index], axis=1)
        d_probs = jnp.sum(jnp.where(one_hot, d_gates[:, :, None], 0.0), axis=1)
        d_logits = router_probs * (
            d_probs - jnp.sum(router_probs * d_probs, axis=-1, keepdims=True)
        )
        d_rows_two = d_rows_two + jnp.dot(d_logits, router.astype(jnp.float32).T, precision=highest)
        router_grads[layer_idx] = jnp.dot(
            rows_two.astype(jnp.float32).T, d_logits, precision=highest
        )
        d_second = sum_rows(d_rows_two)
        d_resid, gain_two, bias_two = norm_backward(d_second, normed_two, inv_two, gain_pair[1])
        grad_rows = grad_rows + d_resid
        grad_attn = gather_rows(grad_rows.astype(jnp.bfloat16))
        d_context = contract_last(grad_attn, wo_part).astype(jnp.bfloat16)
        out_grad = contract_first(context, grad_attn)
        d_queries, d_keys, d_values = lax.map(
            partial(attend_back, key_keep=key_keep, score_scale=score_scale),
            (query_heads, key_heads, value_heads, split_heads(d_context), log_total),
        )
        d_mixed = jnp.concatenate(
            [
                d_queries.reshape(rows_all, head_cols),
                d_keys.reshape(rows_all, head_cols),
                d_values.reshape(rows_all, head_cols),
            ],
            axis=1,
        )
        cat_grad = contract_first(rows_one, d_mixed)
        qkv_grad = jnp.stack(
            [
                cat_grad[:, :head_cols],
                cat_grad[:, head_cols : 2 * head_cols],
                cat_grad[:, 2 * head_cols :],
            ]
        )
        qkv_grads[layer_idx], out_grads[layer_idx] = (
            lax.psum_scatter(qkv_grad, "dp", scatter_dimension=1, tiled=True),
            lax.psum_scatter(out_grad, "dp", scatter_dimension=1, tiled=True),
        )
        d_first = sum_rows(contract_last(d_mixed, w_cat))
        d_hidden, gain_one, bias_one = norm_backward(d_first, normed_one, inv_one, gain_pair[0])
        grad_rows = grad_rows + d_hidden
        gain_grads[layer_idx] = jnp.stack([gain_one, gain_two])
        bias_grads[layer_idx] = jnp.stack([bias_one, bias_two])
    grad_gain, grad_bias, grad_router = (
        lax.psum_scatter(
            jnp.stack(gain_grads).reshape(-1), ("dp", "tensor"), scatter_dimension=0, tiled=True
        ),
        lax.psum_scatter(
            jnp.stack(bias_grads).reshape(-1), ("dp", "tensor"), scatter_dimension=0, tiled=True
        ),
        lax.psum_scatter(
            jnp.stack(router_grads).reshape(-1), ("dp", "tensor"), scatter_dimension=0, tiled=True
        ),
    )
    return (
        hidden,
        grad_rows,
        grad_gain,
        grad_bias,
        grad_router,
        jnp.stack(qkv_grads),
        jnp.stack(out_grads),
        jnp.stack(up_grads),
        jnp.stack(back_grads),
        rms,
    )


bf16 = jnp.bfloat16
f32 = jnp.float32
MESH = pl.DeviceIdType.MESH
VMEM_LIMIT = 63 * 1024 * 1024
EXPERTS = 4
HEADS_PART = 3
QKV = 3 * HEADS_PART * HD


def nn(left, right):
    return jnp.dot(left, right, preferred_element_type=f32)


def nt(left, right):
    return lax.dot_general(left, right, (((1,), (1,)), ((), ())), preferred_element_type=f32)


def tn(left, right):
    return lax.dot_general(left, right, (((0,), (0,)), ((), ())), preferred_element_type=f32)


def group_of(kind):
    dp, part = lax.axis_index("dp"), lax.axis_index("tensor")
    if kind == "plane":
        return dp // 2, 4, lambda place: (place * 2 + dp % 2, part)
    if kind == "column":
        return part, 4, lambda place: (dp, place)
    if kind == "chip":
        return dp % 2, 2, lambda place: (dp // 2 * 2 + place, part)
    return dp * 4 + part, 32, lambda place: (place // 4, place % 4)


def greet(devices):
    barrier = pltpu.get_barrier_semaphore()
    for device in devices:
        pl.semaphore_signal(barrier, inc=1, device_id=device, device_id_type=MESH)
    pl.semaphore_wait(barrier, len(devices))


def relatives():
    dp, part = lax.axis_index("dp"), lax.axis_index("tensor")
    place, core = dp // 2, dp % 2
    row, col = place // 2, place % 2
    near = (row * 2 + 1 - col, (1 - row) * 2 + col, (1 - row) * 2 + 1 - col)
    return place, core, part, [None] + [(at * 2 + core, part) for at in near], (place * 2 + 1 - core, part)


def push(src, dst, send_sem, recv_sem, device):
    return pltpu.make_async_remote_copy(
        src_ref=src, dst_ref=dst, send_sem=send_sem, recv_sem=recv_sem, device_id=device, device_id_type=MESH
    )


def comm_params(collective_id):
    return pltpu.CompilerParams(
        collective_id=collective_id, has_side_effects=True, vmem_limit_bytes=VMEM_LIMIT
    )


ANY_SPEC = pl.BlockSpec(memory_space=pl.ANY)
DMA = pltpu.SemaphoreType.DMA


def column_copies(src, column, send_sem, recv_sem):
    dp, part = lax.axis_index("dp"), lax.axis_index("tensor")
    others = [lax.rem(part + step, 4) for step in range(1, 4)]
    return [
        push(src.at[other], column.at[step], send_sem.at[step], recv_sem.at[step], (dp, other))
        for step, other in enumerate(others)
    ]


def column_greets():
    dp, part = lax.axis_index("dp"), lax.axis_index("tensor")
    return [(dp, lax.rem(part + step, 4)) for step in range(1, 4)]


def column_sum(src, column):
    return (
        src[lax.axis_index("tensor")].astype(f32)
        + column[0].astype(f32)
        + column[1].astype(f32)
        + column[2].astype(f32)
    )


def plane_moves(src, dst, send_sem, recv_sem):
    place, _, _, near, _ = relatives()
    return [
        push(src.at[near[step][0] // 2], dst.at[place], send_sem.at[step - 1], recv_sem.at[step - 1], near[step])
        for step in (1, 2, 3)
    ]


def spread_column_kernel(
    block_ref, small_ref, moved_ref, block_out, small_out, swapped,
    held, local_sem, col_send, col_recv, held_sem, swap_send, swap_recv,
):
    place, _, part, near, _ = relatives()
    bring = pltpu.make_async_copy(moved_ref.at[place], held, held_sem.at[0])
    bring.start()
    pairs = ((block_ref, block_out), (small_ref, small_out))
    locals_ = [
        pltpu.make_async_copy(src, dst.at[part], local_sem.at[which]) for which, (src, dst) in enumerate(pairs)
    ]
    for copy in locals_:
        copy.start()
    greet(column_greets() + near[1:])
    swaps = plane_moves(moved_ref, swapped, swap_send, swap_recv)
    columns = [
        push(src, dst.at[part], col_send.at[which, step], col_recv.at[which, step], other)
        for which, (src, dst) in enumerate(pairs)
        for step, other in enumerate(column_greets())
    ]
    for copy in swaps + columns:
        copy.start()
    bring.wait()
    keep = pltpu.make_async_copy(held, swapped.at[place], held_sem.at[1])
    keep.start()
    for copy in locals_:
        copy.wait()
    keep.wait()
    for copy in swaps + columns:
        copy.wait()


def spread_column(block, small, moved):
    vmem_spec = pl.BlockSpec(memory_space=pltpu.VMEM)
    return pl.pallas_call(
        spread_column_kernel,
        out_shape=(
            jax.ShapeDtypeStruct((4,) + block.shape, block.dtype),
            jax.ShapeDtypeStruct((4,) + small.shape, small.dtype),
            jax.ShapeDtypeStruct(moved.shape, moved.dtype),
        ),
        in_specs=[vmem_spec, vmem_spec, ANY_SPEC],
        out_specs=(ANY_SPEC,) * 3,
        scratch_shapes=[
            pltpu.VMEM(moved.shape[1:], moved.dtype),
            DMA((2,)), DMA((2, 3)), DMA((2, 3)), DMA((2,)), DMA((3,)), DMA((3,)),
        ],
        compiler_params=comm_params(3),
        name="spread_column",
    )(block, small, moved)


def spread_kernel(
    block_ref, small_ref, moved_ref, block_out, small_out, swapped,
    held, local_sem, near_send, near_recv, chip_send, chip_recv, held_sem, swap_send, swap_recv,
):
    place, core, _, near, partner = relatives()
    dp = place * 2 + core
    bring = pltpu.make_async_copy(moved_ref.at[place], held, held_sem.at[0])
    bring.start()
    pairs = ((block_ref, block_out), (small_ref, small_out))
    locals_ = [
        pltpu.make_async_copy(src, dst.at[dp], local_sem.at[which]) for which, (src, dst) in enumerate(pairs)
    ]
    for copy in locals_:
        copy.start()
    greet(near[1:] + [partner])
    nears = [
        [
            push(
                src.at[at], dst.at[dp, at], near_send.at[at, which, step - 1], near_recv.at[at, which, step - 1],
                near[step],
            )
            for which, (src, dst) in enumerate(pairs)
            for step in (1, 2, 3)
        ]
        for at in range(4)
    ]
    chips = [
        push(src.at[at], dst.at[dp, at], chip_send.at[at, which, 0], chip_recv.at[at, which, 0], partner)
        for at in range(4)
        for which, (src, dst) in enumerate(pairs)
    ]
    swaps = plane_moves(moved_ref, swapped, swap_send, swap_recv)
    for listed in nears + [chips, swaps]:
        for copy in listed:
            copy.start()
    bring.wait()
    keep = pltpu.make_async_copy(held, swapped.at[place], held_sem.at[1])
    keep.start()
    for at in range(4):
        for which, (_, dst) in enumerate(pairs):
            for step in (1, 2, 3):
                nears[at][which * 3 + step - 1].wait()
                spot = dst.at[near[step][0], at]
                chips.append(
                    push(spot, spot, chip_send.at[at, which, step], chip_recv.at[at, which, step], partner)
                )
                chips[-1].start()
    for copy in locals_:
        copy.wait()
    keep.wait()
    for copy in chips + swaps:
        copy.wait()


def spread(block, small, moved):
    vmem_spec = pl.BlockSpec(memory_space=pltpu.VMEM)
    return pl.pallas_call(
        spread_kernel,
        out_shape=(
            jax.ShapeDtypeStruct((8,) + block.shape, block.dtype),
            jax.ShapeDtypeStruct((8,) + small.shape, small.dtype),
            jax.ShapeDtypeStruct(moved.shape, moved.dtype),
        ),
        in_specs=[vmem_spec, vmem_spec, ANY_SPEC],
        out_specs=(ANY_SPEC,) * 3,
        scratch_shapes=[
            pltpu.VMEM(moved.shape[1:], moved.dtype),
            DMA((2,)), DMA((4, 2, 3)), DMA((4, 2, 3)), DMA((4, 2, 4)), DMA((4, 2, 4)), DMA((2,)), DMA((3,)), DMA((3,)),
        ],
        compiler_params=comm_params(1),
        name="spread",
    )(block, small, moved)


def plane_sums_kernel(
    src, moved_ref, out, swapped, own, chip, total, arrived, held,
    local_sem, chip_send, chip_recv, near_send, near_recv, held_sem, swap_send, swap_recv,
):
    place, core, _, near, partner = relatives()
    spots = [place] + [near[step][0] // 2 for step in range(1, 4)]
    load = pltpu.make_async_copy(src.at[:, core], own, local_sem.at[0])
    load.start()
    bring = pltpu.make_async_copy(moved_ref.at[place], held, held_sem.at[0])
    bring.start()
    greet(near[1:] + [partner])
    across = push(src.at[:, 1 - core], chip, chip_send.at[0], chip_recv.at[0], partner)
    across.start()
    swaps = plane_moves(moved_ref, swapped, swap_send, swap_recv)
    load.wait()
    across.wait()
    total[...] = own[...] + chip[...]
    nears = [
        push(total.at[spots[step]], arrived.at[step - 1], near_send.at[step - 1], near_recv.at[step - 1], near[step])
        for step in (3, 1, 2)
    ]
    for copy in nears + swaps:
        copy.start()
    bring.wait()
    keep = pltpu.make_async_copy(held, swapped.at[place], held_sem.at[1])
    keep.start()
    for copy in nears:
        copy.wait()
    out[...] = total[place] + arrived[0] + arrived[1] + arrived[2]
    keep.wait()
    for copy in swaps:
        copy.wait()


def plane_sums(array, moved):
    block = array.shape[2:]
    vmem = lambda lead: pltpu.VMEM((lead,) + block, f32)
    return pl.pallas_call(
        plane_sums_kernel,
        out_shape=(jax.ShapeDtypeStruct(block, f32), jax.ShapeDtypeStruct(moved.shape, moved.dtype)),
        in_specs=[ANY_SPEC] * 2,
        out_specs=(pl.BlockSpec(memory_space=pltpu.VMEM), ANY_SPEC),
        scratch_shapes=[
            vmem(4), vmem(4), vmem(4), vmem(3), pltpu.VMEM(moved.shape[1:], moved.dtype),
            DMA((1,)), DMA((1,)), DMA((1,)), DMA((3,)), DMA((3,)), DMA((2,)), DMA((3,)), DMA((3,)),
        ],
        compiler_params=comm_params(2),
        name="plane_sums",
    )(array, moved)


def finish_kernel(count, *refs):
    parts, moved_ref, sums, swapped = refs[:count], refs[count], refs[count + 1 : 2 * count + 1], refs[2 * count + 1]
    columns, rest = refs[2 * count + 2 : 3 * count + 2], refs[3 * count + 2 :]
    held, col_send, col_recv, held_sem, swap_send, swap_recv = rest
    place, _, _, near, _ = relatives()
    bring = pltpu.make_async_copy(moved_ref.at[place], held, held_sem.at[0])
    bring.start()
    greet(column_greets() + near[1:])
    swaps = plane_moves(moved_ref, swapped, swap_send, swap_recv)
    copies = [
        column_copies(parts[which], columns[which], col_send.at[which], col_recv.at[which]) for which in range(count)
    ]
    for listed in [swaps] + copies:
        for copy in listed:
            copy.start()
    bring.wait()
    keep = pltpu.make_async_copy(held, swapped.at[place], held_sem.at[1])
    keep.start()
    for which in range(count):
        for copy in copies[which]:
            copy.wait()
        sums[which][...] = column_sum(parts[which], columns[which])
    keep.wait()
    for copy in swaps:
        copy.wait()


def finish(parts, moved):
    count = len(parts)
    vmem_spec = pl.BlockSpec(memory_space=pltpu.VMEM)
    return pl.pallas_call(
        partial(finish_kernel, count),
        out_shape=tuple(jax.ShapeDtypeStruct(each.shape[1:], f32) for each in parts)
        + (jax.ShapeDtypeStruct(moved.shape, moved.dtype),),
        in_specs=[vmem_spec] * count + [ANY_SPEC],
        out_specs=(vmem_spec,) * count + (ANY_SPEC,),
        scratch_shapes=[pltpu.VMEM((3,) + each.shape[1:], each.dtype) for each in parts]
        + [
            pltpu.VMEM(moved.shape[1:], moved.dtype),
            DMA((count, 3)), DMA((count, 3)), DMA((2,)), DMA((3,)), DMA((3,)),
        ],
        compiler_params=comm_params(6),
        name="finish",
    )(*parts, moved)


def standard(rows):
    centred = rows - jnp.mean(rows, axis=-1, keepdims=True)
    inv_std = lax.rsqrt(jnp.mean(centred * centred, axis=-1, keepdims=True) + eps_norm)
    return centred * inv_std, inv_std


def lane_put(table, lane, column):
    lanes = lax.broadcasted_iota(jnp.int32, table.shape, 1)
    return jnp.where(lanes == lane, column, table)


def masked_scores(query, key):
    scores = nt(query, key) * (HD ** (-0.5))
    slots = lax.broadcasted_iota(jnp.int32, scores.shape, 1)
    return jnp.where(slots < LEN, scores, far_negative)


def weight_spec(layer):
    return pl.BlockSpec((8, 1, 1, D // 8, D), lambda turn: (0, turn, layer, 0, 0))


def attend_kernel(
    hidden_ref, weight_ref, vec_ref, router_ref,
    resid_ref, second_ref, saved_ref, table_ref, logs_ref, first_sc, attn_sc,
):
    turn = pl.program_id(0)
    images = hidden_ref.shape[0] // SEQ
    weight = weight_ref[:, 0, 0].reshape(D, D)

    @pl.when(turn == 0)
    def _():
        normed, _ = standard(hidden_ref[...].astype(f32))
        first_sc[...] = (normed * vec_ref[0:1] + vec_ref[1:2]).astype(bf16)
        attn_sc[...] = jnp.zeros_like(attn_sc)

    for image in range(images):
        rows = pl.ds(image * SEQ, SEQ)
        mixed = nn(first_sc[rows, :], weight[:, :QKV]).astype(bf16)
        logs = jnp.zeros((SEQ, 128), f32)
        contexts = []
        for head in range(HEADS_PART):
            query, key, value = [
                mixed[:, (kind * HEADS_PART + head) * HD : (kind * HEADS_PART + head + 1) * HD]
                for kind in range(3)
            ]
            scores = masked_scores(query, key)
            top = jnp.max(scores, axis=-1, keepdims=True)
            grown = jnp.exp(scores - top)
            total = jnp.sum(grown, axis=-1, keepdims=True)
            weights = (grown / total).astype(bf16)
            contexts.append(nn(weights, value).astype(bf16))
            logs = lane_put(logs, head, top + jnp.log(total))
        context = jnp.concatenate(contexts, axis=1)
        saved_ref[0, rows, :] = jnp.concatenate([mixed, context], axis=1)
        logs_ref[0, rows, :] = logs
        attn_sc[rows, :] += nt(context, weight[:, QKV:])

    @pl.when(turn == pl.num_programs(0) - 1)
    def _():
        attn = attn_sc[...]
        resid = hidden_ref[...].astype(f32) + attn
        resid_ref[...] = resid
        normed, _ = standard(resid)
        second = (normed * vec_ref[2:3] + vec_ref[3:4]).astype(bf16)
        second_ref[...] = second
        logits = nn(second, router_ref[...])
        lanes = lax.broadcasted_iota(jnp.int32, logits.shape, 1)
        logits = jnp.where(lanes < EXPERTS, logits, far_negative)
        grown = jnp.exp(logits - jnp.max(logits, axis=-1, keepdims=True))
        probs = grown / jnp.sum(grown, axis=-1, keepdims=True)
        table_ref[...] = lane_put(probs, EXPERTS, jnp.sum(attn * attn, axis=-1, keepdims=True))


def attend_rows(hidden, weights, vecs, router, layer):
    rows = hidden.shape[0]
    whole = lambda shape: pl.BlockSpec(shape, lambda turn: (0,) * len(shape))
    by_part = lambda shape: pl.BlockSpec((1,) + shape, lambda turn: (turn, 0, 0))
    return pl.pallas_call(
        attend_kernel,
        grid=(4,),
        in_specs=[whole((rows, D)), weight_spec(layer), whole((8, D)), whole((D, 128))],
        out_specs=(
            whole((rows, D)), whole((rows, D)), by_part((rows, D)), whole((rows, 128)), by_part((rows, 128)),
        ),
        out_shape=(
            jax.ShapeDtypeStruct((rows, D), f32),
            jax.ShapeDtypeStruct((rows, D), bf16),
            jax.ShapeDtypeStruct((4, rows, D), bf16),
            jax.ShapeDtypeStruct((rows, 128), f32),
            jax.ShapeDtypeStruct((4, rows, 128), f32),
        ),
        scratch_shapes=[pltpu.VMEM((rows, D), bf16), pltpu.VMEM((rows, D), f32)],
        compiler_params=pltpu.CompilerParams(vmem_limit_bytes=VMEM_LIMIT),
        name="attend_rows",
    )(hidden, weights, vecs, router)


def norm_pull(grad, normed, inv_std, gain):
    scaled = grad * gain
    one = jnp.mean(scaled, axis=-1, keepdims=True)
    two = jnp.mean(scaled * normed, axis=-1, keepdims=True)
    return inv_std * (scaled - one - normed * two)


def attend_pull_kernel(
    grad_ref, moved_ref, hidden_ref, resid_ref, saved_ref, table_ref, logs_ref, dprob_ref,
    weight_ref, vec_ref, router_ref,
    out_ref, partial_ref, small_ref, rgrad_ref,
    first_sc, grad_sc, low_sc, back_sc,
    mine, chip, total, arrived, chip_send, chip_recv, near_send, near_recv,
):
    turn = pl.program_id(0)
    place, core, _, near, partner = relatives()
    spots = [place] + [near[step][0] // 2 for step in range(1, 4)]

    def chip_copy(at):
        return push(mine.at[at, :, 1 - core], chip.at[at], chip_send.at[at], chip_recv.at[at], partner)

    def near_copies(at):
        return [
            push(
                total.at[at, spots[step]], arrived.at[at, step - 1],
                near_send.at[at, step - 1], near_recv.at[at, step - 1], near[step],
            )
            for step in (3, 1, 2)
        ]

    def after_chip(at):
        chip_copy(at).wait()
        total[at] = mine[at, :, core] + chip[at]
        for copy in near_copies(at):
            copy.start()

    def after_near(at):
        for copy in near_copies(at):
            copy.wait()
        partial_ref[at] = (
            total[at, place].astype(f32)
            + arrived[at, 0].astype(f32)
            + arrived[at, 1].astype(f32)
            + arrived[at, 2].astype(f32)
        ).astype(bf16)

    rows_all = grad_ref.shape[0]
    images = rows_all // SEQ
    weight = weight_ref[:, 0, 0].reshape(D, D)
    scale = HD ** (-0.5)

    @pl.when(turn == 0)
    def _():
        greet(near[1:] + [partner])
        normed, inv_std = standard(resid_ref[...])
        second = (normed * vec_ref[2:3] + vec_ref[3:4]).astype(bf16)
        lanes = lax.broadcasted_iota(jnp.int32, (rows_all, 128), 1)
        probs = jnp.where(lanes < EXPERTS, table_ref[...], 0.0)
        dprobs = dprob_ref[...]
        dlogit = probs * (dprobs - jnp.sum(probs * dprobs, axis=-1, keepdims=True))
        high = dlogit.astype(bf16)
        low = (dlogit - high.astype(f32)).astype(bf16)
        rgrad_ref[...] = tn(second, high) + tn(second, low)
        dsecond = nt(high, router_ref[...]) + nt(low, router_ref[...])
        for expert in range(EXPERTS):
            dsecond = dsecond + moved_ref[expert].astype(f32)
        small_ref[2:3] = jnp.sum(dsecond * normed, axis=0, keepdims=True)
        small_ref[3:4] = jnp.sum(dsecond, axis=0, keepdims=True)
        grad = grad_ref[...] + norm_pull(dsecond, normed, inv_std, vec_ref[2:3])
        grad_sc[...] = grad
        low_sc[...] = grad.astype(bf16)
        normed, _ = standard(hidden_ref[...].astype(f32))
        first_sc[...] = (normed * vec_ref[0:1] + vec_ref[1:2]).astype(bf16)
        back_sc[...] = jnp.zeros_like(back_sc)

    mixed_grads = []
    for image in range(images):
        rows = pl.ds(image * SEQ, SEQ)
        saved = saved_ref[0, rows, :]
        dcontext = nn(low_sc[rows, :], weight[:, QKV:]).astype(bf16)
        pieces = [[], [], []]
        for head in range(HEADS_PART):
            query, key, value = [
                saved[:, (kind * HEADS_PART + head) * HD : (kind * HEADS_PART + head + 1) * HD]
                for kind in range(3)
            ]
            dhead = dcontext[:, head * HD : (head + 1) * HD]
            weights = jnp.exp(masked_scores(query, key) - logs_ref[0, rows, head : head + 1])
            dvalue = tn(weights.astype(bf16), dhead)
            dweights = nt(dhead, value)
            inner = jnp.sum(weights * dweights, axis=-1, keepdims=True)
            dscores = (weights * (dweights - inner)).astype(bf16)
            pieces[0].append((nn(dscores, key) * scale).astype(bf16))
            pieces[1].append((tn(dscores, query) * scale).astype(bf16))
            pieces[2].append(dvalue.astype(bf16))
        mixed = jnp.concatenate(pieces[0] + pieces[1] + pieces[2], axis=1)
        back_sc[rows, :] += nt(mixed, weight[:, :QKV])
        mixed_grads.append(mixed)
        if image == 0:

            @pl.when(turn > 0)
            def _():
                after_chip(turn - 1)

    mixed = jnp.concatenate(mixed_grads, axis=0)
    wgrad = jnp.concatenate([tn(first_sc[...], mixed), tn(low_sc[...], saved_ref[0, :, QKV:])], axis=1)
    mine[turn] = wgrad.astype(bf16).reshape(4, 2, D // 8, D)
    chip_copy(turn).start()

    @pl.when(turn > 1)
    def _():
        after_near(turn - 2)

    @pl.when(turn == 3)
    def _():
        after_chip(3)
        dfirst = back_sc[...]
        normed, inv_std = standard(hidden_ref[...].astype(f32))
        small_ref[0:1] = jnp.sum(dfirst * normed, axis=0, keepdims=True)
        small_ref[1:2] = jnp.sum(dfirst, axis=0, keepdims=True)
        small_ref[4:8] = jnp.zeros((4, D), f32)
        out_ref[...] = grad_sc[...] + norm_pull(dfirst, normed, inv_std, vec_ref[0:1])
        after_near(2)
        after_near(3)


def attend_pull(grad, moved, hidden, resid, saved, table, logs, dprob, weights, vecs, router, layer):
    rows = grad.shape[0]
    block = (D // 8, D)
    whole = lambda shape: pl.BlockSpec(shape, lambda turn: (0,) * len(shape))
    by_part = lambda shape: pl.BlockSpec((1,) + shape, lambda turn: (turn, 0, 0))
    return pl.pallas_call(
        attend_pull_kernel,
        grid=(4,),
        in_specs=[
            whole((rows, D)), whole((EXPERTS, rows, D)), whole((rows, D)), whole((rows, D)),
            by_part((rows, D)), whole((rows, 128)), by_part((rows, 128)), whole((rows, 128)),
            weight_spec(layer), whole((8, D)), whole((D, 128)),
        ],
        out_specs=(whole((rows, D)), whole((4,) + block), whole((8, D)), whole((D, 128))),
        out_shape=(
            jax.ShapeDtypeStruct((rows, D), f32),
            jax.ShapeDtypeStruct((4,) + block, bf16),
            jax.ShapeDtypeStruct((8, D), f32),
            jax.ShapeDtypeStruct((D, 128), f32),
        ),
        scratch_shapes=[
            pltpu.VMEM((rows, D), bf16), pltpu.VMEM((rows, D), f32),
            pltpu.VMEM((rows, D), bf16), pltpu.VMEM((rows, D), f32),
            pltpu.VMEM((4, 4, 2) + block, bf16), pltpu.VMEM((4, 4) + block, bf16),
            pltpu.VMEM((4, 4) + block, bf16), pltpu.VMEM((4, 3) + block, bf16),
            DMA((4,)), DMA((4,)), DMA((4, 3)), DMA((4, 3)),
        ],
        compiler_params=comm_params(8 + layer),
        name="attend_pull",
    )(grad, moved, hidden, resid, saved, table, logs, dprob, weights, vecs, router)


GELU_C = math.sqrt(2.0 / math.pi)
GELU_K = 0.044715


def gelu_pair(pre):
    square = pre * pre
    bent = jnp.tanh(GELU_C * pre * (1.0 + GELU_K * square))
    half = 0.5 * (1.0 + bent)
    slope = half + (0.5 * GELU_C) * pre * (1.0 - bent * bent) * (1.0 + (3.0 * GELU_K) * square)
    return pre * half, slope


TILE = 256


def weight_of(held, which, turn):
    return held[which, pl.ds(turn * 4, 4)].reshape(D, D)


def expert_kernel(
    second_ref, pieces_ref, rows_out, back_out, weights_out, act_out, slope_out,
    held, weights, made, acts, slopes, total,
    load_sem, join_send, join_recv, row_send, row_recv, pass_send, pass_recv, back_send, back_recv, out_sem, save_sem,
):
    _, core, _, near, partner = relatives()
    count = second_ref.shape[0]
    half = count // 2
    load = pltpu.make_async_copy(second_ref, held.at[0], load_sem.at[2])
    load.start()
    joins = []
    for which in range(2):
        src, dst = pieces_ref.at[:, which], weights.at[which, :, core]
        joins.append(pltpu.make_async_copy(src, dst, load_sem.at[which]))
        joins[-1].start()
    greet(near[1:] + [partner])
    for which in range(2):
        src, dst = pieces_ref.at[:, which], weights.at[which, :, core]
        joins.append(push(src, dst, join_send.at[which], join_recv.at[which], partner))
        joins[-1].start()
    rows = [
        push(second_ref, held.at[step], row_send.at[step - 1], row_recv.at[step - 1], near[step])
        for step in (1, 2)
    ]
    for copy in rows:
        copy.start()
    low, high = pl.ds(0, half), pl.ds(half, half)
    passed = [
        push(held.at[1, low], held.at[3, low], pass_send.at[0], pass_recv.at[0], near[2]),
        push(held.at[2, high], held.at[3, high], pass_send.at[1], pass_recv.at[1], near[1]),
    ]
    backs = [pltpu.make_async_copy(made.at[0], back_out.at[0], save_sem.at[2])] + [
        push(made.at[step], back_out.at[step], back_send.at[step - 1], back_recv.at[step - 1], near[step])
        for step in (1, 2, 3)
    ]
    save_rows = pltpu.make_async_copy(held, rows_out, save_sem.at[0])
    save_weights = pltpu.make_async_copy(weights, weights_out, save_sem.at[1])
    load.wait()
    for copy in joins:
        copy.wait()
    save_weights.start()

    def outs(slot, step, turn):
        place = pl.ds(pl.multiple_of(step * count, count), count)
        return (
            pltpu.make_async_copy(acts.at[slot], act_out.at[turn, place], out_sem.at[0, slot]),
            pltpu.make_async_copy(slopes.at[slot], slope_out.at[turn, place], out_sem.at[1, slot]),
        )

    def chunk(step, carry):
        @pl.when(step == 1)
        def _():
            for copy in rows:
                copy.wait()
            for copy in passed:
                copy.start()

        @pl.when(step == 3)
        def _():
            for copy in passed:
                copy.wait()
            save_rows.start()

        def part(turn, carry):
            slot = lax.rem(turn, 2)

            @pl.when(step * 4 + turn >= 2)
            def _():
                for copy in outs(slot, step, turn):
                    copy.wait()

            for at in range(0, count, TILE):
                tile = pl.ds(at, TILE)
                act, slope = gelu_pair(nn(held[step, tile, :], weight_of(weights, 0, turn)))
                act = act.astype(bf16)
                acts[slot, tile, :] = act
                slopes[slot, tile, :] = slope.astype(bf16)
                product = nt(act, weight_of(weights, 1, turn))
                total[tile, :] = jnp.where(turn == 0, product, total[tile, :] + product)
            for copy in outs(slot, step, turn):
                copy.start()
            return carry

        lax.fori_loop(0, 4, part, 0)
        made[step] = total[...].astype(bf16)
        for at in range(4):

            @pl.when(step == at)
            def _():
                backs[at].start()

        return carry

    lax.fori_loop(0, 4, chunk, 0)
    for slot in range(2):
        for copy in outs(slot, 3, 2 + slot):
            copy.wait()
    save_rows.wait()
    save_weights.wait()
    for copy in backs:
        copy.wait()


def expert_rows(second, pieces):
    count = second.shape[0]
    block = (count, D)
    weight_shape = (2, 16, 2, D // 8, D)
    return pl.pallas_call(
        expert_kernel,
        in_specs=[ANY_SPEC] * 2,
        out_specs=(ANY_SPEC,) * 5,
        out_shape=(
            jax.ShapeDtypeStruct((4,) + block, bf16),
            jax.ShapeDtypeStruct((4,) + block, bf16),
            jax.ShapeDtypeStruct(weight_shape, bf16),
            jax.ShapeDtypeStruct((4, 4 * count, D), bf16),
            jax.ShapeDtypeStruct((4, 4 * count, D), bf16),
        ),
        scratch_shapes=[
            pltpu.VMEM((4,) + block, bf16),
            pltpu.VMEM(weight_shape, bf16),
            pltpu.VMEM((4,) + block, bf16),
            pltpu.VMEM((2,) + block, bf16),
            pltpu.VMEM((2,) + block, bf16),
            pltpu.VMEM(block, f32),
            DMA((3,)), DMA((2,)), DMA((2,)), DMA((2,)), DMA((2,)), DMA((2,)), DMA((2,)),
            DMA((3,)), DMA((3,)), DMA((2, 2)), DMA((3,)),
        ],
        compiler_params=comm_params(4),
        name="expert_rows",
    )(second, pieces)


def expert_pull_kernel(
    sent_ref, rows_ref, act_ref, slope_ref, weights_ref, moved_out, wgrad_out,
    grads, rows, weights, pres, made, slopes, acts, total, halves, arrived,
    load_sem, row_send, row_recv, back_send, back_recv, slope_sem, act_sem, chip_send, chip_recv, save_sem,
):
    _, core, _, near, partner = relatives()
    count = sent_ref.shape[1]
    own = pltpu.make_async_copy(sent_ref.at[0], grads.at[0], load_sem.at[0])
    load_weights = pltpu.make_async_copy(weights_ref, weights, load_sem.at[1])
    load_rows = pltpu.make_async_copy(rows_ref, rows, load_sem.at[2])

    def slope_load(step, turn, slot):
        place = pl.ds(pl.multiple_of(step * count, count), count)
        return pltpu.make_async_copy(slope_ref.at[turn, place], slopes.at[slot], slope_sem.at[slot])

    def act_load(turn, slot):
        return pltpu.make_async_copy(act_ref.at[turn], acts.at[slot], act_sem.at[slot])

    own.start()
    load_weights.start()
    for slot in range(2):
        slope_load(0, slot, slot).start()
    load_rows.start()
    for slot in range(2):
        act_load(slot, slot).start()
    greet(near[1:] + [partner])
    sends = [None] + [
        push(sent_ref.at[step], grads.at[step], row_send.at[step - 1], row_recv.at[step - 1], near[step])
        for step in (1, 2, 3)
    ]
    sends[1].start()
    sends[2].start()
    backs = [pltpu.make_async_copy(made.at[0], moved_out.at[0], load_sem.at[3])] + [
        push(made.at[step], moved_out.at[step], back_send.at[step - 1], back_recv.at[step - 1], near[step])
        for step in (1, 2, 3)
    ]
    own.wait()
    load_weights.wait()

    def chunk(step, carry):
        @pl.when(step == 1)
        def _():
            sends[3].start()

        for at in (1, 2, 3):

            @pl.when(step == at)
            def _():
                sends[at].wait()

        def part(turn, carry):
            slot = lax.rem(turn, 2)
            slope_load(step, turn, slot).wait()
            for at in range(0, count, TILE):
                tile = pl.ds(at, TILE)
                dact = nn(grads[step, tile, :], weight_of(weights, 1, turn))
                dpre = (slopes[slot, tile, :].astype(f32) * dact).astype(bf16)
                pres[turn, step, tile, :] = dpre
                product = nt(dpre, weight_of(weights, 0, turn))
                total[tile, :] = jnp.where(turn == 0, product, total[tile, :] + product)

            @pl.when(step * 4 + turn < 14)
            def _():
                after = step * 4 + turn + 2
                slope_load(after // 4, after % 4, slot).start()

            return carry

        lax.fori_loop(0, 4, part, 0)
        made[step] = total[...].astype(bf16)
        for at in range(4):

            @pl.when(step == at)
            def _():
                backs[at].start()

        return carry

    lax.fori_loop(0, 4, chunk, 0)
    load_rows.wait()

    def chip_copy(which, turn):
        return push(
            halves.at[which, turn, :, 1 - core], arrived.at[which, turn],
            chip_send.at[which, turn], chip_recv.at[which, turn], partner,
        )

    def save(which, turn):
        return pltpu.make_async_copy(arrived.at[which, turn], wgrad_out.at[turn, :, which], save_sem.at[which, turn])

    def finish(turn):
        for which in range(2):
            chip_copy(which, turn).wait()
            arrived[which, turn] = (
                halves[which, turn, :, core].astype(f32) + arrived[which, turn].astype(f32)
            ).astype(bf16)
            save(which, turn).start()

    def wgrad(turn, carry):
        slot = lax.rem(turn, 2)
        flat = (4 * count, D)
        act_load(turn, slot).wait()
        first = tn(rows[...].reshape(flat), pres[turn].reshape(flat))
        halves[0, turn] = first.astype(bf16).reshape(4, 2, D // 8, D)
        chip_copy(0, turn).start()
        second = tn(grads[...].reshape(flat), acts[slot])
        halves[1, turn] = second.astype(bf16).reshape(4, 2, D // 8, D)
        chip_copy(1, turn).start()

        @pl.when(turn < 2)
        def _():
            act_load(turn + 2, slot).start()

        @pl.when(turn > 0)
        def _():
            finish(turn - 1)

        return carry

    lax.fori_loop(0, 4, wgrad, 0)
    finish(3)
    for turn in range(4):
        for which in range(2):
            save(which, turn).wait()
    for copy in backs:
        copy.wait()


def expert_pull(sent, rows, act, slope, weights):
    count = sent.shape[1]
    block = (count, D)
    slices = D // 8
    return pl.pallas_call(
        expert_pull_kernel,
        in_specs=[ANY_SPEC] * 5,
        out_specs=(ANY_SPEC, ANY_SPEC),
        out_shape=(
            jax.ShapeDtypeStruct((4,) + block, bf16),
            jax.ShapeDtypeStruct((4, 4, 2, slices, D), bf16),
        ),
        scratch_shapes=[
            pltpu.VMEM((4,) + block, bf16),
            pltpu.VMEM((4,) + block, bf16),
            pltpu.VMEM(weights.shape, bf16),
            pltpu.VMEM((4, 4) + block, bf16),
            pltpu.VMEM((4,) + block, bf16),
            pltpu.VMEM((2,) + block, bf16),
            pltpu.VMEM((2, 4 * count, D), bf16),
            pltpu.VMEM(block, f32),
            pltpu.VMEM((2, 4, 4, 2, slices, D), bf16),
            pltpu.VMEM((2, 4, 4, slices, D), bf16),
            DMA((4,)), DMA((3,)), DMA((3,)), DMA((3,)), DMA((3,)), DMA((2,)), DMA((2,)),
            DMA((2, 4)), DMA((2, 4)), DMA((2, 4)),
        ],
        compiler_params=comm_params(5),
        name="expert_pull",
    )(sent, rows, act, slope, weights)


def per_device(
    tokens, counts, routes, norm_gain, norm_bias, w_router, w_qkv, w_out, w_in, w_back, cotangent
):
    dp, part = lax.axis_index("dp"), lax.axis_index("tensor")
    place = dp // 2
    own_rows = tokens.shape[0]
    slices = D // 8
    row_ids = part * own_rows + jnp.arange(own_rows, dtype=jnp.int32)
    image_count = lax.dynamic_index_in_dim(counts, dp, keepdims=False)
    valid = ((row_ids // SEQ < image_count) & (row_ids % SEQ < LEN)).astype(f32)[:, None]
    my_routes = lax.dynamic_slice_in_dim(routes, part * own_rows, own_rows, axis=1)
    row, col = place // 2, place % 2
    served = jnp.stack([place, row * 2 + 1 - col, (1 - row) * 2 + col, (1 - row) * 2 + 1 - col])
    expert_of = served[:, None] == jnp.arange(EXPERTS)[None, :]
    chosen = (my_routes[:, :, :, None] == served).any(axis=2)

    def by_place(table):
        return jnp.sum(jnp.where(expert_of[None], table[:, None, :], 0.0), axis=-1)

    attn_blocks = jnp.concatenate(
        [
            jnp.transpose(w_qkv, (0, 2, 1, 3)).reshape(LAYERS, slices, QKV),
            jnp.transpose(w_out, (0, 2, 1)),
        ],
        axis=2,
    )
    small = jnp.concatenate([norm_gain, norm_bias, w_router])
    small = jnp.pad(small, (0, 2048 - small.shape[0])).reshape(16, 128)

    packed = [jnp.stack([w_in[layer], w_back[layer]], axis=1) for layer in range(LAYERS)]
    blocks_column, small_column, swapped_first = spread_column(attn_blocks, small, packed[0])
    attn_all, small_all, swapped_later = spread(blocks_column, small_column, packed[1])
    pieces = [
        lax.all_gather(swapped, "tensor", axis=0, tiled=True) for swapped in (swapped_first, swapped_later)
    ]
    flat = small_all.reshape(32, 2048)
    vec_count = LAYERS * 2 * D // 32
    gains = flat[:, :vec_count].reshape(LAYERS, 2, D).astype(f32)
    biases = flat[:, vec_count : 2 * vec_count].reshape(LAYERS, 2, D).astype(f32)
    routers = flat[:, 2 * vec_count : 2 * vec_count + LAYERS * D * EXPERTS // 32]
    routers = jnp.pad(routers.reshape(LAYERS, D, EXPERTS), ((0, 0), (0, 0), (0, 128 - EXPERTS)))
    vecs = jnp.pad(
        jnp.stack([gains[:, 0], biases[:, 0], gains[:, 1], biases[:, 1]], axis=1), ((0, 0), (0, 4), (0, 0))
    )

    hidden = tokens
    kept = []
    stats = []
    for layer in range(LAYERS):
        resid, second, saved, table, logs = attend_rows(hidden, attn_all, vecs[layer], routers[layer], layer)
        rows, back, weights, act, slope = expert_rows(second, pieces[layer])
        gates = jnp.where(chosen[layer], by_place(table[:, :EXPERTS]), 0.0)
        moe = sum(gates[:, at : at + 1] * back[at].astype(f32) for at in range(EXPERTS))
        result = resid + moe
        stats.append(
            jnp.stack(
                [
                    jnp.sum(valid * result * result),
                    jnp.sum(valid[:, 0] * table[:, EXPERTS]),
                    jnp.sum(valid * moe * moe),
                ]
            )
        )
        kept.append((hidden, resid, saved, table, logs, rows, weights, act, slope, back, gates))
        hidden = result

    grad = cotangent.astype(f32) * valid
    attn_grads, owned, small_grads, router_grads = [], [], [], []
    for layer in reversed(range(LAYERS)):
        before, resid, saved, table, logs, rows, weights, act, slope, back, gates = kept[layer]
        low = grad.astype(bf16)
        dgate = [jnp.sum(back[at].astype(f32) * low.astype(f32), axis=-1) for at in range(EXPERTS)]
        dprob = by_place(jnp.where(chosen[layer], jnp.stack(dgate, axis=1), 0.0))
        dprob = jnp.pad(dprob, ((0, 0), (0, 128 - EXPERTS)))
        sent = jnp.stack([(gates[:, at : at + 1] * low.astype(f32)).astype(bf16) for at in range(EXPERTS)])
        moved, wgrad = expert_pull(sent, rows, act, slope, weights)
        summed = lax.psum_scatter(wgrad, "tensor", scatter_dimension=0, tiled=False)
        owned.append(summed)
        grad, attn_part, small_grad, router_grad = attend_pull(
            grad, moved, before, resid, saved, table, logs, dprob, attn_all, vecs[layer], routers[layer], layer
        )
        attn_grads.append(attn_part)
        small_grads.append(small_grad[:4])
        router_grads.append(router_grad[:, :EXPERTS])
    for listed in (small_grads, router_grads, owned):
        listed.reverse()

    vec_grads = jnp.stack(small_grads).reshape(LAYERS, 2, 2, D)
    packed = jnp.concatenate(
        [
            vec_grads[:, :, 0].reshape(32, -1),
            vec_grads[:, :, 1].reshape(32, -1),
            jnp.stack(router_grads).reshape(32, -1),
            jnp.broadcast_to(jnp.stack(stats).reshape(1, -1), (32, 3 * LAYERS)),
        ],
        axis=1,
    )
    packed = jnp.pad(packed, ((0, 0), (0, 1024 - packed.shape[1]))).reshape(4, 2, 4, 8, 128)
    small_part, moved_later = plane_sums(packed, owned[1])
    *attn_grads, total, moved_first = finish(attn_grads[::-1] + [small_part], owned[0])
    attn_grad = jnp.stack(attn_grads)
    total = total.reshape(-1)
    share = LAYERS * 2 * D // 32
    router_share = LAYERS * D * EXPERTS // 32
    at = 2 * share + router_share
    denom = jnp.sum(counts).astype(f32) * (LEN * D)
    rms = jnp.sqrt(total[at : at + 3 * LAYERS].reshape(LAYERS, 3) / denom)
    qkv_grad = jnp.transpose(attn_grad[:, :, :QKV].reshape(LAYERS, slices, 3, QKV // 3), (0, 2, 1, 3))
    out_grad = jnp.transpose(attn_grad[:, :, QKV:], (0, 2, 1))
    expert_grad = jnp.stack([moved_first, moved_later], axis=1).astype(f32)
    expert_grad = jnp.transpose(expert_grad, (2, 1, 0, 3, 4))
    return (
        hidden,
        grad,
        total[:share],
        total[share : 2 * share],
        total[2 * share : at],
        qkv_grad,
        out_grad,
        expert_grad[0],
        expert_grad[1],
        rms,
    )


def solution(mesh):
    return jax.shard_map(
        per_device if mesh.shape["dp"] == 8 else per_device_general,
        mesh=mesh,
        in_specs=(
            P(("dp", "tensor"), None),
            P(),
            P(None, "dp", None),
            P(("dp", "tensor")),
            P(("dp", "tensor")),
            P(("dp", "tensor")),
            P(None, None, "dp", "tensor"),
            P(None, "tensor", "dp"),
            P(None, None, "dp", "tensor"),
            P(None, None, "dp", "tensor"),
            P(("dp", "tensor"), None),
        ),
        out_specs=(
            P(("dp", "tensor"), None),
            P(("dp", "tensor"), None),
            P(("dp", "tensor")),
            P(("dp", "tensor")),
            P(("dp", "tensor")),
            P(None, None, "dp", "tensor"),
            P(None, "tensor", "dp"),
            P(None, None, "dp", "tensor"),
            P(None, None, "dp", "tensor"),
            P(),
        ),
        check_vma=False,
    )
```
